128 devices in a mesh: gx: 8 (over z, core), gy: 16 (over x, y).
Axes of the slice: x: 4, y: 4, z: 4, core: 2. Of those that a mesh axis runs over, the one named last changes fastest.
Arguments:
- depth: float32 [4096, 128, 128], P(('gx', 'gy')), may hold values from 0.1 to 2
- discharge: float32 [4096, 2, 128, 128], P(('gx', 'gy')), may hold values from -3 to 3
- bed: float32 [4096, 128, 128], P(('gx', 'gy')), may hold values from -1.5 to 2.5
- friction: float32 [4096, 128, 128], P(('gx', 'gy')), may hold values from 0.004 to 0.1
- tile_ids: int32 [4096], P(('gx', 'gy')), may hold values from -1 to 4095, as said below
- neighbors: int32 [4096, 4], P(('gx', 'gy')), may hold values from -1 to 4095, as said below
- moves: int32 [128, 2, 8, 2], P(('gx', 'gy')), may hold values from -1 to 4095, as said below
Outputs:
- new_depth: float32 [4096, 128, 128], P(('gx', 'gy'))
- new_discharge: float32 [4096, 2, 128, 128], P(('gx', 'gy'))
The draws below stay inside these ranges and needn't reach their ends.
Inputs may be any that keep to these rules, and one draw needn't show every extreme that they name: `tile_ids`: each owner's wet tiles after the moves fill its first slots: those that stayed, in curve order, then those arrived from lower gy, then those arrived from higher gy; an empty slot is -1. `neighbors`: links are symmetric and join only slots with tile_ids >= 0. The tile beside on side 0 or 1 is held by the same owner or by the owner at gx - 1 or gx + 1 respectively; on side 2 or 3 by the same owner or the owner at gy - 1 or gy + 1. At most 4 tiles of an owner have their side 0 (or side 1) neighbour on another owner, and at most 8 their side 2 (or side 3) neighbour; both bounds are reached on some owner. Entries are global slots, -1 if unused, used entries first. Leaving slots lie on the owner and hold no tile that stays; landing slots lie on the owner and are either left by a tile or hold no tile before the moves. The m-th tile leaving owner (a, b) toward higher gy is the m-th arriving at (a, b + 1) from lower gy, and likewise downward; owners at the ends of gy list nothing toward the outside. All 8 entries of a direction are used on some owners.
All inputs are finite; a program needn't handle non-finite values.
Results may differ from the reference program's by a relative error of at most 0.00002.
Values sent between devices are 32-bit elements; how exact they have to be, the bound alone decides.
No kernel may reach another device: no remote copies, remote signals or barrier semaphores. Data moves between devices by JAX's collectives and lax.ppermute only.
A program may use at most 128 MiB of HBM per device.

```python
import math
import jax
import jax.numpy as jnp

TILE = 128
BLOCK_ROWS = 8
BLOCK_COLS = 4
STEPS = 4
SLOTS = 32
MOVERS = 8
OWNERS = 128
TILES = 4096
N_GX = 8
N_GY = 16


def layout(key):
    rows_all = BLOCK_ROWS * N_GX
    cols_all = BLOCK_COLS * N_GY
    key_level, key_roll = jax.random.split(jax.random.fold_in(key, 29))
    level = jax.random.randint(key_level, (N_GX, N_GY), 30, 96)
    roll = jax.random.randint(key_roll, (rows_all, cols_all), 0, 100)
    cutoff = jnp.repeat(jnp.repeat(level, BLOCK_ROWS, axis=0), BLOCK_COLS, axis=1)
    row_idx = jnp.arange(rows_all)[:, None]
    col_idx = jnp.arange(cols_all)[None, :]
    wet = (roll < cutoff) | (row_idx == BLOCK_ROWS - 1) | (row_idx == BLOCK_ROWS)
    wet = wet | (col_idx == BLOCK_COLS - 1) | (col_idx == BLOCK_COLS)

    def to_blocks(plane):
        return plane.reshape(N_GX, BLOCK_ROWS, N_GY, BLOCK_COLS).transpose(0, 2, 1, 3).reshape(N_GX, N_GY, SLOTS)

    def from_blocks(blocks):
        return blocks.reshape(N_GX, N_GY, BLOCK_ROWS, BLOCK_COLS).transpose(0, 2, 1, 3).reshape(rows_all, cols_all)
    local_row = jnp.arange(BLOCK_ROWS)[:, None]
    local_col = jnp.arange(BLOCK_COLS)[None, :]
    curve = (local_row * BLOCK_COLS + jnp.where(local_row % 2 == 0, local_col, BLOCK_COLS - 1 - local_col)).reshape(-1)
    earlier = curve[None, :] < curve[:, None]
    flat_col = jnp.arange(SLOTS) % BLOCK_COLS
    flat_row = jnp.arange(SLOTS) // BLOCK_COLS
    owner_col = jnp.arange(N_GY)[None, :, None]
    wet_blocks = to_blocks(wet)
    from_low = wet_blocks & (flat_col == 0)[None, None, :] & (owner_col >= 1)
    from_high = wet_blocks & (flat_col == BLOCK_COLS - 1)[None, None, :] & (owner_col <= N_GY - 2)
    stay = wet_blocks & ~from_low & ~from_high
    rank = jnp.sum(stay[:, :, None, :] & earlier[None, None], axis=-1).astype(jnp.int32)
    count_stay = jnp.sum(stay.astype(jnp.int32), -1)
    low_col = from_low.reshape(N_GX, N_GY, BLOCK_ROWS, BLOCK_COLS)[..., 0]
    high_col = from_high.reshape(N_GX, N_GY, BLOCK_ROWS, BLOCK_COLS)[..., BLOCK_COLS - 1]
    order_low = jnp.cumsum(low_col.astype(jnp.int32), -1) - 1
    order_high = jnp.cumsum(high_col.astype(jnp.int32), -1) - 1
    count_low = jnp.sum(low_col.astype(jnp.int32), -1)
    count_high = jnp.sum(high_col.astype(jnp.int32), -1)
    local_slot = jnp.where(stay, rank, jnp.where(from_low, count_stay[..., None] + order_low[..., flat_row], count_stay[..., None] + count_low[..., None] + order_high[..., flat_row]))
    owner = (jnp.arange(N_GX)[:, None] * N_GY + jnp.arange(N_GY)[None, :]).astype(jnp.int32)
    post = jnp.where(wet_blocks, owner[:, :, None] * SLOTS + local_slot, -1).astype(jnp.int32)
    post_grid = from_blocks(post)
    ids_grid = (row_idx * cols_all + col_idx).astype(jnp.int32)
    target = jnp.where(wet, post_grid, TILES).reshape(-1).astype(jnp.int32)
    tile_ids = jnp.full((TILES,), -1, jnp.int32).at[target].set(ids_grid.reshape(-1), mode='drop')
    padded = jnp.pad(post_grid, 1, constant_values=-1)
    sides = jnp.stack([padded[:-2, 1:-1], padded[2:, 1:-1], padded[1:-1, :-2], padded[1:-1, 2:]], -1).reshape(-1, 4)
    neighbors = jnp.full((TILES, 4), -1, jnp.int32).at[target].set(sides.astype(jnp.int32), mode='drop')
    entry = jnp.arange(MOVERS)[None, None, :]
    base = owner[..., None] * SLOTS + count_stay[..., None]
    arrive_low = jnp.where(entry < count_low[..., None], base + entry, -1)
    arrive_high = jnp.where(entry < count_high[..., None], base + count_low[..., None] + entry, -1)
    zero_col = jnp.zeros((N_GX, 1), jnp.int32)
    count_down = jnp.concatenate([zero_col, count_high[:, :-1]], 1)
    count_up = jnp.concatenate([count_low[:, 1:], zero_col], 1)
    leave_down = jnp.where(entry < count_down[..., None], base + entry, -1)
    leave_up = jnp.where(entry < count_up[..., None], base + count_down[..., None] + entry, -1)
    way_down = jnp.stack([leave_down, arrive_low], -1)
    way_up = jnp.stack([leave_up, arrive_high], -1)
    moves = jnp.stack([way_down, way_up], 2).reshape(OWNERS, 2, MOVERS, 2).astype(jnp.int32)
    return (tile_ids, neighbors, moves)


def draw_tile_ids(key, part):
    return layout(key)[0]


def draw_neighbors(key, part):
    return layout(key)[1]


def draw_moves(key, part):
    return layout(key)[2]


def draw_bed(key, part):
    rough = 0.3 * jax.random.normal(jax.random.fold_in(key, 5), (TILES, TILE, TILE), jnp.float32)
    return jnp.clip(rough, -1.5, 2.5)


def shard_levels(rng, extent, shards, smallest, largest):
    def one(position, parts):
        draws = jax.random.uniform(jax.random.fold_in(jax.random.fold_in(rng, 6), position), (parts,), jnp.float32, smallest / len(shards), largest / len(shards))
        return jnp.repeat(jnp.exp(draws), extent[position] // parts).reshape((-1,) + (1,) * (len(extent) - position - 1))

    gain = one(*shards[0])
    for cut in shards[1:]:
        gain = gain * one(*cut)
    return gain


def gaussian(rng, shape, spread, most, cuts=(), kind=jnp.bfloat16):
    values = spread * jax.random.normal(rng, shape, jnp.float32)
    if cuts:
        values = values * shard_levels(rng, shape, cuts, -0.22, 0.18)
    return jnp.clip(values, -most, most).astype(kind)


def setup_inputs(seed: int = 0) -> dict:
    arg_keys = jax.random.split(jax.random.key(seed), 8)
    depth = jnp.clip(0.1 + 1.9 * jax.random.uniform(arg_keys[0], (TILES, TILE, TILE), jnp.float32) ** shard_levels(arg_keys[0], (TILES, TILE, TILE), ((0, 128),), -0.2, 0.2), 0.1, 2.0)
    discharge = gaussian(arg_keys[1], (TILES, 2, TILE, TILE), 0.5, 3.0, ((0, 128),), jnp.float32)
    bed = draw_bed(jax.random.fold_in(arg_keys[7], 71), 0)
    friction = jnp.clip(jnp.exp(math.log(0.1) - 3.218876 * jax.random.uniform(arg_keys[3], (TILES, TILE, TILE), jnp.float32) ** shard_levels(arg_keys[3], (TILES, TILE, TILE), ((0, 128),), -0.2, 0.2)), 0.004, 0.1)
    tile_ids = draw_tile_ids(jax.random.fold_in(arg_keys[7], 71), 0)
    neighbors = draw_neighbors(jax.random.fold_in(arg_keys[7], 71), 0)
    moves = draw_moves(jax.random.fold_in(arg_keys[7], 71), 0)
    return {"depth": depth, "discharge": discharge, "bed": bed, "friction": friction, "tile_ids": tile_ids, "neighbors": neighbors, "moves": moves}


gravity = 9.81
step_time = 0.25
spacing = 2.0
min_depth = 0.15


def face_flux(flow, h_lo, h_hi, z_lo, z_hi, n_lo, n_hi):
    depth_face = jnp.maximum(0.5 * (h_lo + h_hi), min_depth)
    drive = flow - (gravity * step_time / spacing) * depth_face * ((h_hi + z_hi) - (h_lo + z_lo))
    drag = 1.0 + gravity * step_time * 0.5 * (n_lo + n_hi) * jnp.abs(flow) * jnp.exp(-(7.0 / 3.0) * jnp.log(depth_face))
    return drive / drag


def edge_take(rows, link):
    got = jnp.take(rows, jnp.maximum(link, 0).astype(jnp.int32), axis=0)
    return jnp.where((link >= 0)[:, None], got, 0.0)


def advance(h, qx, qy, z, fr, links):
    h_hi = jnp.concatenate([h[:, 1:, :], edge_take(h[:, 0, :], links[:, 1])[:, None, :]], 1)
    z_hi = jnp.concatenate([z[:, 1:, :], edge_take(z[:, 0, :], links[:, 1])[:, None, :]], 1)
    n_hi = jnp.concatenate([fr[:, 1:, :], edge_take(fr[:, 0, :], links[:, 1])[:, None, :]], 1)
    inside_x = jnp.arange(TILE)[None, :, None] < TILE - 1
    qx_new = jnp.where(inside_x | (links[:, 1] >= 0)[:, None, None], face_flux(qx, h, h_hi, z, z_hi, fr, n_hi), 0.0)
    h_rt = jnp.concatenate([h[:, :, 1:], edge_take(h[:, :, 0], links[:, 3])[:, :, None]], 2)
    z_rt = jnp.concatenate([z[:, :, 1:], edge_take(z[:, :, 0], links[:, 3])[:, :, None]], 2)
    n_rt = jnp.concatenate([fr[:, :, 1:], edge_take(fr[:, :, 0], links[:, 3])[:, :, None]], 2)
    inside_y = jnp.arange(TILE)[None, None, :] < TILE - 1
    qy_new = jnp.where(inside_y | (links[:, 3] >= 0)[:, None, None], face_flux(qy, h, h_rt, z, z_rt, fr, n_rt), 0.0)
    in_x = jnp.concatenate([edge_take(qx_new[:, -1, :], links[:, 0])[:, None, :], qx_new[:, :-1, :]], 1)
    in_y = jnp.concatenate([edge_take(qy_new[:, :, -1], links[:, 2])[:, :, None], qy_new[:, :, :-1]], 2)
    h_new = h + (step_time / spacing) * ((in_x - qx_new) + (in_y - qy_new))
    return h_new, qx_new, qy_new


def reference(depth, discharge, bed, friction, tile_ids, neighbors, moves):
    grid = moves.reshape(N_GX, N_GY, 2, MOVERS, 2)
    source = jnp.concatenate([grid[:, :-1, 1, :, 0].reshape(-1), grid[:, 1:, 0, :, 0].reshape(-1)]).astype(jnp.int32)
    target = jnp.concatenate([grid[:, 1:, 0, :, 1].reshape(-1), grid[:, :-1, 1, :, 1].reshape(-1)]).astype(jnp.int32)
    valid = source >= 0
    source_at = jnp.where(valid, source, TILES).astype(jnp.int32)
    target_at = jnp.where(valid, target, TILES).astype(jnp.int32)
    leaving = jnp.zeros((TILES,), bool).at[source_at].set(True, mode="drop")
    pick = jnp.maximum(source, 0).astype(jnp.int32)

    def settle(field):
        shape = (-1,) + (1,) * (field.ndim - 1)
        kept = jnp.where(leaving.reshape(shape), 0.0, field)
        return kept.at[target_at].set(jnp.take(field, pick, axis=0), mode="drop")

    h = settle(depth)
    flows = settle(discharge)
    z = settle(bed)
    fr = settle(friction)
    qx = flows[:, 0]
    qy = flows[:, 1]
    for turn in range(STEPS):
        h, qx, qy = advance(h, qx, qy, z, fr, neighbors)
    live = (tile_ids >= 0)[:, None, None]
    new_depth = jnp.where(live, h, 0.0)
    new_discharge = jnp.stack([jnp.where(live, qx, 0.0), jnp.where(live, qy, 0.0)], 1)
    return new_depth, new_discharge
```

```python
import jax
import jax.numpy as jnp
from jax import lax
from jax.experimental import pallas as pl
from jax.experimental.pallas import tpu as pltpu
from jax.sharding import PartitionSpec as P

TILE = 128
SLOTS = 32
MOVERS = 8
DEPTH = 4
STRIPS = 2 * DEPTH
ROUNDS = 4
PER_ROUND = MOVERS // ROUNDS
FIELD = STRIPS * TILE
CHUNK_ROWS = PER_ROUND * 5 * TILE
GROUP = 8
BUFFERS = 4

gravity = 9.81
step_time = 0.25
spacing = 2.0
min_depth = 0.15
PULL = gravity * step_time / spacing
RUB = gravity * step_time * 0.5
GAIN = step_time / spacing

f32 = jnp.float32
bf16 = jnp.bfloat16
i32 = jnp.int32


def flux(flow, h_lo, h_hi, slope, rub):
    depth_face = jnp.maximum(0.5 * (h_lo + h_hi), min_depth)
    drive = flow - (PULL * depth_face) * ((h_hi - h_lo) + slope)
    loss = jnp.exp2(jnp.log2(depth_face) * (-7.0 / 3.0))
    return drive / (1.0 + (rub * jnp.abs(flow)) * loss)


def iota(shape, dim):
    return lax.broadcasted_iota(i32, shape, dim)


def route(onehot, rows):
    a = rows.astype(bf16)
    rest = rows - a.astype(f32)
    b = rest.astype(bf16)
    c = (rest - b.astype(f32)).astype(bf16)
    take = onehot.astype(bf16)

    def part(x):
        return jnp.dot(take, x, preferred_element_type=f32)

    return part(a) + part(b) + part(c)


def side_links(nb_ref, base, side):
    link = nb_ref[:, side : side + 1].astype(f32) - base.astype(f32)
    missing = nb_ref[:, side : side + 1] < 0
    local = (link >= 0.0) & (link < SLOTS)
    far = jnp.where(missing | local, 0.0, 1.0)
    square = (SLOTS, SLOTS)
    rows = iota(square, 0)
    cols = iota(square, 1)
    link_b = jnp.broadcast_to(link, square)
    far_b = jnp.broadcast_to(far, square)
    near = jnp.where(link_b == cols.astype(f32), 1.0, 0.0)
    link_row = jnp.sum(jnp.where(rows == cols, link_b, 0.0), 0, keepdims=True)
    far_row = jnp.sum(jnp.where(rows == cols, far_b, 0.0), 0, keepdims=True)
    rank = jnp.sum(jnp.where(link_row < link_b, jnp.broadcast_to(far_row, square), 0.0), 1, keepdims=True)
    order_row = jnp.sum(jnp.where(rows < cols, far_b, 0.0), 0, keepdims=True)
    place = jnp.where(
        (jnp.broadcast_to(rank, (SLOTS, MOVERS)) == iota((SLOTS, MOVERS), 1).astype(f32))
        & (jnp.broadcast_to(far, (SLOTS, MOVERS)) > 0.0),
        1.0,
        0.0,
    )
    pick = jnp.where(
        (jnp.broadcast_to(order_row, (MOVERS, SLOTS)) == iota((MOVERS, SLOTS), 0).astype(f32))
        & (jnp.broadcast_to(far_row, (MOVERS, SLOTS)) > 0.0),
        1.0,
        0.0,
    )
    exists = jnp.where(missing, 0.0, 1.0)
    return near, place, pick, exists


def halo_of(links, rows, message):
    near, place, _, _ = links
    return route(near, rows) + route(place, message)


def extract_kernel(moves, base, depth, discharge, bed, friction, frames, up_out, down_out, lo_acc, hi_acc, turned):
    g = pl.program_id(0)
    lane = iota((TILE, TILE), 1)

    def strip(f, k):
        return pl.ds((f * STRIPS + k) * TILE, TILE)

    sources = ((depth, 0, 1), (discharge, 0, 2), (discharge, 1, 2), (bed, 0, 1), (friction, 0, 1))
    home = pl.ds(pl.multiple_of(g * GROUP, GROUP), GROUP)
    for f, (ref, part, parts) in enumerate(sources):
        for k in range(STRIPS):
            row = k if k < DEPTH else TILE - STRIPS + k
            frames[home, strip(f, k)] = ref[pl.ds(part * TILE + row, GROUP, stride=parts * TILE), :]
        high = None
        low = None
        for t in range(GROUP):
            tile = ref[pl.ds((t * parts + part) * TILE, TILE), :]
            turn = pltpu.roll(tile, DEPTH * t + DEPTH, 1)
            high = turn if t == 0 else jnp.where(lane >= DEPTH * t, turn, high)
            low = turn if t == 0 else jnp.where(lane >= DEPTH * t + DEPTH, turn, low)
        shift = g * (GROUP * DEPTH)
        high = pltpu.roll(high, shift, 1)
        low = pltpu.roll(low, shift, 1)
        hi_acc[f] = jnp.where(lane // (GROUP * DEPTH) == g, high, hi_acc[f])
        lo_acc[f] = jnp.where(((lane + (TILE - DEPTH)) % TILE) // (GROUP * DEPTH) == g, low, lo_acc[f])

    @pl.when(g == pl.num_programs(0) - 1)
    def _():
        for f in range(5):
            to = (0, 2, 1, 3, 4)[f]
            for half in range(2):
                block = hi_acc[f] if half else pltpu.roll(lo_acc[f], TILE - DEPTH, 1)
                turned[...] = block.T
                for k in range(DEPTH):
                    frames[pl.ds(SLOTS, SLOTS), strip(to, half * DEPTH + k)] = turned[pl.ds(k, SLOTS, stride=DEPTH), :]
        shape = (2 * MOVERS, SLOTS)
        pick = jnp.zeros(shape, f32)
        for m in range(MOVERS):
            for way in range(2):
                leaver = moves[way, m, 0] - base[0]
                spot = (iota(shape, 0) == (1 - way) * MOVERS + m) & (iota(shape, 1) == leaver)
                pick = jnp.where(spot, 1.0, pick)
        width = FIELD
        for axis in range(2):
            for c in range(5):
                got = route(pick, frames[pl.ds(axis * SLOTS, SLOTS), pl.ds(c * width, width)])
                to = pl.ds((axis * 5 + c) * width, width)
                up_out[:, to] = got[:MOVERS]
                down_out[:, to] = got[MOVERS:]


def start_chunk(index, moves, base, tiles, box, sem):
    depth, discharge, bed, friction = tiles
    for way in range(2):
        for i in range(PER_ROUND):
            slot = jnp.clip(moves[1 - way, index * PER_ROUND + i, 0] - base[0], 0, SLOTS - 1)
            at = (way * PER_ROUND + i) * 5 * TILE
            one = pl.ds(pl.multiple_of(slot * TILE, TILE), TILE)
            two = pl.ds(pl.multiple_of(slot * (2 * TILE), TILE), 2 * TILE)
            pltpu.make_async_copy(depth.at[one], box.at[pl.ds(at, TILE)], sem).start()
            pltpu.make_async_copy(discharge.at[two], box.at[pl.ds(at + TILE, 2 * TILE)], sem).start()
            pltpu.make_async_copy(bed.at[one], box.at[pl.ds(at + 3 * TILE, TILE)], sem).start()
            pltpu.make_async_copy(friction.at[one], box.at[pl.ds(at + 4 * TILE, TILE)], sem).start()


def forward_chunk(box, up_out, down_out, sem, out_sem):
    pltpu.make_async_copy(box, box, sem).wait()
    body = pl.ds(0, CHUNK_ROWS)
    for way, out in enumerate((up_out, down_out)):
        pltpu.make_async_copy(box.at[pl.ds(way * CHUNK_ROWS, CHUNK_ROWS)], out.at[body], out_sem.at[way]).start()


def finish_chunk(extra_up, extra_down, up_out, down_out, out_sem):
    edge = pl.ds(CHUNK_ROWS, extra_up.shape[0])
    pltpu.make_async_copy(extra_up, up_out.at[edge], out_sem.at[2]).start()
    pltpu.make_async_copy(extra_down, down_out.at[edge], out_sem.at[3]).start()
    body = pl.ds(0, CHUNK_ROWS)
    for way, out in enumerate((up_out, down_out)):
        pltpu.make_async_copy(out.at[body], out.at[body], out_sem.at[way]).wait()
        pltpu.make_async_copy(out.at[edge], out.at[edge], out_sem.at[2 + way]).wait()


def settle_kernel(
    moves, base, nb, frames, from_low, from_high, depth, discharge, bed, friction,
    dyn, fixed, x_up, x_down, y_up, y_down, edge_up, edge_down, box, sem, out_sem,
):
    start_chunk(0, moves, base, (depth, discharge, bed, friction), box, sem)
    shape = (SLOTS, 2 * MOVERS)
    land = jnp.zeros(shape, f32)
    left = jnp.zeros((SLOTS, TILE), f32)
    for m in range(MOVERS):
        for way in range(2):
            lander = moves[way, m, 1] - base[0]
            leaver = moves[way, m, 0] - base[0]
            spot = (iota(shape, 0) == lander) & (iota(shape, 1) == way * MOVERS + m)
            land = jnp.where(spot, 1.0, land)
            row = iota((SLOTS, TILE), 0)
            left = jnp.where((row == leaver) | (row == lander), 1.0, left)
    for axis in range(2):
        home = pl.ds(axis * SLOTS, SLOTS)
        for f in range(5):
            part = pl.ds(f * FIELD, FIELD)
            came = pl.ds((axis * 5 + f) * FIELD, FIELD)
            fresh = route(land, jnp.concatenate([from_low[:, came], from_high[:, came]], 0))
            for k in range(STRIPS):
                sub = pl.ds(f * FIELD + k * TILE, TILE)
                value = jnp.where(left > 0.0, 0.0, frames[home, sub]) + fresh[:, k * TILE : (k + 1) * TILE]
                if f < 3:
                    dyn[home, sub] = value
                else:
                    fixed[home, pl.ds((f - 3) * FIELD + k * TILE, TILE)] = value

    forward_chunk(box, y_up, y_down, sem, out_sem)

    def edge(ref, axis, f, k):
        return ref[pl.ds(axis * SLOTS, SLOTS), pl.ds(f * FIELD + k * TILE, TILE)]

    last = STRIPS - 1
    for axis, up, down in ((0, x_up, x_down), (1, edge_up, edge_down)):
        lower = side_links(nb, base[0], 2 * axis)
        higher = side_links(nb, base[0], 2 * axis + 1)
        ups = (edge(dyn, axis, 0, last), edge(fixed, axis, 0, last), edge(fixed, axis, 1, last), edge(dyn, axis, 1, last))
        downs = (edge(dyn, axis, 0, 0), edge(fixed, axis, 0, 0), edge(fixed, axis, 1, 0))
        for f, rows in enumerate(ups):
            up[pl.ds(f * MOVERS, MOVERS), :] = route(higher[2], rows)
        for f, rows in enumerate(downs):
            down[pl.ds(f * MOVERS, MOVERS), :] = route(lower[2], rows)
        down[pl.ds(3 * MOVERS, MOVERS), :] = jnp.zeros((MOVERS, TILE), f32)
    finish_chunk(edge_up, edge_down, y_up, y_down, out_sem)


def other_axis(x):
    return jnp.concatenate([x[SLOTS:], x[:SLOTS]], 0)


def gather_halos(nb, base, dyn, fixed, messages, first):
    last = STRIPS - 1
    out = {}
    parts = {name: [] for name in ("h_lo", "h_hi", "z_lo", "n_lo", "q_lo", "z_hi", "n_hi", "lo", "hi")}
    picks = []
    for axis in range(2):
        home = pl.ds(axis * SLOTS, SLOTS)
        lower = side_links(nb, base, 2 * axis)
        higher = side_links(nb, base, 2 * axis + 1)
        picks.append((lower[2], higher[2]))
        from_lower, from_higher = messages[axis]

        def strip(ref, f, k):
            return ref[home, pl.ds(f * FIELD + k * TILE, TILE)]

        def low(f, rows):
            return halo_of(lower, rows, from_lower[pl.ds(f * MOVERS, MOVERS), :])

        def high(f, rows):
            return halo_of(higher, rows, from_higher[pl.ds(f * MOVERS, MOVERS), :])

        parts["h_lo"].append(low(0, strip(dyn, 0, last)))
        parts["h_hi"].append(high(0, strip(dyn, 0, 0)))
        if first:
            parts["z_lo"].append(low(1, strip(fixed, 0, last)))
            parts["n_lo"].append(low(2, strip(fixed, 1, last)))
            parts["q_lo"].append(low(3, strip(dyn, 1, last)))
            parts["z_hi"].append(high(1, strip(fixed, 0, 0)))
            parts["n_hi"].append(high(2, strip(fixed, 1, 0)))
        parts["lo"].append(jnp.broadcast_to(lower[3], (SLOTS, TILE)))
        parts["hi"].append(jnp.broadcast_to(higher[3], (SLOTS, TILE)))
    for name, pieces in parts.items():
        if pieces:
            out[name] = jnp.concatenate(pieces, 0)
    return out, picks


def step_kernel(turn, moves, base, nb, dyn, fixed, *rest):
    first = turn == 0
    if first:
        still = None
        (xl, xh, yl, yh), rest = rest[:4], rest[4:]
    else:
        still = rest[0]
        (xl, xh, yl, yh), rest = rest[1:5], rest[5:]
    depth, discharge, bed, friction = rest[:4]
    (dyn_out, still_out, trail, x_up, x_down, y_up, y_down, edge_up, edge_down, box, sem, out_sem) = rest[4:]
    start_chunk(turn + 1, moves, base, (depth, discharge, bed, friction), box, sem)
    halo, picks = gather_halos(nb, base[0], dyn, fixed, ((xl, xh), (yl, yh)), first)
    names = ("z_lo", "n_lo", "z_hi", "n_hi", "q_lo")
    if not first:
        for j, name in enumerate(names):
            halo[name] = still[:, pl.ds(j * TILE, TILE)]

    def get(ref, f, k):
        return ref[:, pl.ds(f * FIELD + k * TILE, TILE)]

    last = STRIPS - 1
    h = [get(dyn, 0, k) for k in range(STRIPS)]
    z = [get(fixed, 0, k) for k in range(STRIPS)]
    n = [get(fixed, 1, k) for k in range(STRIPS)]
    low_face = flux(halo["q_lo"], halo["h_lo"], h[0], z[0] - halo["z_lo"], RUB * (halo["n_lo"] + n[0]))
    low_face = jnp.where(halo["lo"] > 0.0, low_face, 0.0)
    high_face = flux(get(dyn, 1, last), h[last], halo["h_hi"], halo["z_hi"] - z[last], RUB * (n[last] + halo["n_hi"]))
    high_face = jnp.where(halo["hi"] > 0.0, high_face, 0.0)
    for j, name in enumerate(names[:4]):
        still_out[:, pl.ds(j * TILE, TILE)] = halo[name]
    still_out[:, pl.ds(4 * TILE, TILE)] = low_face
    trail[:, pl.ds(0, TILE)] = low_face
    trail[:, pl.ds(TILE, TILE)] = halo["h_hi"]

    forward_chunk(box, y_up, y_down, sem, out_sem)
    lane = iota((2 * SLOTS, TILE), 1)
    side_h = other_axis(halo["h_hi"])
    side_z = other_axis(halo["z_hi"])
    side_n = other_axis(halo["n_hi"])
    side_wall = other_axis(halo["hi"]) <= 0.0
    side_in = other_axis(low_face)

    def cell(x, k):
        at = k if k < DEPTH else TILE - STRIPS + k
        return jnp.broadcast_to(x[:, at : at + 1], x.shape)

    def ahead(x, k, side):
        return jnp.where(lane == TILE - 1, cell(side, k), pltpu.roll(x, TILE - 1, 1))

    reach = DEPTH - 1 - turn
    low_keep = list(range(reach))
    high_keep = list(range(STRIPS - reach, STRIPS))
    face = {-1: low_face, last: high_face}
    for k in low_keep + [x - 1 for x in high_keep]:
        face[k] = flux(get(dyn, 1, k), h[k], h[k + 1], z[k + 1] - z[k], RUB * (n[k] + n[k + 1]))
    new = {}
    for k in low_keep + high_keep:
        side = flux(
            get(dyn, 2, k), h[k], ahead(h[k], k, side_h), ahead(z[k], k, side_z) - z[k],
            RUB * (n[k] + ahead(n[k], k, side_n)),
        )
        side = jnp.where((lane == TILE - 1) & side_wall, 0.0, side)
        before = jnp.where(lane == 0, cell(side_in, k), pltpu.roll(side, 1, 1))
        new[k] = h[k] + GAIN * ((face[k - 1] - face[k]) + (before - side))
        dyn_out[:, pl.ds(2 * FIELD + k * TILE, TILE)] = side
    blank = jnp.zeros((2 * SLOTS, TILE), f32)
    for k in range(STRIPS):
        dyn_out[:, pl.ds(k * TILE, TILE)] = new[k] if k in new else blank
        dyn_out[:, pl.ds(FIELD + k * TILE, TILE)] = face[k] if k in face else blank
        if k not in new:
            dyn_out[:, pl.ds(2 * FIELD + k * TILE, TILE)] = blank
    for axis, up, down in ((0, x_up, x_down), (1, edge_up, edge_down)):
        home = slice(axis * SLOTS, (axis + 1) * SLOTS)
        up[...] = route(picks[axis][1], new[last][home])
        down[...] = route(picks[axis][0], new[0][home])
    finish_chunk(edge_up, edge_down, y_up, y_down, out_sem)


def tile_kernel(
    moves, base, ids, nb_s, nb, dyn, fixed, still, xl, xh, yl, yh, t0, t1, t2,
    depth, discharge, bed, friction, l0, l1, l2, l3, u0, u1, u2, u3,
    depth_out, flow_out,
    inbox, outbox, zeros, edges, columns, turned, water, stream_x, stream_y, slope_x, slope_y, rub_x, rub_y, origin,
    in_sem, out_sem, zero_sem,
):
    lows = (l0, l1, l2, l3)
    highs = (u0, u1, u2, u3)

    def count_live(t, total):
        origin[t] = 0
        return total + jnp.where(ids[t] >= 0, 1, 0)

    live = lax.fori_loop(0, SLOTS, count_live, 0)
    for m in range(MOVERS):
        for way in range(2):
            lander = moves[way, m, 1]

            @pl.when(lander >= 0)
            def _():
                origin[lander - base[0]] = 1 + way * MOVERS + m

    def fetch(t):
        buf = t % BUFFERS
        sem = in_sem.at[buf]
        box = inbox.at[buf]
        kind = origin[t]

        @pl.when(kind == 0)
        def _():
            one = pl.ds(pl.multiple_of(t * TILE, TILE), TILE)
            two = pl.ds(pl.multiple_of(t * (2 * TILE), TILE), 2 * TILE)
            pltpu.make_async_copy(depth.at[one], box.at[pl.ds(0, TILE)], sem).start()
            pltpu.make_async_copy(discharge.at[two], box.at[pl.ds(TILE, 2 * TILE)], sem).start()
            pltpu.make_async_copy(bed.at[one], box.at[pl.ds(3 * TILE, TILE)], sem).start()
            pltpu.make_async_copy(friction.at[one], box.at[pl.ds(4 * TILE, TILE)], sem).start()

        for way, chunks in ((0, lows), (1, highs)):
            for m in range(MOVERS):

                @pl.when(kind == 1 + way * MOVERS + m)
                def _():
                    src = chunks[m // PER_ROUND].at[pl.ds((m % PER_ROUND) * 5 * TILE, 5 * TILE)]
                    pltpu.make_async_copy(src, box, sem).start()

    def arrived(buf):
        box = inbox.at[buf]
        pltpu.make_async_copy(box, box, in_sem.at[buf]).wait()

    def send(t, buf):
        box = outbox.at[buf]
        one = pl.ds(pl.multiple_of(t * TILE, TILE), TILE)
        two = pl.ds(pl.multiple_of(t * (2 * TILE), TILE), 2 * TILE)
        pltpu.make_async_copy(box.at[pl.ds(0, TILE)], depth_out.at[one], out_sem.at[buf]).start()
        pltpu.make_async_copy(box.at[pl.ds(TILE, 2 * TILE)], flow_out.at[two], out_sem.at[buf]).start()

    def sent(buf):
        box = outbox.at[buf]
        pltpu.make_async_copy(box, box, out_sem.at[buf]).wait()

    for t in range(BUFFERS - 1):

        @pl.when(t < live)
        def _():
            fetch(t)

    zeros[...] = jnp.zeros(zeros.shape, f32)

    def blank(t, carry):
        one = pl.ds(pl.multiple_of(t * TILE, TILE), TILE)
        two = pl.ds(pl.multiple_of(t * (2 * TILE), TILE), 2 * TILE)
        pltpu.make_async_copy(zeros.at[pl.ds(0, TILE)], depth_out.at[one], zero_sem).start()
        pltpu.make_async_copy(zeros.at[pl.ds(TILE, 2 * TILE)], flow_out.at[two], zero_sem).start()
        return carry

    lax.fori_loop(live, SLOTS, blank, 0)

    last = STRIPS - 1
    halo, _ = gather_halos(nb, base[0], dyn, fixed, ((xl, xh), (yl, yh)), False)

    def kept(j):
        return still[:, pl.ds(j * TILE, TILE)]

    n_first = fixed[:, pl.ds(FIELD, TILE)]
    z_first = fixed[:, pl.ds(0, TILE)]
    low_face = flux(
        kept(4), halo["h_lo"], dyn[:, pl.ds(0, TILE)], z_first - kept(0), RUB * (kept(1) + n_first)
    )
    low_face = jnp.where(halo["lo"] > 0.0, low_face, 0.0)
    trails = [(t[:, pl.ds(0, TILE)], t[:, pl.ds(TILE, TILE)]) for t in (t0, t1, t2)]
    trails.append((low_face, halo["h_hi"]))
    for s, (inflow, ahead_h) in enumerate(trails):
        edges[s] = inflow[:SLOTS]
        edges[4 + s] = ahead_h[:SLOTS]
        turned[pl.ds(64 * (s % 2), SLOTS, stride=2), :] = ahead_h[SLOTS:]
        turned[pl.ds(64 * (s % 2) + 1, SLOTS, stride=2), :] = inflow[SLOTS:]
        if s % 2:
            columns[s // 2] = turned[...].T
    edges[8] = kept(2)[:SLOTS]
    edges[9] = kept(3)[:SLOTS]
    turned[pl.ds(0, SLOTS), :] = kept(2)[SLOTS:]
    turned[pl.ds(SLOTS, SLOTS), :] = kept(3)[SLOTS:]
    columns[2] = turned[...].T

    part_rows = 32
    parts = TILE // part_rows
    lane = iota((part_rows, TILE), 1)
    row = iota((part_rows, TILE), 0)
    at_first = lane == 0
    at_last = lane == TILE - 1
    bottom = row == part_rows - 1

    def one_tile(t, carry):
        buf = t % BUFFERS

        @pl.when(t + BUFFERS - 1 < live)
        def _():
            fetch(t + BUFFERS - 1)

        arrived(buf)

        @pl.when(t >= BUFFERS)
        def _():
            sent(buf)

        box = inbox.at[buf]
        out = outbox.at[buf]
        wall_x = nb_s[t, 1] < 0
        wall_y = nb_s[t, 3] < 0

        def edge_row(j):
            return edges[j, pl.ds(t, 1), :]

        z_next = edge_row(8)
        n_next = edge_row(9)
        for p in range(parts):
            rows = pl.ds(p * part_rows, part_rows)
            zr = pl.ds(3 * TILE + p * part_rows, part_rows)
            nr = pl.ds(4 * TILE + p * part_rows, part_rows)
            z = box[zr, :]
            n = box[nr, :]
            if p < parts - 1:
                z_dn = box[pl.ds(3 * TILE + p * part_rows + 1, part_rows), :]
                n_dn = box[pl.ds(4 * TILE + p * part_rows + 1, part_rows), :]
            else:
                z_dn = jnp.where(bottom, z_next, pltpu.roll(z, part_rows - 1, 0))
                n_dn = jnp.where(bottom, n_next, pltpu.roll(n, part_rows - 1, 0))
            side = columns[2, rows, :]
            z_rt = jnp.where(at_last, pltpu.roll(side, TILE - 1 - t, 1), pltpu.roll(z, TILE - 1, 1))
            n_rt = jnp.where(at_last, pltpu.roll(side, TILE - 1 - SLOTS - t, 1), pltpu.roll(n, TILE - 1, 1))
            slope_x[rows, :] = z_dn - z
            slope_y[rows, :] = z_rt - z
            rub_x[rows, :] = RUB * (n + n_dn)
            rub_y[rows, :] = RUB * (n + n_rt)
            water[pl.ds(p * part_rows, part_rows), :] = box[rows, :]
        for s in range(4):
            water[pl.ds(TILE, 1), :] = edge_row(4 + s)
            stream_x[pl.ds(7, 1), :] = edge_row(s)
            for p in range(parts):
                rows = pl.ds(p * part_rows, part_rows)
                h = water[rows, :]
                h_dn = water[pl.ds(p * part_rows + 1, part_rows), :]
                side = pltpu.roll(columns[s // 2, rows, :], TILE - 1 - 64 * (s % 2) - 2 * t, 1)
                h_rt = jnp.where(at_last, side, pltpu.roll(h, TILE - 1, 1))
                if s == 0:
                    flow_x = box[pl.ds(TILE + p * part_rows, part_rows), :]
                    flow_y = box[pl.ds(2 * TILE + p * part_rows, part_rows), :]
                else:
                    flow_x = stream_x[pl.ds(8 + p * part_rows, part_rows), :]
                    flow_y = stream_y[rows, :]
                new_x = flux(flow_x, h, h_dn, slope_x[rows, :], rub_x[rows, :])
                if p == parts - 1:
                    new_x = jnp.where(bottom & wall_x, 0.0, new_x)
                new_y = flux(flow_y, h, h_rt, slope_y[rows, :], rub_y[rows, :])
                new_y = jnp.where(at_last & wall_y, 0.0, new_y)
                if s < 3:
                    stream_y[rows, :] = new_y
                else:
                    out[pl.ds(TILE + p * part_rows, part_rows), :] = new_x
                    out[pl.ds(2 * TILE + p * part_rows, part_rows), :] = new_y
                in_y = jnp.where(at_first, side, pltpu.roll(new_y, 1, 1))
                stream_x[pl.ds(8 + p * part_rows, part_rows), :] = new_x
                in_x = stream_x[pl.ds(7 + p * part_rows, part_rows), :]
                h_new = h + GAIN * ((in_x - new_x) + (in_y - new_y))
                if s < 3:
                    water[rows, :] = h_new
                else:
                    out[rows, :] = h_new
        send(t, buf)
        return carry

    lax.fori_loop(0, live, one_tile, 0)
    for b in range(BUFFERS):

        @pl.when(b < live)
        def _():
            sent(b)

    def blanked(t, carry):
        pltpu.make_async_copy(zeros, zeros, zero_sem).wait()
        return carry

    lax.fori_loop(live, SLOTS, blanked, 0)


SMEM = pl.BlockSpec(memory_space=pltpu.SMEM)
VMEM = pl.BlockSpec(memory_space=pltpu.VMEM)
ANY = pl.BlockSpec(memory_space=pl.ANY)


def shifted(block, axis, distance):
    devices = range(lax.axis_size(axis))
    route_pairs = [(i - distance, i) for i in devices if i - distance in devices]
    return lax.ppermute(block, axis, route_pairs)


def exchange(x_up, x_down, y_up, y_down):
    got_y = shifted(y_up, "gy", 1), shifted(y_down, "gy", -1)
    got_x = shifted(x_up, "gx", 1), shifted(x_down, "gx", -1)
    return got_x[0], got_x[1], got_y[0], got_y[1]


def struct(*shape):
    return jax.ShapeDtypeStruct(shape, f32)


def shards(depth, discharge, bed, friction, tile_ids, neighbors, moves):
    base = (lax.axis_index(("gx", "gy")) * SLOTS).astype(i32).reshape(1)
    plan = moves[0]
    tiles = (
        depth.reshape(SLOTS * TILE, TILE),
        discharge.reshape(SLOTS * 2 * TILE, TILE),
        bed.reshape(SLOTS * TILE, TILE),
        friction.reshape(SLOTS * TILE, TILE),
    )
    one = pl.BlockSpec((GROUP * TILE, TILE), lambda g: (g, 0))
    two = pl.BlockSpec((GROUP * 2 * TILE, TILE), lambda g: (g, 0))

    def whole(*shape):
        return pl.BlockSpec(shape, lambda g: (0,) * len(shape))

    frames, up, down = pl.pallas_call(
        extract_kernel,
        grid=(SLOTS // GROUP,),
        in_specs=[SMEM, SMEM, one, two, one, one],
        out_specs=[whole(2 * SLOTS, 5 * FIELD), whole(MOVERS, 10 * FIELD), whole(MOVERS, 10 * FIELD)],
        out_shape=[struct(2 * SLOTS, 5 * FIELD), struct(MOVERS, 10 * FIELD), struct(MOVERS, 10 * FIELD)],
        scratch_shapes=[
            pltpu.VMEM((5, TILE, TILE), f32),
            pltpu.VMEM((5, TILE, TILE), f32),
            pltpu.VMEM((TILE, TILE), f32),
        ],
        name="extract",
    )(plan, base, *tiles)
    from_low = shifted(up, "gy", 1)
    from_high = shifted(down, "gy", -1)

    def chunk_scratch(rows):
        return [
            pltpu.VMEM((rows, TILE), f32),
            pltpu.VMEM((rows, TILE), f32),
            pltpu.VMEM((2 * CHUNK_ROWS, TILE), f32),
            pltpu.SemaphoreType.DMA,
            pltpu.SemaphoreType.DMA((4,)),
        ]

    first_rows = 4 * MOVERS
    dyn, fixed, *sends = pl.pallas_call(
        settle_kernel,
        in_specs=[SMEM, SMEM, VMEM, VMEM, VMEM, VMEM, ANY, ANY, ANY, ANY],
        out_specs=[VMEM, VMEM, VMEM, VMEM, ANY, ANY],
        out_shape=[
            struct(2 * SLOTS, 3 * FIELD),
            struct(2 * SLOTS, 2 * FIELD),
            struct(first_rows, TILE),
            struct(first_rows, TILE),
            struct(CHUNK_ROWS + first_rows, TILE),
            struct(CHUNK_ROWS + first_rows, TILE),
        ],
        scratch_shapes=chunk_scratch(first_rows),
        name="settle",
    )(plan, base, neighbors, frames, from_low, from_high, *tiles)
    got = exchange(*sends)
    lows = [got[2]]
    highs = [got[3]]
    still = []
    trails = []

    def edge_specs(rows):
        at = CHUNK_ROWS // rows
        return [VMEM, VMEM] + [pl.BlockSpec((rows, TILE), lambda i: (at, 0))] * 2

    def flat(spec, shape):
        return spec

    rows = first_rows
    for turn in range(3):

        def body(*refs, turn=turn):
            step_kernel(turn, *refs)

        at = CHUNK_ROWS // rows
        full = [pl.BlockSpec(a.shape, lambda i: (0, 0)) for a in (neighbors, dyn, fixed, *still)]
        sides = [pl.BlockSpec(got[0].shape, lambda i: (0, 0)), pl.BlockSpec(got[1].shape, lambda i: (0, 0))]
        ends = [pl.BlockSpec((rows, TILE), lambda i, at=at: (at, 0))] * 2
        shapes = [
            (2 * SLOTS, 3 * FIELD),
            (2 * SLOTS, 5 * TILE),
            (2 * SLOTS, 2 * TILE),
            (MOVERS, TILE),
            (MOVERS, TILE),
        ]
        dyn, kept, trail, *sends = pl.pallas_call(
            body,
            grid=(1,),
            in_specs=[SMEM, SMEM, *full, *sides, *ends, ANY, ANY, ANY, ANY],
            out_specs=[pl.BlockSpec(s, lambda i: (0, 0)) for s in shapes] + [ANY, ANY],
            out_shape=[struct(*s) for s in shapes] + [struct(CHUNK_ROWS + MOVERS, TILE)] * 2,
            scratch_shapes=chunk_scratch(MOVERS),
            name="edge_step",
        )(plan, base, neighbors, dyn, fixed, *still, *got, *tiles)
        still = [kept]
        trails.append(trail)
        got = exchange(*sends)
        lows.append(got[2])
        highs.append(got[3])
        rows = MOVERS

    at = CHUNK_ROWS // rows
    full = [pl.BlockSpec(a.shape, lambda i: (0, 0)) for a in (neighbors, dyn, fixed, *still)]
    sides = [pl.BlockSpec(got[0].shape, lambda i: (0, 0)), pl.BlockSpec(got[1].shape, lambda i: (0, 0))]
    ends = [pl.BlockSpec((rows, TILE), lambda i: (at, 0))] * 2
    trail_specs = [pl.BlockSpec(t.shape, lambda i: (0, 0)) for t in trails]
    new_depth, new_flow = pl.pallas_call(
        tile_kernel,
        grid=(1,),
        in_specs=[SMEM, SMEM, SMEM, SMEM, *full, *sides, *ends, *trail_specs, *([ANY] * 12)],
        out_specs=[ANY, ANY],
        out_shape=[struct(SLOTS * TILE, TILE), struct(SLOTS * 2 * TILE, TILE)],
        scratch_shapes=[
            pltpu.VMEM((BUFFERS, 5 * TILE, TILE), f32),
            pltpu.VMEM((BUFFERS, 3 * TILE, TILE), f32),
            pltpu.VMEM((3 * TILE, TILE), f32),
            pltpu.VMEM((10, SLOTS, TILE), f32),
            pltpu.VMEM((3, TILE, TILE), f32),
            pltpu.VMEM((TILE, TILE), f32),
            pltpu.VMEM((TILE + 8, TILE), f32),
            pltpu.VMEM((TILE + 8, TILE), f32),
            pltpu.VMEM((TILE, TILE), f32),
            pltpu.VMEM((TILE, TILE), f32),
            pltpu.VMEM((TILE, TILE), f32),
            pltpu.VMEM((TILE, TILE), f32),
            pltpu.VMEM((TILE, TILE), f32),
            pltpu.SMEM((SLOTS,), i32),
            pltpu.SemaphoreType.DMA((BUFFERS,)),
            pltpu.SemaphoreType.DMA((BUFFERS,)),
            pltpu.SemaphoreType.DMA,
        ],
        name="tiles",
    )(plan, base, tile_ids, neighbors, neighbors, dyn, fixed, *still, *got, *trails, *tiles, *lows, *highs)
    return (
        new_depth.reshape(SLOTS, TILE, TILE),
        new_flow.reshape(SLOTS, 2, TILE, TILE),
    )


def solution(mesh):
    return jax.shard_map(
        shards,
        mesh=mesh,
        in_specs=(
            P(("gx", "gy"), None, None),
            P(("gx", "gy"), None, None, None),
            P(("gx", "gy"), None, None),
            P(("gx", "gy"), None, None),
            P(("gx", "gy")),
            P(("gx", "gy"), None),
            P(("gx", "gy"), None, None, None),
        ),
        out_specs=(P(("gx", "gy"), None, None), P(("gx", "gy"), None, None, None)),
        check_vma=False,
    )
```

```python
import jax
import jax.numpy as jnp
from jax import lax
from jax.experimental import pallas as pl
from jax.experimental.pallas import tpu as pltpu
from jax.sharding import PartitionSpec as P


TILE = 128
SLOTS = 32
MOVERS = 8
DEPTH = 4
STRIPS = 2 * DEPTH
FIELD = STRIPS * TILE
STATE = 5 * TILE
EARLY = (0, 1)
RIDERS = (2, 3, 4, 5)
LATE = (6, 7)
GROUP = 8
GY = 16
BUFFERS = 4

gravity = 9.81
step_time = 0.25
spacing = 2.0
min_depth = 0.15
PULL = gravity * step_time / spacing
RUB = gravity * step_time * 0.5
GAIN = step_time / spacing

f32 = jnp.float32
bf16 = jnp.bfloat16
i32 = jnp.int32


def flux(flow, h_lo, h_hi, slope, rub):
    depth_face = jnp.maximum(0.5 * (h_lo + h_hi), min_depth)
    drive = flow - (PULL * depth_face) * ((h_hi - h_lo) + slope)
    loss = jnp.exp2(jnp.log2(depth_face) * (-7.0 / 3.0))
    return drive / (1.0 + (rub * jnp.abs(flow)) * loss)


def iota(shape, dim):
    return lax.broadcasted_iota(i32, shape, dim)


def route(onehot, rows):
    a = rows.astype(bf16)
    rest = rows - a.astype(f32)
    b = rest.astype(bf16)
    c = (rest - b.astype(f32)).astype(bf16)
    take = onehot.astype(bf16)

    def part(x):
        return jnp.dot(take, x, preferred_element_type=f32)

    return part(a) + part(b) + part(c)


def side_links(nb_ref, base, side):
    square = (SLOTS, SLOTS)
    rows = iota(square, 0)
    cols = iota(square, 1)
    link_row = jnp.broadcast_to(nb_ref[side : side + 1, :].astype(f32), square)
    diagonal = rows == cols

    def column(x):
        return jnp.broadcast_to(jnp.sum(jnp.where(diagonal, x, 0.0), 1, keepdims=True), square)

    first = base.astype(f32)

    def remote(link):
        return jnp.where((link >= 0.0) & ((link < first) | (link >= first + SLOTS)), 1.0, 0.0)

    link_b = column(link_row)
    missing = link_b[:, :1] < 0.0
    far_b = remote(link_b)
    far = far_b[:, :1]
    far_row = remote(link_row)
    near = jnp.where(link_b - first == cols.astype(f32), 1.0, 0.0)
    rank = jnp.sum(jnp.where(link_row < link_b, far_row, 0.0), 1, keepdims=True)
    order_row = jnp.sum(jnp.where(rows < cols, far_b, 0.0), 0, keepdims=True)
    far_row = far_row[:1]
    place = jnp.where(
        (jnp.broadcast_to(rank, (SLOTS, MOVERS)) == iota((SLOTS, MOVERS), 1).astype(f32))
        & (jnp.broadcast_to(far, (SLOTS, MOVERS)) > 0.0),
        1.0,
        0.0,
    )
    pick = jnp.where(
        (jnp.broadcast_to(order_row, (MOVERS, SLOTS)) == iota((MOVERS, SLOTS), 0).astype(f32))
        & (jnp.broadcast_to(far_row, (MOVERS, SLOTS)) > 0.0),
        1.0,
        0.0,
    )
    exists = jnp.where(missing, 0.0, 1.0)
    return near, place, pick, exists


def halo_of(links, rows, message):
    near, place, _, _ = links
    return route(near, rows) + route(place, message)


def extract_kernel(
    moves, base, depth, discharge, bed, friction, frames, up_out, down_out, early_up, early_down,
    depth_v, flow_v, bed_v, rough_v, lo_acc, hi_acc, turned, load_sem, sem,
):
    lane = iota((TILE, TILE), 1)
    groups = SLOTS // GROUP
    loads = []
    for g in range(groups):
        one = pl.ds(g * GROUP * TILE, GROUP * TILE)
        two = pl.ds(g * GROUP * 2 * TILE, GROUP * 2 * TILE)
        pairs = ((depth, depth_v, one), (discharge, flow_v, two), (bed, bed_v, one), (friction, rough_v, one))
        copies = [pltpu.make_async_copy(a.at[r], b.at[r], load_sem.at[g, i]) for i, (a, b, r) in enumerate(pairs)]
        for c in copies:
            c.start()
        loads.append(copies)
    start_chunk(EARLY, moves, base, (depth, discharge, bed, friction), early_up, early_down, sem)

    def strip(f, k):
        return pl.ds((f * STRIPS + k) * TILE, TILE)

    sources = ((depth_v, 0, 1), (flow_v, 0, 2), (flow_v, 1, 2), (bed_v, 0, 1), (rough_v, 0, 1))
    for g in range(groups):
        for c in loads[g]:
            c.wait()
        home = pl.ds(g * GROUP, GROUP)
        for f, (ref, part, parts) in enumerate(sources):
            top = (g * GROUP * parts + part) * TILE
            for k in range(STRIPS):
                row = k if k < DEPTH else TILE - STRIPS + k
                frames[home, strip(f, k)] = ref[pl.ds(top + row, GROUP, stride=parts * TILE), :]
            high = hi_acc[f] if g else None
            low = lo_acc[f] if g else None
            for t in range(GROUP):
                tile = ref[pl.ds(top + t * parts * TILE, TILE), :]
                at = g * GROUP * DEPTH + DEPTH * t
                turn = pltpu.roll(tile, (at + DEPTH) % TILE, 1)
                high = turn if high is None else jnp.where(lane >= at, turn, high)
                if low is None:
                    low = turn
                elif at + DEPTH < TILE:
                    low = jnp.where(lane >= at + DEPTH, turn, low)
                else:
                    low = jnp.where(lane < DEPTH, turn, low)
            hi_acc[f] = high
            lo_acc[f] = low

    for f in range(5):
        to = (0, 2, 1, 3, 4)[f]
        for half in range(2):
            block = hi_acc[f] if half else pltpu.roll(lo_acc[f], TILE - DEPTH, 1)
            turned[...] = block.T
            for k in range(DEPTH):
                frames[pl.ds(SLOTS, SLOTS), strip(to, half * DEPTH + k)] = turned[pl.ds(k, SLOTS, stride=DEPTH), :]
    shape = (2 * MOVERS, SLOTS)
    pick = jnp.zeros(shape, f32)
    for m in range(MOVERS):
        for way in range(2):
            leaver = moves[way, 0, m] - base[0]
            spot = (iota(shape, 0) == (1 - way) * MOVERS + m) & (iota(shape, 1) == leaver)
            pick = jnp.where(spot, 1.0, pick)
    for axis in range(2):
        for c in range(5):
            got = route(pick, frames[pl.ds(axis * SLOTS, SLOTS), pl.ds(c * FIELD, FIELD)])
            to = pl.ds((axis * 5 + c) * FIELD, FIELD)
            up_out[:, to] = got[:MOVERS]
            down_out[:, to] = got[MOVERS:]
    finish_chunk(EARLY, early_up, early_down, sem)


def start_chunk(entries, moves, base, tiles, up_out, down_out, sem):
    depth, discharge, bed, friction = tiles
    for way, out in ((1, up_out), (0, down_out)):
        for i, m in enumerate(entries):
            slot = jnp.clip(moves[way, 0, m] - base[0], 0, SLOTS - 1)
            at = i * STATE
            one = pl.ds(pl.multiple_of(slot * TILE, TILE), TILE)
            two = pl.ds(pl.multiple_of(slot * (2 * TILE), TILE), 2 * TILE)
            pltpu.make_async_copy(depth.at[one], out.at[pl.ds(at, TILE)], sem.at[way]).start()
            pltpu.make_async_copy(discharge.at[two], out.at[pl.ds(at + TILE, 2 * TILE)], sem.at[way]).start()
            pltpu.make_async_copy(bed.at[one], out.at[pl.ds(at + 3 * TILE, TILE)], sem.at[way]).start()
            pltpu.make_async_copy(friction.at[one], out.at[pl.ds(at + 4 * TILE, TILE)], sem.at[way]).start()


def finish_chunk(entries, up_out, down_out, sem):
    body = pl.ds(0, len(entries) * STATE)
    for way, out in ((1, up_out), (0, down_out)):
        pltpu.make_async_copy(out.at[body], out.at[body], sem.at[way]).wait()


def is_odd(base):
    return ((base[0] // (SLOTS * GY)) % 2) == 1


def swap(odd, a, b):
    return jnp.where(odd, b, a), jnp.where(odd, a, b)


def settle_kernel(
    moves, base, nb, frames, from_low, from_high, depth, discharge, bed, friction,
    dyn, fixed, x_0, x_1, y_up, y_down, sem,
):
    ride = RIDERS[:1]
    start_chunk(ride, moves, base, (depth, discharge, bed, friction), y_up, y_down, sem)
    shape = (SLOTS, 2 * MOVERS)
    land = jnp.zeros(shape, f32)
    left = jnp.zeros((SLOTS, TILE), f32)
    for m in range(MOVERS):
        for way in range(2):
            lander = moves[way, 1, m] - base[0]
            leaver = moves[way, 0, m] - base[0]
            spot = (iota(shape, 0) == lander) & (iota(shape, 1) == way * MOVERS + m)
            land = jnp.where(spot, 1.0, land)
            row = iota((SLOTS, TILE), 0)
            left = jnp.where((row == leaver) | (row == lander), 1.0, left)
    for axis in range(2):
        home = pl.ds(axis * SLOTS, SLOTS)
        for f in range(5):
            part = pl.ds(f * FIELD, FIELD)
            came = pl.ds((axis * 5 + f) * FIELD, FIELD)
            fresh = route(land, jnp.concatenate([from_low[:, came], from_high[:, came]], 0))
            for k in range(STRIPS):
                sub = pl.ds(f * FIELD + k * TILE, TILE)
                value = jnp.where(left > 0.0, 0.0, frames[home, sub]) + fresh[:, k * TILE : (k + 1) * TILE]
                if f < 3:
                    dyn[home, sub] = value
                else:
                    fixed[home, pl.ds((f - 3) * FIELD + k * TILE, TILE)] = value

    def edge(ref, axis, f, k):
        return ref[pl.ds(axis * SLOTS, SLOTS), pl.ds(f * FIELD + k * TILE, TILE)]

    last = STRIPS - 1
    blank = jnp.zeros((MOVERS, TILE), f32)
    for axis in range(2):
        lower = side_links(nb, base[0], 2 * axis)
        higher = side_links(nb, base[0], 2 * axis + 1)
        ups = (edge(dyn, axis, 0, last), edge(fixed, axis, 0, last), edge(fixed, axis, 1, last), edge(dyn, axis, 1, last))
        downs = (edge(dyn, axis, 0, 0), edge(fixed, axis, 0, 0), edge(fixed, axis, 1, 0))
        for f in range(4):
            up = route(higher[2], ups[f])
            down = route(lower[2], downs[f]) if f < 3 else blank
            if axis == 0:
                up, down = swap(is_odd(base), up, down)
                x_0[pl.ds(f * MOVERS, MOVERS), :] = up
                x_1[pl.ds(f * MOVERS, MOVERS), :] = down
            else:
                y_up[pl.ds(STATE + f * MOVERS, MOVERS), :] = up
                y_down[pl.ds(STATE + f * MOVERS, MOVERS), :] = down
    finish_chunk(ride, y_up, y_down, sem)


def other_axis(x):
    return jnp.concatenate([x[SLOTS:], x[:SLOTS]], 0)


def gather_halos(nb, base_ref, dyn, fixed, messages, first):
    last = STRIPS - 1
    out = {}
    parts = {name: [] for name in ("h_lo", "h_hi", "z_lo", "n_lo", "q_lo", "z_hi", "n_hi", "lo", "hi")}
    picks = []
    for axis in range(2):
        home = pl.ds(axis * SLOTS, SLOTS)
        lower = side_links(nb, base_ref[0], 2 * axis)
        higher = side_links(nb, base_ref[0], 2 * axis + 1)
        picks.append((lower[2], higher[2]))

        def message(f):
            if axis == 0:
                rows = pl.ds(f * MOVERS, MOVERS)
                from_higher, from_lower = swap(is_odd(base_ref), messages[0][0][rows, :], messages[0][1][rows, :])
                return from_lower, from_higher
            rows = pl.ds(STATE + f * MOVERS, MOVERS)
            return messages[1][0][rows, :], messages[1][1][rows, :]

        def strip(ref, f, k):
            return ref[home, pl.ds(f * FIELD + k * TILE, TILE)]

        def low(f, rows):
            return halo_of(lower, rows, message(f)[0])

        def high(f, rows):
            return halo_of(higher, rows, message(f)[1])

        parts["h_lo"].append(low(0, strip(dyn, 0, last)))
        parts["h_hi"].append(high(0, strip(dyn, 0, 0)))
        if first:
            parts["z_lo"].append(low(1, strip(fixed, 0, last)))
            parts["n_lo"].append(low(2, strip(fixed, 1, last)))
            parts["q_lo"].append(low(3, strip(dyn, 1, last)))
            parts["z_hi"].append(high(1, strip(fixed, 0, 0)))
            parts["n_hi"].append(high(2, strip(fixed, 1, 0)))
        parts["lo"].append(jnp.broadcast_to(lower[3], (SLOTS, TILE)))
        parts["hi"].append(jnp.broadcast_to(higher[3], (SLOTS, TILE)))
    for name, pieces in parts.items():
        if pieces:
            out[name] = jnp.concatenate(pieces, 0)
    return out, picks


def step_kernel(turn, moves, base, nb, dyn, fixed, *rest):
    first = turn == 0
    if first:
        still = None
        (xl, xh, yl, yh), rest = rest[:4], rest[4:]
    else:
        still = rest[0]
        (xl, xh, yl, yh), rest = rest[1:5], rest[5:]
    depth, discharge, bed, friction = rest[:4]
    tiles = (depth, discharge, bed, friction)
    final = turn == 2
    if final:
        (dyn_out, still_out, trail, x_0, x_1, y_up, y_down, late_up, late_down, sem) = rest[4:]
    else:
        (dyn_out, still_out, trail, x_0, x_1, y_up, y_down, sem) = rest[4:]
    ride = RIDERS[turn + 1 : turn + 2]
    start_chunk(ride, moves, base, tiles, y_up, y_down, sem.at[0])
    if final:
        start_chunk(LATE, moves, base, tiles, late_up, late_down, sem.at[1])
    halo, picks = gather_halos(nb, base, dyn, fixed, ((xl, xh), (yl, yh)), first)
    names = ("z_lo", "n_lo", "z_hi", "n_hi", "q_lo")
    if not first:
        for j, name in enumerate(names):
            halo[name] = still[:, pl.ds(j * TILE, TILE)]

    def get(ref, f, k):
        return ref[:, pl.ds(f * FIELD + k * TILE, TILE)]

    last = STRIPS - 1
    h = [get(dyn, 0, k) for k in range(STRIPS)]
    z = [get(fixed, 0, k) for k in range(STRIPS)]
    n = [get(fixed, 1, k) for k in range(STRIPS)]
    low_face = flux(halo["q_lo"], halo["h_lo"], h[0], z[0] - halo["z_lo"], RUB * (halo["n_lo"] + n[0]))
    low_face = jnp.where(halo["lo"] > 0.0, low_face, 0.0)
    high_face = flux(get(dyn, 1, last), h[last], halo["h_hi"], halo["z_hi"] - z[last], RUB * (n[last] + halo["n_hi"]))
    high_face = jnp.where(halo["hi"] > 0.0, high_face, 0.0)
    for j, name in enumerate(names[:4]):
        still_out[:, pl.ds(j * TILE, TILE)] = halo[name]
    still_out[:, pl.ds(4 * TILE, TILE)] = low_face
    trail[:, pl.ds(0, TILE)] = low_face
    trail[:, pl.ds(TILE, TILE)] = halo["h_hi"]

    lane = iota((2 * SLOTS, TILE), 1)
    side_h = other_axis(halo["h_hi"])
    side_z = other_axis(halo["z_hi"])
    side_n = other_axis(halo["n_hi"])
    side_wall = other_axis(halo["hi"]) <= 0.0
    side_in = other_axis(low_face)

    def cell(x, k):
        at = k if k < DEPTH else TILE - STRIPS + k
        return jnp.broadcast_to(x[:, at : at + 1], x.shape)

    def ahead(x, k, side):
        return jnp.where(lane == TILE - 1, cell(side, k), pltpu.roll(x, TILE - 1, 1))

    reach = DEPTH - 1 - turn
    low_keep = list(range(reach))
    high_keep = list(range(STRIPS - reach, STRIPS))
    face = {-1: low_face, last: high_face}
    for k in low_keep + [x - 1 for x in high_keep]:
        face[k] = flux(get(dyn, 1, k), h[k], h[k + 1], z[k + 1] - z[k], RUB * (n[k] + n[k + 1]))
    new = {}
    for k in low_keep + high_keep:
        side = flux(
            get(dyn, 2, k), h[k], ahead(h[k], k, side_h), ahead(z[k], k, side_z) - z[k],
            RUB * (n[k] + ahead(n[k], k, side_n)),
        )
        side = jnp.where((lane == TILE - 1) & side_wall, 0.0, side)
        before = jnp.where(lane == 0, cell(side_in, k), pltpu.roll(side, 1, 1))
        new[k] = h[k] + GAIN * ((face[k - 1] - face[k]) + (before - side))
        dyn_out[:, pl.ds(2 * FIELD + k * TILE, TILE)] = side
    blank = jnp.zeros((2 * SLOTS, TILE), f32)
    for k in range(STRIPS):
        dyn_out[:, pl.ds(k * TILE, TILE)] = new[k] if k in new else blank
        dyn_out[:, pl.ds(FIELD + k * TILE, TILE)] = face[k] if k in face else blank
        if k not in new:
            dyn_out[:, pl.ds(2 * FIELD + k * TILE, TILE)] = blank
    for axis in range(2):
        home = slice(axis * SLOTS, (axis + 1) * SLOTS)
        up = route(picks[axis][1], new[last][home])
        down = route(picks[axis][0], new[0][home])
        if axis == 0:
            x_0[...], x_1[...] = swap(is_odd(base), up, down)
        else:
            y_up[pl.ds(STATE, MOVERS), :] = up
            y_down[pl.ds(STATE, MOVERS), :] = down
    finish_chunk(ride, y_up, y_down, sem.at[0])
    if final:
        finish_chunk(LATE, late_up, late_down, sem.at[1])


def run_tiles(
    queue, origin, count, moves_sources, tiles, nb_s, edges, columns, outs, before_loop,
    inbox, outbox, water, stream_x, stream_y, slope_x, slope_y, rub_x, rub_y, in_sem, out_sem,
):
    depth, discharge, bed, friction = tiles
    depth_out, flow_out = outs

    def fetch(j):
        t = queue[j]
        buf = j % BUFFERS
        sem = in_sem.at[buf]
        box = inbox.at[buf]
        kind = origin[t]

        if depth is not None:

            @pl.when(kind == 0)
            def _():
                one = pl.ds(pl.multiple_of(t * TILE, TILE), TILE)
                two = pl.ds(pl.multiple_of(t * (2 * TILE), TILE), 2 * TILE)
                pltpu.make_async_copy(depth.at[one], box.at[pl.ds(0, TILE)], sem).start()
                pltpu.make_async_copy(discharge.at[two], box.at[pl.ds(TILE, 2 * TILE)], sem).start()
                pltpu.make_async_copy(bed.at[one], box.at[pl.ds(3 * TILE, TILE)], sem).start()
                pltpu.make_async_copy(friction.at[one], box.at[pl.ds(4 * TILE, TILE)], sem).start()

        for code, ref, at in moves_sources:

            @pl.when(kind == code)
            def _():
                pltpu.make_async_copy(ref.at[pl.ds(at, STATE)], box, sem).start()

    def arrived(buf):
        box = inbox.at[buf]
        pltpu.make_async_copy(box, box, in_sem.at[buf]).wait()

    def send(t, buf):
        box = outbox.at[buf]
        one = pl.ds(pl.multiple_of(t * TILE, TILE), TILE)
        two = pl.ds(pl.multiple_of(t * (2 * TILE), TILE), 2 * TILE)
        pltpu.make_async_copy(box.at[pl.ds(0, TILE)], depth_out.at[one], out_sem.at[buf]).start()
        pltpu.make_async_copy(box.at[pl.ds(TILE, 2 * TILE)], flow_out.at[two], out_sem.at[buf]).start()

    def sent(buf):
        box = outbox.at[buf]
        pltpu.make_async_copy(box, box, out_sem.at[buf]).wait()

    def prime():
        for j in range(BUFFERS - 1):

            @pl.when(j < count)
            def _():
                fetch(j)

    prime()
    before_loop()
    part_rows = 32
    parts = TILE // part_rows
    lane = iota((part_rows, TILE), 1)
    row = iota((part_rows, TILE), 0)
    at_first = lane == 0
    at_last = lane == TILE - 1
    bottom = row == part_rows - 1

    def one_tile(j, carry):
        t = queue[j]
        buf = j % BUFFERS

        @pl.when(j + BUFFERS - 1 < count)
        def _():
            fetch(j + BUFFERS - 1)

        arrived(buf)

        @pl.when(j >= BUFFERS)
        def _():
            sent(buf)

        box = inbox.at[buf]
        out = outbox.at[buf]
        wall_x = nb_s[1, t] < 0
        wall_y = nb_s[3, t] < 0

        def edge_row(j):
            return edges[j, pl.ds(t, 1), :]

        z_next = edge_row(8)
        n_next = edge_row(9)
        for p in range(parts):
            rows = pl.ds(p * part_rows, part_rows)
            zr = pl.ds(3 * TILE + p * part_rows, part_rows)
            nr = pl.ds(4 * TILE + p * part_rows, part_rows)
            z = box[zr, :]
            n = box[nr, :]
            if p < parts - 1:
                z_dn = box[pl.ds(3 * TILE + p * part_rows + 1, part_rows), :]
                n_dn = box[pl.ds(4 * TILE + p * part_rows + 1, part_rows), :]
            else:
                z_dn = jnp.where(bottom, z_next, pltpu.roll(z, part_rows - 1, 0))
                n_dn = jnp.where(bottom, n_next, pltpu.roll(n, part_rows - 1, 0))
            side = columns[2, rows, :]
            z_rt = jnp.where(at_last, pltpu.roll(side, TILE - 1 - t, 1), pltpu.roll(z, TILE - 1, 1))
            n_rt = jnp.where(at_last, pltpu.roll(side, TILE - 1 - SLOTS - t, 1), pltpu.roll(n, TILE - 1, 1))
            slope_x[rows, :] = z_dn - z
            slope_y[rows, :] = z_rt - z
            rub_x[rows, :] = RUB * (n + n_dn)
            rub_y[rows, :] = RUB * (n + n_rt)
            water[pl.ds(p * part_rows, part_rows), :] = box[rows, :]
        for s in range(4):
            water[pl.ds(TILE, 1), :] = edge_row(4 + s)
            stream_x[pl.ds(7, 1), :] = edge_row(s)
            for p in range(parts):
                rows = pl.ds(p * part_rows, part_rows)
                h = water[rows, :]
                h_dn = water[pl.ds(p * part_rows + 1, part_rows), :]
                side = pltpu.roll(columns[s // 2, rows, :], TILE - 1 - 64 * (s % 2) - 2 * t, 1)
                h_rt = jnp.where(at_last, side, pltpu.roll(h, TILE - 1, 1))
                if s == 0:
                    flow_x = box[pl.ds(TILE + p * part_rows, part_rows), :]
                    flow_y = box[pl.ds(2 * TILE + p * part_rows, part_rows), :]
                else:
                    flow_x = stream_x[pl.ds(8 + p * part_rows, part_rows), :]
                    flow_y = stream_y[rows, :]
                new_x = flux(flow_x, h, h_dn, slope_x[rows, :], rub_x[rows, :])
                if p == parts - 1:
                    new_x = jnp.where(bottom & wall_x, 0.0, new_x)
                new_y = flux(flow_y, h, h_rt, slope_y[rows, :], rub_y[rows, :])
                new_y = jnp.where(at_last & wall_y, 0.0, new_y)
                if s < 3:
                    stream_y[rows, :] = new_y
                else:
                    out[pl.ds(TILE + p * part_rows, part_rows), :] = new_x
                    out[pl.ds(2 * TILE + p * part_rows, part_rows), :] = new_y
                in_y = jnp.where(at_first, side, pltpu.roll(new_y, 1, 1))
                stream_x[pl.ds(8 + p * part_rows, part_rows), :] = new_x
                in_x = stream_x[pl.ds(7 + p * part_rows, part_rows), :]
                h_new = h + GAIN * ((in_x - new_x) + (in_y - new_y))
                if s < 3:
                    water[rows, :] = h_new
                else:
                    out[rows, :] = h_new
        send(t, buf)
        return carry

    lax.fori_loop(0, count, one_tile, 0)
    for b in range(BUFFERS):

        @pl.when(b < count)
        def _():
            sent(b)


def chunk_sources(entries, low, high):
    found = []
    for way, ref in ((0, low), (1, high)):
        for i, m in enumerate(entries):
            found.append((1 + way * MOVERS + m, ref, i * STATE))
    return found


def note_arrivals(entries, moves, base, visit):
    for m in entries:
        for way in range(2):
            lander = moves[way, 1, m]

            @pl.when(lander >= 0)
            def _():
                visit(lander - base[0], 1 + way * MOVERS + m)


def tile_kernel(
    moves, base, ids, nb_s, nb, dyn, fixed, still, x_0, x_1, l3, u3, t0, t1, t2,
    l0, l1, l2, u0, u1, u2, early_low, early_high, depth, discharge, bed, friction,
    depth_out, flow_out, edges, columns,
    zeros, turned, queue, origin, zero_sem, *scratch,
):
    def clear(t, total):
        origin[t] = 0
        return total + jnp.where(ids[t] >= 0, 1, 0)

    live = lax.fori_loop(0, SLOTS, clear, 0)

    def mark(t, code):
        origin[t] = code

    note_arrivals(EARLY + RIDERS, moves, base, mark)
    note_arrivals(LATE, moves, base, lambda t, code: mark(t, -1))

    def enqueue(t, size):
        keep = origin[t] >= 0
        queue[size] = t
        return size + jnp.where(keep, 1, 0)

    count = lax.fori_loop(0, live, enqueue, 0)
    zeros[...] = jnp.zeros(zeros.shape, f32)

    def blank(t, carry):
        one = pl.ds(pl.multiple_of(t * TILE, TILE), TILE)
        two = pl.ds(pl.multiple_of(t * (2 * TILE), TILE), 2 * TILE)
        pltpu.make_async_copy(zeros.at[pl.ds(0, TILE)], depth_out.at[one], zero_sem).start()
        pltpu.make_async_copy(zeros.at[pl.ds(TILE, 2 * TILE)], flow_out.at[two], zero_sem).start()
        return carry

    def before_loop():
        lax.fori_loop(live, SLOTS, blank, 0)
        halo, _ = gather_halos(nb, base, dyn, fixed, ((x_0, x_1), (l3, u3)), False)

        def kept(j):
            return still[:, pl.ds(j * TILE, TILE)]

        n_first = fixed[:, pl.ds(FIELD, TILE)]
        z_first = fixed[:, pl.ds(0, TILE)]
        low_face = flux(
            kept(4), halo["h_lo"], dyn[:, pl.ds(0, TILE)], z_first - kept(0), RUB * (kept(1) + n_first)
        )
        low_face = jnp.where(halo["lo"] > 0.0, low_face, 0.0)
        trails = [(t[:, pl.ds(0, TILE)], t[:, pl.ds(TILE, TILE)]) for t in (t0, t1, t2)]
        trails.append((low_face, halo["h_hi"]))
        for s, (inflow, ahead_h) in enumerate(trails):
            edges[s] = inflow[:SLOTS]
            edges[4 + s] = ahead_h[:SLOTS]
            turned[pl.ds(64 * (s % 2), SLOTS, stride=2), :] = ahead_h[SLOTS:]
            turned[pl.ds(64 * (s % 2) + 1, SLOTS, stride=2), :] = inflow[SLOTS:]
            if s % 2:
                columns[s // 2] = turned[...].T
        edges[8] = kept(2)[:SLOTS]
        edges[9] = kept(3)[:SLOTS]
        turned[pl.ds(0, SLOTS), :] = kept(2)[SLOTS:]
        turned[pl.ds(SLOTS, SLOTS), :] = kept(3)[SLOTS:]
        columns[2] = turned[...].T

    sources = chunk_sources(EARLY, early_low, early_high)
    for m, low, high in zip(RIDERS, (l0, l1, l2, l3), (u0, u1, u2, u3)):
        sources += chunk_sources((m,), low, high)
    run_tiles(
        queue, origin, count, sources, (depth, discharge, bed, friction), nb_s, edges, columns,
        (depth_out, flow_out), before_loop, *scratch,
    )

    def blanked(t, carry):
        pltpu.make_async_copy(zeros, zeros, zero_sem).wait()
        return carry

    lax.fori_loop(live, SLOTS, blanked, 0)


def late_kernel(
    moves, base, nb_s, edges, columns, late_low, late_high, depth_in, flow_in,
    depth_out, flow_out, queue, origin, size, *scratch,
):
    size[0] = 0

    def enqueue(t, code):
        queue[size[0]] = t
        origin[t] = code
        size[0] = size[0] + 1

    note_arrivals(LATE, moves, base, enqueue)
    run_tiles(
        queue, origin, size[0], chunk_sources(LATE, late_low, late_high), (None,) * 4, nb_s, edges, columns,
        (depth_out, flow_out), lambda: None, *scratch,
    )


SMEM = pl.BlockSpec(memory_space=pltpu.SMEM)
VMEM = pl.BlockSpec(memory_space=pltpu.VMEM)
HBM = pl.BlockSpec(memory_space=pltpu.HBM)


def ride_up(block, axis, distance):
    devices = range(lax.axis_size(axis))
    route_pairs = [(i - distance, i) for i in devices if i - distance in devices]
    return lax.ppermute(block, axis, route_pairs)


def trade(block, pairing):
    size = lax.axis_size("gx")
    pairs = []
    for i in range(size):
        other = i ^ 1 if pairing == 0 else ((i + 1) ^ 1) - 1
        if 0 <= other < size:
            pairs.append((i, other))
    return lax.ppermute(block, "gx", pairs)


def both_ways(up, down):
    low = ride_up(up, "gy", 1)
    high = ride_up(down, "gy", -1)
    return low, high


def exchange(x_0, x_1, y_up, y_down):
    got_y = both_ways(y_up, y_down)
    return trade(x_0, 0), trade(x_1, 1), got_y[0], got_y[1]


def held(*shape):
    return pltpu.VMEM(shape, f32)


def on_core(*arrays):
    return [pltpu.with_memory_space_constraint(a, pltpu.VMEM) for a in arrays]


def call(kernel, **settings):
    return pl.pallas_call(kernel, **settings)


def struct(*shape):
    return jax.ShapeDtypeStruct(shape, f32)


def loop_scratch():
    return [
        pltpu.VMEM((BUFFERS, STATE, TILE), f32),
        pltpu.VMEM((BUFFERS, 3 * TILE, TILE), f32),
        pltpu.VMEM((TILE + 8, TILE), f32),
        pltpu.VMEM((TILE + 8, TILE), f32),
        pltpu.VMEM((TILE, TILE), f32),
        pltpu.VMEM((TILE, TILE), f32),
        pltpu.VMEM((TILE, TILE), f32),
        pltpu.VMEM((TILE, TILE), f32),
        pltpu.VMEM((TILE, TILE), f32),
        pltpu.SemaphoreType.DMA((BUFFERS,)),
        pltpu.SemaphoreType.DMA((BUFFERS,)),
    ]


def shards(depth, discharge, bed, friction, tile_ids, neighbors, moves):
    base = (lax.axis_index(("gx", "gy")) * SLOTS).astype(i32).reshape(1)
    plan = moves[0].transpose(0, 2, 1)
    nb = neighbors.T
    tiles = [
        pltpu.with_memory_space_constraint(a, pltpu.HBM)
        for a in (
            depth.reshape(SLOTS * TILE, TILE),
            discharge.reshape(SLOTS * 2 * TILE, TILE),
            bed.reshape(SLOTS * TILE, TILE),
            friction.reshape(SLOTS * TILE, TILE),
        )
    ]
    early_rows = len(EARLY) * STATE
    frames, up, down, early_up, early_down = pl.pallas_call(
        extract_kernel,
        in_specs=[SMEM, SMEM] + [HBM] * 4,
        out_specs=[VMEM] * 5,
        out_shape=[
            held(2 * SLOTS, 5 * FIELD),
            held(MOVERS, 10 * FIELD),
            held(MOVERS, 10 * FIELD),
            held(early_rows, TILE),
            held(early_rows, TILE),
        ],
        scratch_shapes=[
            pltpu.VMEM((SLOTS * TILE, TILE), f32),
            pltpu.VMEM((SLOTS * 2 * TILE, TILE), f32),
            pltpu.VMEM((SLOTS * TILE, TILE), f32),
            pltpu.VMEM((SLOTS * TILE, TILE), f32),
            pltpu.VMEM((5, TILE, TILE), f32),
            pltpu.VMEM((5, TILE, TILE), f32),
            pltpu.VMEM((TILE, TILE), f32),
            pltpu.SemaphoreType.DMA((SLOTS // GROUP, 4)),
            pltpu.SemaphoreType.DMA((2,)),
        ],
        compiler_params=pltpu.CompilerParams(vmem_limit_bytes=20 * 2**20),
        name="extract",
    )(plan, base, *tiles)
    from_low, from_high = both_ways(up, down)
    early_low, early_high = both_ways(early_up, early_down)

    first_rows = 4 * MOVERS
    dyn, fixed, *sends = call(
        settle_kernel,
        in_specs=[SMEM, SMEM] + [VMEM] * 4 + [HBM] * 4,
        out_specs=[VMEM] * 6,
        out_shape=[
            held(2 * SLOTS, 3 * FIELD),
            held(2 * SLOTS, 2 * FIELD),
            held(first_rows, TILE),
            held(first_rows, TILE),
            held(STATE + first_rows, TILE),
            held(STATE + first_rows, TILE),
        ],
        scratch_shapes=[pltpu.SemaphoreType.DMA((2,))],
        compiler_params=pltpu.CompilerParams(vmem_limit_bytes=12 * 2**20),
    )(plan, base, *on_core(nb, frames, from_low, from_high), *tiles)
    got = exchange(*sends)
    lows = [got[2]]
    highs = [got[3]]
    still = []
    trails = []
    late = []
    for turn in range(3):

        def body(*refs, turn=turn):
            step_kernel(turn, *refs)

        shapes = [
            (2 * SLOTS, 3 * FIELD),
            (2 * SLOTS, 5 * TILE),
            (2 * SLOTS, 2 * TILE),
            (MOVERS, TILE),
            (MOVERS, TILE),
            (STATE + MOVERS, TILE),
            (STATE + MOVERS, TILE),
        ]
        if turn == 2:
            shapes += [(len(LATE) * STATE, TILE)] * 2
        dyn, kept, trail, *sends = call(
            body,
            in_specs=[SMEM, SMEM] + [VMEM] * (7 + len(still)) + [HBM] * 4,
            out_specs=[VMEM] * len(shapes),
            out_shape=[held(*s) for s in shapes],
            scratch_shapes=[pltpu.SemaphoreType.DMA((2, 2))],
            compiler_params=pltpu.CompilerParams(vmem_limit_bytes=12 * 2**20),
        )(plan, base, *on_core(nb, dyn, fixed, *still, *got), *tiles)
        still = [kept]
        trails.append(trail)
        late = sends[4:]
        got = exchange(*sends[:4])
        lows.append(got[2])
        highs.append(got[3])

    late_low, late_high = both_ways(*late)
    kept_inputs = on_core(
        nb, dyn, fixed, *still, *got, *trails, *lows[:3], *highs[:3], early_low, early_high
    )
    new_depth, new_flow, edges, columns = call(
        tile_kernel,
        in_specs=[SMEM] * 4 + [VMEM] * len(kept_inputs) + [HBM] * 4,
        out_specs=[HBM, HBM, VMEM, VMEM],
        out_shape=[
            struct(SLOTS * TILE, TILE),
            struct(SLOTS * 2 * TILE, TILE),
            held(10, SLOTS, TILE),
            held(3, TILE, TILE),
        ],
        scratch_shapes=[
            pltpu.VMEM((3 * TILE, TILE), f32),
            pltpu.VMEM((TILE, TILE), f32),
            pltpu.SMEM((SLOTS,), i32),
            pltpu.SMEM((SLOTS,), i32),
            pltpu.SemaphoreType.DMA,
            *loop_scratch(),
        ],
        compiler_params=pltpu.CompilerParams(vmem_limit_bytes=12 * 2**20),
    )(plan, base, tile_ids, nb, *kept_inputs, *tiles)
    new_depth, new_flow = pl.pallas_call(
        late_kernel,
        in_specs=[SMEM] * 3 + [VMEM] * 4 + [HBM] * 2,
        out_specs=[HBM, HBM],
        out_shape=[struct(SLOTS * TILE, TILE), struct(SLOTS * 2 * TILE, TILE)],
        input_output_aliases={7: 0, 8: 1},
        scratch_shapes=[
            pltpu.SMEM((SLOTS,), i32),
            pltpu.SMEM((SLOTS,), i32),
            pltpu.SMEM((1,), i32),
            *loop_scratch(),
        ],
        compiler_params=pltpu.CompilerParams(vmem_limit_bytes=12 * 2**20),
        name="late_tiles",
    )(plan, base, nb, *on_core(edges, columns, late_low, late_high), new_depth, new_flow)
    return (
        new_depth.reshape(SLOTS, TILE, TILE),
        new_flow.reshape(SLOTS, 2, TILE, TILE),
    )


def solution(mesh):
    return jax.shard_map(
        shards,
        mesh=mesh,
        in_specs=(
            P(("gx", "gy"), None, None),
            P(("gx", "gy"), None, None, None),
            P(("gx", "gy"), None, None),
            P(("gx", "gy"), None, None),
            P(("gx", "gy")),
            P(("gx", "gy"), None),
            P(("gx", "gy"), None, None, None),
        ),
        out_specs=(P(("gx", "gy"), None, None), P(("gx", "gy"), None, None, None)),
        check_vma=False,
    )
```

```python
import jax
import jax.numpy as jnp
from jax import lax
from jax.experimental import pallas as pl
from jax.experimental.pallas import tpu as pltpu
from jax.sharding import PartitionSpec as P


TILE = 128
SLOTS = 32
MOVERS = 8
DEPTH = 4
STRIPS = 2 * DEPTH
FIELD = STRIPS * TILE
STATE = 5 * TILE
EARLY = (0, 1)
RIDERS = (2, 3, 4, 5)
LATE = (6, 7)
GROUP = 8
GY = 16
BUFFERS = 4

gravity = 9.81
step_time = 0.25
spacing = 2.0
min_depth = 0.15
PULL = gravity * step_time / spacing
RUB = gravity * step_time * 0.5
GAIN = step_time / spacing
UNIT_H = 2.0 / (GAIN * PULL)
UNIT_Q = UNIT_H / GAIN
FLOOR = 2.0 * min_depth / UNIT_H
DRAG = RUB * UNIT_Q * (0.5 * UNIT_H) ** (-7.0 / 3.0)

f32 = jnp.float32
bf16 = jnp.bfloat16
i32 = jnp.int32


def flux(flow, h_lo, h_hi, slope, rub):
    depth_face = jnp.maximum(0.5 * (h_lo + h_hi), min_depth)
    drive = flow - (PULL * depth_face) * ((h_hi - h_lo) + slope)
    loss = jnp.exp2(jnp.log2(depth_face) * (-7.0 / 3.0))
    return drive / (1.0 + (rub * jnp.abs(flow)) * loss)


def unit_flux(flow, h_lo, h_hi, slope, rub):
    depth_sum = jnp.maximum(h_lo + h_hi, FLOOR)
    drive = flow - depth_sum * ((h_hi - h_lo) + slope)
    loss = jnp.exp2(jnp.log2(depth_sum) * (-7.0 / 3.0))
    return drive / (1.0 + (rub * jnp.abs(flow)) * loss)


def iota(shape, dim):
    return lax.broadcasted_iota(i32, shape, dim)


def route(onehot, rows):
    a = rows.astype(bf16)
    rest = rows - a.astype(f32)
    b = rest.astype(bf16)
    c = (rest - b.astype(f32)).astype(bf16)
    take = onehot.astype(bf16)

    def part(x):
        return jnp.dot(take, x, preferred_element_type=f32)

    return part(a) + part(b) + part(c)


def side_links(nb_ref, base, side):
    square = (SLOTS, SLOTS)
    rows = iota(square, 0)
    cols = iota(square, 1)
    link_row = jnp.broadcast_to(nb_ref[side : side + 1, :].astype(f32), square)
    diagonal = rows == cols

    def column(x):
        return jnp.broadcast_to(jnp.sum(jnp.where(diagonal, x, 0.0), 1, keepdims=True), square)

    first = base.astype(f32)

    def remote(link):
        return jnp.where((link >= 0.0) & ((link < first) | (link >= first + SLOTS)), 1.0, 0.0)

    link_b = column(link_row)
    missing = link_b[:, :1] < 0.0
    far_b = remote(link_b)
    far = far_b[:, :1]
    far_row = remote(link_row)
    near = jnp.where(link_b - first == cols.astype(f32), 1.0, 0.0)
    rank = jnp.sum(jnp.where(link_row < link_b, far_row, 0.0), 1, keepdims=True)
    order_row = jnp.sum(jnp.where(rows < cols, far_b, 0.0), 0, keepdims=True)
    far_row = far_row[:1]
    place = jnp.where(
        (jnp.broadcast_to(rank, (SLOTS, MOVERS)) == iota((SLOTS, MOVERS), 1).astype(f32))
        & (jnp.broadcast_to(far, (SLOTS, MOVERS)) > 0.0),
        1.0,
        0.0,
    )
    pick = jnp.where(
        (jnp.broadcast_to(order_row, (MOVERS, SLOTS)) == iota((MOVERS, SLOTS), 0).astype(f32))
        & (jnp.broadcast_to(far_row, (MOVERS, SLOTS)) > 0.0),
        1.0,
        0.0,
    )
    exists = jnp.where(missing, 0.0, 1.0)
    return near, place, pick, exists


def halo_of(links, rows, message):
    near, place, _, _ = links
    return route(near, rows) + route(place, message)


def extract_kernel(
    moves, base, depth, discharge, bed, friction, frames, out_0, out_1, early_0, early_1,
    depth_v, flow_v, bed_v, rough_v, lo_acc, hi_acc, turned, load_sem, sem,
):
    lane = iota((TILE, TILE), 1)
    groups = SLOTS // GROUP
    loads = []
    for g in range(groups):
        one = pl.ds(g * GROUP * TILE, GROUP * TILE)
        two = pl.ds(g * GROUP * 2 * TILE, GROUP * 2 * TILE)
        pairs = ((depth, depth_v, one), (discharge, flow_v, two), (bed, bed_v, one), (friction, rough_v, one))
        copies = [pltpu.make_async_copy(a.at[r], b.at[r], load_sem.at[g, i]) for i, (a, b, r) in enumerate(pairs)]
        for c in copies:
            c.start()
        loads.append(copies)
    start_chunk(EARLY, moves, base, (depth, discharge, bed, friction), early_0, early_1, sem)

    def strip(f, k):
        return pl.ds((f * STRIPS + k) * TILE, TILE)

    sources = ((depth_v, 0, 1), (flow_v, 0, 2), (flow_v, 1, 2), (bed_v, 0, 1), (rough_v, 0, 1))
    for g in range(groups):
        for c in loads[g]:
            c.wait()
        home = pl.ds(g * GROUP, GROUP)
        for f, (ref, part, parts) in enumerate(sources):
            top = (g * GROUP * parts + part) * TILE
            for k in range(STRIPS):
                row = k if k < DEPTH else TILE - STRIPS + k
                frames[home, strip(f, k)] = ref[pl.ds(top + row, GROUP, stride=parts * TILE), :]
            high = hi_acc[f] if g else None
            low = lo_acc[f] if g else None
            for t in range(GROUP):
                tile = ref[pl.ds(top + t * parts * TILE, TILE), :]
                at = g * GROUP * DEPTH + DEPTH * t
                turn = pltpu.roll(tile, (at + DEPTH) % TILE, 1)
                high = turn if high is None else jnp.where(lane >= at, turn, high)
                if low is None:
                    low = turn
                elif at + DEPTH < TILE:
                    low = jnp.where(lane >= at + DEPTH, turn, low)
                else:
                    low = jnp.where(lane < DEPTH, turn, low)
            hi_acc[f] = high
            lo_acc[f] = low

    for f in range(5):
        to = (0, 2, 1, 3, 4)[f]
        for half in range(2):
            block = hi_acc[f] if half else pltpu.roll(lo_acc[f], TILE - DEPTH, 1)
            turned[...] = block.T
            for k in range(DEPTH):
                frames[pl.ds(SLOTS, SLOTS), strip(to, half * DEPTH + k)] = turned[pl.ds(k, SLOTS, stride=DEPTH), :]
    shape = (2 * MOVERS, SLOTS)
    pick = jnp.zeros(shape, f32)
    for m in range(MOVERS):
        for pairing in range(2):
            leaver = moves[way_of(base, pairing), 0, m] - base[0]
            spot = (iota(shape, 0) == pairing * MOVERS + m) & (iota(shape, 1) == leaver)
            pick = jnp.where(spot, 1.0, pick)
    for axis in range(2):
        for c in range(5):
            got = route(pick, frames[pl.ds(axis * SLOTS, SLOTS), pl.ds(c * FIELD, FIELD)])
            to = pl.ds((axis * 5 + c) * FIELD, FIELD)
            out_0[:, to] = got[:MOVERS]
            out_1[:, to] = got[MOVERS:]
    finish_chunk(EARLY, early_0, early_1, sem)


def start_chunk(entries, moves, base, tiles, out_0, out_1, sem):
    depth, discharge, bed, friction = tiles
    for pairing, out in enumerate((out_0, out_1)):
        way = way_of(base, pairing)
        for i, m in enumerate(entries):
            slot = jnp.clip(moves[way, 0, m] - base[0], 0, SLOTS - 1)
            at = i * STATE
            one = pl.ds(pl.multiple_of(slot * TILE, TILE), TILE)
            two = pl.ds(pl.multiple_of(slot * (2 * TILE), TILE), 2 * TILE)
            pltpu.make_async_copy(depth.at[one], out.at[pl.ds(at, TILE)], sem.at[pairing]).start()
            pltpu.make_async_copy(discharge.at[two], out.at[pl.ds(at + TILE, 2 * TILE)], sem.at[pairing]).start()
            pltpu.make_async_copy(bed.at[one], out.at[pl.ds(at + 3 * TILE, TILE)], sem.at[pairing]).start()
            pltpu.make_async_copy(friction.at[one], out.at[pl.ds(at + 4 * TILE, TILE)], sem.at[pairing]).start()


def finish_chunk(entries, out_0, out_1, sem):
    body = pl.ds(0, len(entries) * STATE)
    for pairing, out in enumerate((out_0, out_1)):
        pltpu.make_async_copy(out.at[body], out.at[body], sem.at[pairing]).wait()


def is_odd(base, axis):
    return ((base[0] // (SLOTS * (GY if axis == 0 else 1))) % 2) == 1


def way_of(base, pairing):
    odd = (base[0] // SLOTS) % 2
    return odd if pairing else 1 - odd


def swap(odd, a, b):
    return jnp.where(odd, b, a), jnp.where(odd, a, b)


def settle_kernel(
    moves, base, nb, frames, from_0, from_1, depth, discharge, bed, friction,
    dyn, fixed, x_0, x_1, y_0, y_1, sem,
):
    ride = RIDERS[:1]
    start_chunk(ride, moves, base, (depth, discharge, bed, friction), y_0, y_1, sem)
    shape = (SLOTS, 2 * MOVERS)
    land = jnp.zeros(shape, f32)
    left = jnp.zeros((SLOTS, TILE), f32)
    for m in range(MOVERS):
        for pairing in range(2):
            way = way_of(base, pairing)
            lander = moves[way, 1, m] - base[0]
            leaver = moves[way, 0, m] - base[0]
            spot = (iota(shape, 0) == lander) & (iota(shape, 1) == pairing * MOVERS + m)
            land = jnp.where(spot, 1.0, land)
            row = iota((SLOTS, TILE), 0)
            left = jnp.where((row == leaver) | (row == lander), 1.0, left)
    for axis in range(2):
        home = pl.ds(axis * SLOTS, SLOTS)
        for f in range(5):
            part = pl.ds(f * FIELD, FIELD)
            came = pl.ds((axis * 5 + f) * FIELD, FIELD)
            fresh = route(land, jnp.concatenate([from_0[:, came], from_1[:, came]], 0))
            for k in range(STRIPS):
                sub = pl.ds(f * FIELD + k * TILE, TILE)
                value = jnp.where(left > 0.0, 0.0, frames[home, sub]) + fresh[:, k * TILE : (k + 1) * TILE]
                if f < 3:
                    dyn[home, sub] = value
                else:
                    fixed[home, pl.ds((f - 3) * FIELD + k * TILE, TILE)] = value

    def edge(ref, axis, f, k):
        return ref[pl.ds(axis * SLOTS, SLOTS), pl.ds(f * FIELD + k * TILE, TILE)]

    last = STRIPS - 1
    blank = jnp.zeros((MOVERS, TILE), f32)
    for axis in range(2):
        lower = side_links(nb, base[0], 2 * axis)
        higher = side_links(nb, base[0], 2 * axis + 1)
        ups = (edge(dyn, axis, 0, last), edge(fixed, axis, 0, last), edge(fixed, axis, 1, last), edge(dyn, axis, 1, last))
        downs = (edge(dyn, axis, 0, 0), edge(fixed, axis, 0, 0), edge(fixed, axis, 1, 0))
        for f in range(4):
            up = route(higher[2], ups[f])
            down = route(lower[2], downs[f]) if f < 3 else blank
            up, down = swap(is_odd(base, axis), up, down)
            if axis == 0:
                x_0[pl.ds(f * MOVERS, MOVERS), :] = up
                x_1[pl.ds(f * MOVERS, MOVERS), :] = down
            else:
                y_0[pl.ds(STATE + f * MOVERS, MOVERS), :] = up
                y_1[pl.ds(STATE + f * MOVERS, MOVERS), :] = down
    finish_chunk(ride, y_0, y_1, sem)


def other_axis(x):
    return jnp.concatenate([x[SLOTS:], x[:SLOTS]], 0)


def gather_halos(nb, base_ref, dyn, fixed, messages, first):
    last = STRIPS - 1
    out = {}
    parts = {name: [] for name in ("h_lo", "h_hi", "z_lo", "n_lo", "q_lo", "z_hi", "n_hi", "lo", "hi")}
    picks = []
    for axis in range(2):
        home = pl.ds(axis * SLOTS, SLOTS)
        lower = side_links(nb, base_ref[0], 2 * axis)
        higher = side_links(nb, base_ref[0], 2 * axis + 1)
        picks.append((lower[2], higher[2]))

        def message(f):
            rows = pl.ds(axis * STATE + f * MOVERS, MOVERS)
            pair = messages[axis]
            from_higher, from_lower = swap(is_odd(base_ref, axis), pair[0][rows, :], pair[1][rows, :])
            return from_lower, from_higher

        def strip(ref, f, k):
            return ref[home, pl.ds(f * FIELD + k * TILE, TILE)]

        def low(f, rows):
            return halo_of(lower, rows, message(f)[0])

        def high(f, rows):
            return halo_of(higher, rows, message(f)[1])

        parts["h_lo"].append(low(0, strip(dyn, 0, last)))
        parts["h_hi"].append(high(0, strip(dyn, 0, 0)))
        if first:
            parts["z_lo"].append(low(1, strip(fixed, 0, last)))
            parts["n_lo"].append(low(2, strip(fixed, 1, last)))
            parts["q_lo"].append(low(3, strip(dyn, 1, last)))
            parts["z_hi"].append(high(1, strip(fixed, 0, 0)))
            parts["n_hi"].append(high(2, strip(fixed, 1, 0)))
        parts["lo"].append(jnp.broadcast_to(lower[3], (SLOTS, TILE)))
        parts["hi"].append(jnp.broadcast_to(higher[3], (SLOTS, TILE)))
    for name, pieces in parts.items():
        if pieces:
            out[name] = jnp.concatenate(pieces, 0)
    return out, picks


def step_kernel(turn, moves, base, nb, dyn, fixed, *rest):
    first = turn == 0
    if first:
        still = None
        (x0, x1, y0, y1), rest = rest[:4], rest[4:]
    else:
        still = rest[0]
        (x0, x1, y0, y1), rest = rest[1:5], rest[5:]
    depth, discharge, bed, friction = rest[:4]
    tiles = (depth, discharge, bed, friction)
    final = turn == 2
    if final:
        (dyn_out, still_out, trail, x_0, x_1, y_0, y_1, late_0, late_1, sem) = rest[4:]
    else:
        (dyn_out, still_out, trail, x_0, x_1, y_0, y_1, sem) = rest[4:]
    ride = RIDERS[turn + 1 : turn + 2]
    start_chunk(ride, moves, base, tiles, y_0, y_1, sem.at[0])
    if final:
        start_chunk(LATE, moves, base, tiles, late_0, late_1, sem.at[1])
    halo, picks = gather_halos(nb, base, dyn, fixed, ((x0, x1), (y0, y1)), first)
    names = ("z_lo", "n_lo", "z_hi", "n_hi", "q_lo")
    if not first:
        for j, name in enumerate(names):
            halo[name] = still[:, pl.ds(j * TILE, TILE)]

    def get(ref, f, k):
        return ref[:, pl.ds(f * FIELD + k * TILE, TILE)]

    last = STRIPS - 1
    h = [get(dyn, 0, k) for k in range(STRIPS)]
    z = [get(fixed, 0, k) for k in range(STRIPS)]
    n = [get(fixed, 1, k) for k in range(STRIPS)]
    low_face = flux(halo["q_lo"], halo["h_lo"], h[0], z[0] - halo["z_lo"], RUB * (halo["n_lo"] + n[0]))
    low_face = jnp.where(halo["lo"] > 0.0, low_face, 0.0)
    high_face = flux(get(dyn, 1, last), h[last], halo["h_hi"], halo["z_hi"] - z[last], RUB * (n[last] + halo["n_hi"]))
    high_face = jnp.where(halo["hi"] > 0.0, high_face, 0.0)
    for j, name in enumerate(names[:4]):
        still_out[:, pl.ds(j * TILE, TILE)] = halo[name]
    still_out[:, pl.ds(4 * TILE, TILE)] = low_face
    trail[:, pl.ds(0, TILE)] = low_face
    trail[:, pl.ds(TILE, TILE)] = halo["h_hi"]

    lane = iota((2 * SLOTS, TILE), 1)
    side_h = other_axis(halo["h_hi"])
    side_z = other_axis(halo["z_hi"])
    side_n = other_axis(halo["n_hi"])
    side_wall = other_axis(halo["hi"]) <= 0.0
    side_in = other_axis(low_face)

    def cell(x, k):
        at = k if k < DEPTH else TILE - STRIPS + k
        return jnp.broadcast_to(x[:, at : at + 1], x.shape)

    def ahead(x, k, side):
        return jnp.where(lane == TILE - 1, cell(side, k), pltpu.roll(x, TILE - 1, 1))

    reach = DEPTH - 1 - turn
    low_keep = list(range(reach))
    high_keep = list(range(STRIPS - reach, STRIPS))
    face = {-1: low_face, last: high_face}
    for k in low_keep + [x - 1 for x in high_keep]:
        face[k] = flux(get(dyn, 1, k), h[k], h[k + 1], z[k + 1] - z[k], RUB * (n[k] + n[k + 1]))
    new = {}
    for k in low_keep + high_keep:
        side = flux(
            get(dyn, 2, k), h[k], ahead(h[k], k, side_h), ahead(z[k], k, side_z) - z[k],
            RUB * (n[k] + ahead(n[k], k, side_n)),
        )
        side = jnp.where((lane == TILE - 1) & side_wall, 0.0, side)
        before = jnp.where(lane == 0, cell(side_in, k), pltpu.roll(side, 1, 1))
        new[k] = h[k] + GAIN * ((face[k - 1] - face[k]) + (before - side))
        dyn_out[:, pl.ds(2 * FIELD + k * TILE, TILE)] = side
    blank = jnp.zeros((2 * SLOTS, TILE), f32)
    for k in range(STRIPS):
        dyn_out[:, pl.ds(k * TILE, TILE)] = new[k] if k in new else blank
        dyn_out[:, pl.ds(FIELD + k * TILE, TILE)] = face[k] if k in face else blank
        if k not in new:
            dyn_out[:, pl.ds(2 * FIELD + k * TILE, TILE)] = blank
    for axis in range(2):
        home = slice(axis * SLOTS, (axis + 1) * SLOTS)
        up = route(picks[axis][1], new[last][home])
        down = route(picks[axis][0], new[0][home])
        up, down = swap(is_odd(base, axis), up, down)
        if axis == 0:
            x_0[...] = up
            x_1[...] = down
        else:
            y_0[pl.ds(STATE, MOVERS), :] = up
            y_1[pl.ds(STATE, MOVERS), :] = down
    finish_chunk(ride, y_0, y_1, sem.at[0])
    if final:
        finish_chunk(LATE, late_0, late_1, sem.at[1])


def run_tiles(
    queue, origin, count, moves_sources, tiles, nb_s, edges, columns, outs, before_loop,
    inbox, outbox, water, stream_x, stream_y, slope_x, slope_y, rub_x, rub_y, in_sem, out_sem,
):
    depth, discharge, bed, friction = tiles
    depth_out, flow_out = outs

    def fetch(j):
        t = queue[j]
        buf = j % BUFFERS
        sem = in_sem.at[buf]
        box = inbox.at[buf]
        kind = origin[t]

        if depth is not None:

            @pl.when(kind == 0)
            def _():
                one = pl.ds(pl.multiple_of(t * TILE, TILE), TILE)
                two = pl.ds(pl.multiple_of(t * (2 * TILE), TILE), 2 * TILE)
                pltpu.make_async_copy(depth.at[one], box.at[pl.ds(0, TILE)], sem).start()
                pltpu.make_async_copy(discharge.at[two], box.at[pl.ds(TILE, 2 * TILE)], sem).start()
                pltpu.make_async_copy(bed.at[one], box.at[pl.ds(3 * TILE, TILE)], sem).start()
                pltpu.make_async_copy(friction.at[one], box.at[pl.ds(4 * TILE, TILE)], sem).start()

        for code, ref, at in moves_sources:

            @pl.when(kind == code)
            def _():
                pltpu.make_async_copy(ref.at[pl.ds(at, STATE)], box, sem).start()

    def arrived(buf):
        box = inbox.at[buf]
        pltpu.make_async_copy(box, box, in_sem.at[buf]).wait()

    def send(t, buf):
        box = outbox.at[buf]
        one = pl.ds(pl.multiple_of(t * TILE, TILE), TILE)
        two = pl.ds(pl.multiple_of(t * (2 * TILE), TILE), 2 * TILE)
        pltpu.make_async_copy(box.at[pl.ds(0, TILE)], depth_out.at[one], out_sem.at[buf]).start()
        pltpu.make_async_copy(box.at[pl.ds(TILE, 2 * TILE)], flow_out.at[two], out_sem.at[buf]).start()

    def sent(buf):
        box = outbox.at[buf]
        pltpu.make_async_copy(box, box, out_sem.at[buf]).wait()

    def prime():
        for j in range(BUFFERS - 1):

            @pl.when(j < count)
            def _():
                fetch(j)

    prime()
    before_loop()
    part_rows = 16
    parts = TILE // part_rows
    lane = iota((part_rows, TILE), 1)
    row = iota((part_rows, TILE), 0)
    at_first = lane == 0
    at_last = lane == TILE - 1
    bottom = row == part_rows - 1

    def one_tile(j, carry):
        t = queue[j]
        buf = j % BUFFERS

        @pl.when(j + BUFFERS - 1 < count)
        def _():
            fetch(j + BUFFERS - 1)

        arrived(buf)

        @pl.when(j >= BUFFERS)
        def _():
            sent(buf)

        box = inbox.at[buf]
        out = outbox.at[buf]
        wall_x = nb_s[1, t] < 0
        wall_y = nb_s[3, t] < 0

        def edge_row(j):
            return edges[j, pl.ds(t, 1), :]

        z_next = edge_row(8)
        n_next = edge_row(9)
        for p in range(parts):
            rows = pl.ds(p * part_rows, part_rows)
            zr = pl.ds(3 * TILE + p * part_rows, part_rows)
            nr = pl.ds(4 * TILE + p * part_rows, part_rows)
            z = box[zr, :] * (1.0 / UNIT_H)
            n = box[nr, :]
            if p < parts - 1:
                z_dn = box[pl.ds(3 * TILE + p * part_rows + 1, part_rows), :] * (1.0 / UNIT_H)
                n_dn = box[pl.ds(4 * TILE + p * part_rows + 1, part_rows), :]
            else:
                z_dn = jnp.where(bottom, z_next, pltpu.roll(z, part_rows - 1, 0))
                n_dn = jnp.where(bottom, n_next, pltpu.roll(n, part_rows - 1, 0))
            side = columns[2, rows, :]
            z_rt = jnp.where(at_last, pltpu.roll(side, TILE - 1 - t, 1), pltpu.roll(z, TILE - 1, 1))
            n_rt = jnp.where(at_last, pltpu.roll(side, TILE - 1 - SLOTS - t, 1), pltpu.roll(n, TILE - 1, 1))
            slope_x[rows, :] = z_dn - z
            slope_y[rows, :] = z_rt - z
            rub_x[rows, :] = DRAG * (n + n_dn)
            rub_y[rows, :] = DRAG * (n + n_rt)
            water[rows, :] = box[rows, :] * (1.0 / UNIT_H)
        for s in range(4):
            water[pl.ds(TILE, 1), :] = edge_row(4 + s)
            stream_x[pl.ds(7, 1), :] = edge_row(s)
            for p in range(parts):
                rows = pl.ds(p * part_rows, part_rows)
                h = water[rows, :]
                h_dn = water[pl.ds(p * part_rows + 1, part_rows), :]
                side = pltpu.roll(columns[s // 2, rows, :], TILE - 1 - 64 * (s % 2) - 2 * t, 1)
                h_rt = jnp.where(at_last, side, pltpu.roll(h, TILE - 1, 1))
                if s == 0:
                    flow_x = box[pl.ds(TILE + p * part_rows, part_rows), :] * (1.0 / UNIT_Q)
                    flow_y = box[pl.ds(2 * TILE + p * part_rows, part_rows), :] * (1.0 / UNIT_Q)
                else:
                    flow_x = stream_x[pl.ds(8 + p * part_rows, part_rows), :]
                    flow_y = stream_y[rows, :]
                new_x = unit_flux(flow_x, h, h_dn, slope_x[rows, :], rub_x[rows, :])
                if p == parts - 1:
                    new_x = jnp.where(bottom & wall_x, 0.0, new_x)
                new_y = unit_flux(flow_y, h, h_rt, slope_y[rows, :], rub_y[rows, :])
                new_y = jnp.where(at_last & wall_y, 0.0, new_y)
                if s < 3:
                    stream_y[rows, :] = new_y
                else:
                    out[pl.ds(TILE + p * part_rows, part_rows), :] = new_x * UNIT_Q
                    out[pl.ds(2 * TILE + p * part_rows, part_rows), :] = new_y * UNIT_Q
                in_y = jnp.where(at_first, side, pltpu.roll(new_y, 1, 1))
                stream_x[pl.ds(8 + p * part_rows, part_rows), :] = new_x
                in_x = stream_x[pl.ds(7 + p * part_rows, part_rows), :]
                h_new = h + ((in_x - new_x) + (in_y - new_y))
                if s < 3:
                    water[rows, :] = h_new
                else:
                    out[rows, :] = h_new * UNIT_H
        send(t, buf)
        return carry

    lax.fori_loop(0, count, one_tile, 0)
    for b in range(BUFFERS):

        @pl.when(b < count)
        def _():
            sent(b)


def chunk_sources(entries, *chunks):
    found = []
    for pairing, ref in enumerate(chunks):
        for i, m in enumerate(entries):
            found.append((1 + pairing * MOVERS + m, ref, i * STATE))
    return found


def note_arrivals(entries, moves, base, visit):
    for m in entries:
        for pairing in range(2):
            lander = moves[way_of(base, pairing), 1, m]

            @pl.when(lander >= 0)
            def _():
                visit(lander - base[0], 1 + pairing * MOVERS + m)


def tile_kernel(
    moves, base, ids, nb_s, nb, dyn, fixed, still, x_0, x_1, l3, u3, t0, t1, t2,
    l0, l1, l2, u0, u1, u2, early_0, early_1, depth, discharge, bed, friction,
    depth_out, flow_out, edges, columns,
    zeros, turned, queue, origin, zero_sem, *scratch,
):
    def clear(t, total):
        origin[t] = 0
        return total + jnp.where(ids[t] >= 0, 1, 0)

    live = lax.fori_loop(0, SLOTS, clear, 0)

    def mark(t, code):
        origin[t] = code

    note_arrivals(EARLY + RIDERS, moves, base, mark)
    note_arrivals(LATE, moves, base, lambda t, code: mark(t, -1))

    def enqueue(t, size):
        keep = origin[t] >= 0
        queue[size] = t
        return size + jnp.where(keep, 1, 0)

    count = lax.fori_loop(0, live, enqueue, 0)
    zeros[...] = jnp.zeros(zeros.shape, f32)

    def blank(t, carry):
        one = pl.ds(pl.multiple_of(t * TILE, TILE), TILE)
        two = pl.ds(pl.multiple_of(t * (2 * TILE), TILE), 2 * TILE)
        pltpu.make_async_copy(zeros.at[pl.ds(0, TILE)], depth_out.at[one], zero_sem).start()
        pltpu.make_async_copy(zeros.at[pl.ds(TILE, 2 * TILE)], flow_out.at[two], zero_sem).start()
        return carry

    def before_loop():
        lax.fori_loop(live, SLOTS, blank, 0)
        halo, _ = gather_halos(nb, base, dyn, fixed, ((x_0, x_1), (l3, u3)), False)

        def kept(j):
            return still[:, pl.ds(j * TILE, TILE)]

        n_first = fixed[:, pl.ds(FIELD, TILE)]
        z_first = fixed[:, pl.ds(0, TILE)]
        low_face = flux(
            kept(4), halo["h_lo"], dyn[:, pl.ds(0, TILE)], z_first - kept(0), RUB * (kept(1) + n_first)
        )
        low_face = jnp.where(halo["lo"] > 0.0, low_face, 0.0)
        trails = [(t[:, pl.ds(0, TILE)], t[:, pl.ds(TILE, TILE)]) for t in (t0, t1, t2)]
        trails.append((low_face, halo["h_hi"]))
        for s, (inflow, ahead_h) in enumerate(trails):
            inflow = inflow * (1.0 / UNIT_Q)
            ahead_h = ahead_h * (1.0 / UNIT_H)
            edges[s] = inflow[:SLOTS]
            edges[4 + s] = ahead_h[:SLOTS]
            turned[pl.ds(64 * (s % 2), SLOTS, stride=2), :] = ahead_h[SLOTS:]
            turned[pl.ds(64 * (s % 2) + 1, SLOTS, stride=2), :] = inflow[SLOTS:]
            if s % 2:
                columns[s // 2] = turned[...].T
        z_ahead = kept(2) * (1.0 / UNIT_H)
        edges[8] = z_ahead[:SLOTS]
        edges[9] = kept(3)[:SLOTS]
        turned[pl.ds(0, SLOTS), :] = z_ahead[SLOTS:]
        turned[pl.ds(SLOTS, SLOTS), :] = kept(3)[SLOTS:]
        columns[2] = turned[...].T

    sources = chunk_sources(EARLY, early_0, early_1)
    for m, chunk_0, chunk_1 in zip(RIDERS, (l0, l1, l2, l3), (u0, u1, u2, u3)):
        sources += chunk_sources((m,), chunk_0, chunk_1)
    run_tiles(
        queue, origin, count, sources, (depth, discharge, bed, friction), nb_s, edges, columns,
        (depth_out, flow_out), before_loop, *scratch,
    )

    def blanked(t, carry):
        pltpu.make_async_copy(zeros, zeros, zero_sem).wait()
        return carry

    lax.fori_loop(live, SLOTS, blanked, 0)


def late_kernel(
    moves, base, nb_s, edges, columns, late_0, late_1, depth_in, flow_in,
    depth_out, flow_out, queue, origin, size, *scratch,
):
    size[0] = 0

    def enqueue(t, code):
        queue[size[0]] = t
        origin[t] = code
        size[0] = size[0] + 1

    note_arrivals(LATE, moves, base, enqueue)
    run_tiles(
        queue, origin, size[0], chunk_sources(LATE, late_0, late_1), (None,) * 4, nb_s, edges, columns,
        (depth_out, flow_out), lambda: None, *scratch,
    )


SMEM = pl.BlockSpec(memory_space=pltpu.SMEM)
VMEM = pl.BlockSpec(memory_space=pltpu.VMEM)
HBM = pl.BlockSpec(memory_space=pltpu.HBM)


def trade(block, axis, pairing):
    size = lax.axis_size(axis)
    pairs = []
    for i in range(size):
        other = i ^ 1 if pairing == 0 else ((i + 1) ^ 1) - 1
        if 0 <= other < size:
            pairs.append((i, other))
    return lax.ppermute(block, axis, pairs)


def trade_both(block_0, block_1, axis):
    got_1 = trade(block_1, axis, 1)
    got_0 = trade(block_0, axis, 0)
    return got_0, got_1


def exchange(x_0, x_1, y_0, y_1):
    got_y = trade_both(y_0, y_1, "gy")
    got_x = trade_both(x_0, x_1, "gx")
    return *got_x, *got_y


def held(*shape):
    return pltpu.VMEM(shape, f32)


def on_core(*arrays):
    return [pltpu.with_memory_space_constraint(a, pltpu.VMEM) for a in arrays]


def call(kernel, **settings):
    return pl.pallas_call(kernel, **settings)


def struct(*shape):
    return jax.ShapeDtypeStruct(shape, f32)


def loop_scratch():
    return [
        pltpu.VMEM((BUFFERS, STATE, TILE), f32),
        pltpu.VMEM((BUFFERS, 3 * TILE, TILE), f32),
        pltpu.VMEM((TILE + 8, TILE), f32),
        pltpu.VMEM((TILE + 8, TILE), f32),
        pltpu.VMEM((TILE, TILE), f32),
        pltpu.VMEM((TILE, TILE), f32),
        pltpu.VMEM((TILE, TILE), f32),
        pltpu.VMEM((TILE, TILE), f32),
        pltpu.VMEM((TILE, TILE), f32),
        pltpu.SemaphoreType.DMA((BUFFERS,)),
        pltpu.SemaphoreType.DMA((BUFFERS,)),
    ]


def shards(depth, discharge, bed, friction, tile_ids, neighbors, moves):
    base = (lax.axis_index(("gx", "gy")) * SLOTS).astype(i32).reshape(1)
    plan = moves[0].transpose(0, 2, 1)
    nb = neighbors.T
    tiles = [
        pltpu.with_memory_space_constraint(a, pltpu.HBM)
        for a in (
            depth.reshape(SLOTS * TILE, TILE),
            discharge.reshape(SLOTS * 2 * TILE, TILE),
            bed.reshape(SLOTS * TILE, TILE),
            friction.reshape(SLOTS * TILE, TILE),
        )
    ]
    early_rows = len(EARLY) * STATE
    frames, up, down, early_0, early_1 = pl.pallas_call(
        extract_kernel,
        in_specs=[SMEM, SMEM] + [HBM] * 4,
        out_specs=[VMEM] * 5,
        out_shape=[
            held(2 * SLOTS, 5 * FIELD),
            held(MOVERS, 10 * FIELD),
            held(MOVERS, 10 * FIELD),
            held(early_rows, TILE),
            held(early_rows, TILE),
        ],
        scratch_shapes=[
            pltpu.VMEM((SLOTS * TILE, TILE), f32),
            pltpu.VMEM((SLOTS * 2 * TILE, TILE), f32),
            pltpu.VMEM((SLOTS * TILE, TILE), f32),
            pltpu.VMEM((SLOTS * TILE, TILE), f32),
            pltpu.VMEM((5, TILE, TILE), f32),
            pltpu.VMEM((5, TILE, TILE), f32),
            pltpu.VMEM((TILE, TILE), f32),
            pltpu.SemaphoreType.DMA((SLOTS // GROUP, 4)),
            pltpu.SemaphoreType.DMA((2,)),
        ],
        compiler_params=pltpu.CompilerParams(vmem_limit_bytes=20 * 2**20),
        name="extract",
    )(plan, base, *tiles)
    from_0, from_1 = trade_both(up, down, "gy")
    early_0, early_1 = trade_both(early_0, early_1, "gy")

    first_rows = 4 * MOVERS
    dyn, fixed, *sends = call(
        settle_kernel,
        in_specs=[SMEM, SMEM] + [VMEM] * 4 + [HBM] * 4,
        out_specs=[VMEM] * 6,
        out_shape=[
            held(2 * SLOTS, 3 * FIELD),
            held(2 * SLOTS, 2 * FIELD),
            held(first_rows, TILE),
            held(first_rows, TILE),
            held(STATE + first_rows, TILE),
            held(STATE + first_rows, TILE),
        ],
        scratch_shapes=[pltpu.SemaphoreType.DMA((2,))],
        compiler_params=pltpu.CompilerParams(vmem_limit_bytes=12 * 2**20),
    )(plan, base, *on_core(nb, frames, from_0, from_1), *tiles)
    got = exchange(*sends)
    lows = [got[2]]
    highs = [got[3]]
    still = []
    trails = []
    late = []
    for turn in range(3):

        def body(*refs, turn=turn):
            step_kernel(turn, *refs)

        shapes = [
            (2 * SLOTS, 3 * FIELD),
            (2 * SLOTS, 5 * TILE),
            (2 * SLOTS, 2 * TILE),
            (MOVERS, TILE),
            (MOVERS, TILE),
            (STATE + MOVERS, TILE),
            (STATE + MOVERS, TILE),
        ]
        if turn == 2:
            shapes += [(len(LATE) * STATE, TILE)] * 2
        dyn, kept, trail, *sends = call(
            body,
            in_specs=[SMEM, SMEM] + [VMEM] * (7 + len(still)) + [HBM] * 4,
            out_specs=[VMEM] * len(shapes),
            out_shape=[held(*s) for s in shapes],
            scratch_shapes=[pltpu.SemaphoreType.DMA((2, 2))],
            compiler_params=pltpu.CompilerParams(vmem_limit_bytes=12 * 2**20),
        )(plan, base, *on_core(nb, dyn, fixed, *still, *got), *tiles)
        still = [kept]
        trails.append(trail)
        late = sends[4:]
        got = exchange(*sends[:4])
        lows.append(got[2])
        highs.append(got[3])

    late_0, late_1 = trade_both(*late, "gy")
    kept_inputs = on_core(
        nb, dyn, fixed, *still, *got, *trails, *lows[:3], *highs[:3], early_0, early_1
    )
    new_depth, new_flow, edges, columns = call(
        tile_kernel,
        in_specs=[SMEM] * 4 + [VMEM] * len(kept_inputs) + [HBM] * 4,
        out_specs=[HBM, HBM, VMEM, VMEM],
        out_shape=[
            struct(SLOTS * TILE, TILE),
            struct(SLOTS * 2 * TILE, TILE),
            held(10, SLOTS, TILE),
            held(3, TILE, TILE),
        ],
        scratch_shapes=[
            pltpu.VMEM((3 * TILE, TILE), f32),
            pltpu.VMEM((TILE, TILE), f32),
            pltpu.SMEM((SLOTS,), i32),
            pltpu.SMEM((SLOTS,), i32),
            pltpu.SemaphoreType.DMA,
            *loop_scratch(),
        ],
        compiler_params=pltpu.CompilerParams(vmem_limit_bytes=12 * 2**20),
    )(plan, base, tile_ids, nb, *kept_inputs, *tiles)
    new_depth, new_flow = pl.pallas_call(
        late_kernel,
        in_specs=[SMEM] * 3 + [VMEM] * 4 + [HBM] * 2,
        out_specs=[HBM, HBM],
        out_shape=[struct(SLOTS * TILE, TILE), struct(SLOTS * 2 * TILE, TILE)],
        input_output_aliases={7: 0, 8: 1},
        scratch_shapes=[
            pltpu.SMEM((SLOTS,), i32),
            pltpu.SMEM((SLOTS,), i32),
            pltpu.SMEM((1,), i32),
            *loop_scratch(),
        ],
        compiler_params=pltpu.CompilerParams(vmem_limit_bytes=12 * 2**20),
        name="late_tiles",
    )(plan, base, nb, *on_core(edges, columns, late_0, late_1), new_depth, new_flow)
    return (
        new_depth.reshape(SLOTS, TILE, TILE),
        new_flow.reshape(SLOTS, 2, TILE, TILE),
    )


def solution(mesh):
    return jax.shard_map(
        shards,
        mesh=mesh,
        in_specs=(
            P(("gx", "gy"), None, None),
            P(("gx", "gy"), None, None, None),
            P(("gx", "gy"), None, None),
            P(("gx", "gy"), None, None),
            P(("gx", "gy")),
            P(("gx", "gy"), None),
            P(("gx", "gy"), None, None, None),
        ),
        out_specs=(P(("gx", "gy"), None, None), P(("gx", "gy"), None, None, None)),
        check_vma=False,
    )
```

```python
import jax
import jax.numpy as jnp
from jax import lax
from jax.experimental import pallas as pl
from jax.experimental.pallas import tpu as pltpu
from jax.sharding import PartitionSpec as P


TILE = 128
SLOTS = 32
MOVERS = 8
DEPTH = 4
STRIPS = 2 * DEPTH
FIELD = STRIPS * TILE
STATE = 5 * TILE
EARLY = (0, 1)
RIDERS = ((), (2,), (3,), (4,))
LATE = (5, 6, 7)
GROUP = 8
GY = 16
BUFFERS = 6
OUT_BUFFERS = 4

gravity = 9.81
step_time = 0.25
spacing = 2.0
min_depth = 0.15
PULL = gravity * step_time / spacing
RUB = gravity * step_time * 0.5
GAIN = step_time / spacing
UNIT_H = 2.0 / (GAIN * PULL)
UNIT_Q = UNIT_H / GAIN
FLOOR = 2.0 * min_depth / UNIT_H
DRAG = RUB * UNIT_Q * (0.5 * UNIT_H) ** (-7.0 / 3.0)

f32 = jnp.float32
bf16 = jnp.bfloat16
i32 = jnp.int32


def flux(flow, h_lo, h_hi, slope, rub):
    depth_face = jnp.maximum(0.5 * (h_lo + h_hi), min_depth)
    drive = flow - (PULL * depth_face) * ((h_hi - h_lo) + slope)
    loss = jnp.exp2(jnp.log2(depth_face) * (-7.0 / 3.0))
    return drive / (1.0 + (rub * jnp.abs(flow)) * loss)


def unit_flux(flow, h_lo, h_hi, slope, rub):
    depth_sum = jnp.maximum(h_lo + h_hi, FLOOR)
    drive = flow - depth_sum * ((h_hi - h_lo) + slope)
    loss = jnp.exp2(jnp.log2(depth_sum) * (-7.0 / 3.0))
    return drive / (1.0 + (rub * jnp.abs(flow)) * loss)


def iota(shape, dim):
    return lax.broadcasted_iota(i32, shape, dim)


def route(onehot, rows):
    a = rows.astype(bf16)
    rest = rows - a.astype(f32)
    b = rest.astype(bf16)
    c = (rest - b.astype(f32)).astype(bf16)
    take = onehot.astype(bf16)

    def part(x):
        return jnp.dot(take, x, preferred_element_type=f32)

    return part(a) + part(b) + part(c)


def side_links(nb_ref, base, side):
    square = (SLOTS, SLOTS)
    rows = iota(square, 0)
    cols = iota(square, 1)
    link_row = jnp.broadcast_to(nb_ref[side : side + 1, :].astype(f32), square)
    diagonal = rows == cols

    def column(x):
        return jnp.broadcast_to(jnp.sum(jnp.where(diagonal, x, 0.0), 1, keepdims=True), square)

    first = base.astype(f32)

    def remote(link):
        return jnp.where((link >= 0.0) & ((link < first) | (link >= first + SLOTS)), 1.0, 0.0)

    link_b = column(link_row)
    missing = link_b[:, :1] < 0.0
    far_b = remote(link_b)
    far = far_b[:, :1]
    far_row = remote(link_row)
    near = jnp.where(link_b - first == cols.astype(f32), 1.0, 0.0)
    rank = jnp.sum(jnp.where(link_row < link_b, far_row, 0.0), 1, keepdims=True)
    order_row = jnp.sum(jnp.where(rows < cols, far_b, 0.0), 0, keepdims=True)
    far_row = far_row[:1]
    place = jnp.where(
        (jnp.broadcast_to(rank, (SLOTS, MOVERS)) == iota((SLOTS, MOVERS), 1).astype(f32))
        & (jnp.broadcast_to(far, (SLOTS, MOVERS)) > 0.0),
        1.0,
        0.0,
    )
    pick = jnp.where(
        (jnp.broadcast_to(order_row, (MOVERS, SLOTS)) == iota((MOVERS, SLOTS), 0).astype(f32))
        & (jnp.broadcast_to(far_row, (MOVERS, SLOTS)) > 0.0),
        1.0,
        0.0,
    )
    exists = jnp.where(missing, 0.0, 1.0)
    return near, place, pick, exists


def halo_of(links, rows, message):
    near, place, _, _ = links
    return route(near, rows) + route(place, message)


def extract_kernel(
    moves, base, depth, discharge, bed, friction, frames, out_0, out_1, early_0, early_1,
    depth_v, flow_v, bed_v, rough_v, acc, turned, load_sem, sem,
):
    lane = iota((TILE, TILE), 1)
    groups = SLOTS // GROUP
    loads = []
    for g in range(groups):
        one = pl.ds(g * GROUP * TILE, GROUP * TILE)
        two = pl.ds(g * GROUP * 2 * TILE, GROUP * 2 * TILE)
        pairs = ((depth, depth_v, one), (discharge, flow_v, two), (bed, bed_v, one), (friction, rough_v, one))
        copies = [pltpu.make_async_copy(a.at[r], b.at[r], load_sem.at[g, i]) for i, (a, b, r) in enumerate(pairs)]
        for c in copies:
            c.start()
        loads.append(copies)
    start_chunk(EARLY, moves, base, (depth, discharge, bed, friction), early_0, early_1, sem)

    def strip(f, k):
        return pl.ds((f * STRIPS + k) * TILE, TILE)

    sources = ((depth_v, 0, 1), (flow_v, 0, 2), (flow_v, 1, 2), (bed_v, 0, 1), (rough_v, 0, 1))
    for g in range(groups):
        for c in loads[g]:
            c.wait()
        home = pl.ds(g * GROUP, GROUP)
        for f, (ref, part, parts) in enumerate(sources):
            top = (g * GROUP * parts + part) * TILE
            for k in range(STRIPS):
                row = k if k < DEPTH else TILE - STRIPS + k
                frames[home, strip(f, k)] = ref[pl.ds(top + row, GROUP, stride=parts * TILE), :]
            half = g * GROUP * STRIPS // TILE
            packed = acc[half, f] if g * GROUP * STRIPS % TILE else None
            for t in range(GROUP):
                tile = ref[pl.ds(top + t * parts * TILE, TILE), :]
                at = (g * GROUP + t) * STRIPS % TILE
                turn = pltpu.roll(tile, (at + DEPTH) % TILE, 1)
                packed = turn if packed is None else jnp.where(lane >= at, turn, packed)
            acc[half, f] = packed

    per = TILE // STRIPS
    for f in range(5):
        to = (0, 2, 1, 3, 4)[f]
        for half in range(SLOTS // per):
            turned[half] = acc[half, f].T
            for k in range(STRIPS):
                frames[pl.ds(SLOTS + half * per, per), strip(to, k)] = turned[
                    half, pl.ds((k + DEPTH) % STRIPS, per, stride=STRIPS), :
                ]
    shape = (2 * MOVERS, SLOTS)
    pick = jnp.zeros(shape, f32)
    for m in range(MOVERS):
        for pairing in range(2):
            leaver = moves[way_of(base, pairing), 0, m] - base[0]
            spot = (iota(shape, 0) == pairing * MOVERS + m) & (iota(shape, 1) == leaver)
            pick = jnp.where(spot, 1.0, pick)
    for axis in range(2):
        for c in range(5):
            got = route(pick, frames[pl.ds(axis * SLOTS, SLOTS), pl.ds(c * FIELD, FIELD)])
            to = pl.ds((axis * 5 + c) * FIELD, FIELD)
            out_0[:, to] = got[:MOVERS]
            out_1[:, to] = got[MOVERS:]
    finish_chunk(EARLY, early_0, early_1, sem)


def start_chunk(entries, moves, base, tiles, out_0, out_1, sem):
    depth, discharge, bed, friction = tiles
    for pairing, out in enumerate((out_0, out_1)):
        way = way_of(base, pairing)
        for i, m in enumerate(entries):
            slot = jnp.clip(moves[way, 0, m] - base[0], 0, SLOTS - 1)
            at = i * STATE
            one = pl.ds(pl.multiple_of(slot * TILE, TILE), TILE)
            two = pl.ds(pl.multiple_of(slot * (2 * TILE), TILE), 2 * TILE)
            pltpu.make_async_copy(depth.at[one], out.at[pl.ds(at, TILE)], sem.at[pairing]).start()
            pltpu.make_async_copy(discharge.at[two], out.at[pl.ds(at + TILE, 2 * TILE)], sem.at[pairing]).start()
            pltpu.make_async_copy(bed.at[one], out.at[pl.ds(at + 3 * TILE, TILE)], sem.at[pairing]).start()
            pltpu.make_async_copy(friction.at[one], out.at[pl.ds(at + 4 * TILE, TILE)], sem.at[pairing]).start()


def finish_chunk(entries, out_0, out_1, sem):
    if not entries:
        return
    body = pl.ds(0, len(entries) * STATE)
    for pairing, out in enumerate((out_0, out_1)):
        pltpu.make_async_copy(out.at[body], out.at[body], sem.at[pairing]).wait()


def is_odd(base, axis):
    return ((base[0] // (SLOTS * (GY if axis == 0 else 1))) % 2) == 1


def way_of(base, pairing):
    odd = (base[0] // SLOTS) % 2
    return odd if pairing else 1 - odd


def swap(odd, a, b):
    return jnp.where(odd, b, a), jnp.where(odd, a, b)


def settle_kernel(
    moves, base, nb, frames, from_0, from_1, depth, discharge, bed, friction,
    dyn, fixed, x_0, x_1, y_0, y_1, sem,
):
    ride = RIDERS[0]
    start_chunk(ride, moves, base, (depth, discharge, bed, friction), y_0, y_1, sem)
    shape = (SLOTS, 2 * MOVERS)
    land = jnp.zeros(shape, f32)
    left = jnp.zeros((SLOTS, TILE), f32)
    for m in range(MOVERS):
        for pairing in range(2):
            way = way_of(base, pairing)
            lander = moves[way, 1, m] - base[0]
            leaver = moves[way, 0, m] - base[0]
            spot = (iota(shape, 0) == lander) & (iota(shape, 1) == pairing * MOVERS + m)
            land = jnp.where(spot, 1.0, land)
            row = iota((SLOTS, TILE), 0)
            left = jnp.where((row == leaver) | (row == lander), 1.0, left)
    for axis in range(2):
        home = pl.ds(axis * SLOTS, SLOTS)
        for f in range(5):
            part = pl.ds(f * FIELD, FIELD)
            came = pl.ds((axis * 5 + f) * FIELD, FIELD)
            fresh = route(land, jnp.concatenate([from_0[:, came], from_1[:, came]], 0))
            for k in range(STRIPS):
                sub = pl.ds(f * FIELD + k * TILE, TILE)
                value = jnp.where(left > 0.0, 0.0, frames[home, sub]) + fresh[:, k * TILE : (k + 1) * TILE]
                if f < 3:
                    dyn[home, sub] = value
                else:
                    fixed[home, pl.ds((f - 3) * FIELD + k * TILE, TILE)] = value

    def edge(ref, axis, f, k):
        return ref[pl.ds(axis * SLOTS, SLOTS), pl.ds(f * FIELD + k * TILE, TILE)]

    last = STRIPS - 1
    blank = jnp.zeros((MOVERS, TILE), f32)
    for axis in range(2):
        lower = side_links(nb, base[0], 2 * axis)
        higher = side_links(nb, base[0], 2 * axis + 1)
        ups = (edge(dyn, axis, 0, last), edge(fixed, axis, 0, last), edge(fixed, axis, 1, last), edge(dyn, axis, 1, last))
        downs = (edge(dyn, axis, 0, 0), edge(fixed, axis, 0, 0), edge(fixed, axis, 1, 0))
        for f in range(4):
            up = route(higher[2], ups[f])
            down = route(lower[2], downs[f]) if f < 3 else blank
            up, down = swap(is_odd(base, axis), up, down)
            if axis == 0:
                x_0[pl.ds(f * MOVERS, MOVERS), :] = up
                x_1[pl.ds(f * MOVERS, MOVERS), :] = down
            else:
                y_0[pl.ds(len(ride) * STATE + f * MOVERS, MOVERS), :] = up
                y_1[pl.ds(len(ride) * STATE + f * MOVERS, MOVERS), :] = down
    finish_chunk(ride, y_0, y_1, sem)


def other_axis(x):
    return jnp.concatenate([x[SLOTS:], x[:SLOTS]], 0)


def gather_halos(nb, base_ref, dyn, fixed, messages, turn):
    first = turn == 0
    riding = len(RIDERS[turn])
    last = STRIPS - 1
    out = {}
    parts = {name: [] for name in ("h_lo", "h_hi", "z_lo", "n_lo", "q_lo", "z_hi", "n_hi", "lo", "hi")}
    picks = []
    for axis in range(2):
        home = pl.ds(axis * SLOTS, SLOTS)
        lower = side_links(nb, base_ref[0], 2 * axis)
        higher = side_links(nb, base_ref[0], 2 * axis + 1)
        picks.append((lower[2], higher[2]))

        def message(f):
            rows = pl.ds(axis * riding * STATE + f * MOVERS, MOVERS)
            pair = messages[axis]
            from_higher, from_lower = swap(is_odd(base_ref, axis), pair[0][rows, :], pair[1][rows, :])
            return from_lower, from_higher

        def strip(ref, f, k):
            return ref[home, pl.ds(f * FIELD + k * TILE, TILE)]

        def low(f, rows):
            return halo_of(lower, rows, message(f)[0])

        def high(f, rows):
            return halo_of(higher, rows, message(f)[1])

        parts["h_lo"].append(low(0, strip(dyn, 0, last)))
        parts["h_hi"].append(high(0, strip(dyn, 0, 0)))
        if first:
            parts["z_lo"].append(low(1, strip(fixed, 0, last)))
            parts["n_lo"].append(low(2, strip(fixed, 1, last)))
            parts["q_lo"].append(low(3, strip(dyn, 1, last)))
            parts["z_hi"].append(high(1, strip(fixed, 0, 0)))
            parts["n_hi"].append(high(2, strip(fixed, 1, 0)))
        parts["lo"].append(jnp.broadcast_to(lower[3], (SLOTS, TILE)))
        parts["hi"].append(jnp.broadcast_to(higher[3], (SLOTS, TILE)))
    for name, pieces in parts.items():
        if pieces:
            out[name] = jnp.concatenate(pieces, 0)
    return out, picks


def step_kernel(turn, moves, base, nb, dyn, fixed, *rest):
    first = turn == 0
    if first:
        still = None
        (x0, x1, y0, y1), rest = rest[:4], rest[4:]
    else:
        still = rest[0]
        (x0, x1, y0, y1), rest = rest[1:5], rest[5:]
    depth, discharge, bed, friction = rest[:4]
    tiles = (depth, discharge, bed, friction)
    final = turn == 2
    if final:
        (dyn_out, still_out, trail, x_0, x_1, y_0, y_1, late_0, late_1, sem) = rest[4:]
    else:
        (dyn_out, still_out, trail, x_0, x_1, y_0, y_1, sem) = rest[4:]
    ride = RIDERS[turn + 1]
    start_chunk(ride, moves, base, tiles, y_0, y_1, sem.at[0])
    if final:
        start_chunk(LATE, moves, base, tiles, late_0, late_1, sem.at[1])
    halo, picks = gather_halos(nb, base, dyn, fixed, ((x0, x1), (y0, y1)), turn)
    names = ("z_lo", "n_lo", "z_hi", "n_hi", "q_lo")
    if not first:
        for j, name in enumerate(names):
            halo[name] = still[:, pl.ds(j * TILE, TILE)]

    def get(ref, f, k):
        return ref[:, pl.ds(f * FIELD + k * TILE, TILE)]

    last = STRIPS - 1
    h = [get(dyn, 0, k) for k in range(STRIPS)]
    z = [get(fixed, 0, k) for k in range(STRIPS)]
    n = [get(fixed, 1, k) for k in range(STRIPS)]
    low_face = flux(halo["q_lo"], halo["h_lo"], h[0], z[0] - halo["z_lo"], RUB * (halo["n_lo"] + n[0]))
    low_face = jnp.where(halo["lo"] > 0.0, low_face, 0.0)
    high_face = flux(get(dyn, 1, last), h[last], halo["h_hi"], halo["z_hi"] - z[last], RUB * (n[last] + halo["n_hi"]))
    high_face = jnp.where(halo["hi"] > 0.0, high_face, 0.0)
    for j, name in enumerate(names[:4]):
        still_out[:, pl.ds(j * TILE, TILE)] = halo[name]
    still_out[:, pl.ds(4 * TILE, TILE)] = low_face
    trail[:, pl.ds(0, TILE)] = low_face
    trail[:, pl.ds(TILE, TILE)] = halo["h_hi"]

    lane = iota((2 * SLOTS, TILE), 1)
    side_h = other_axis(halo["h_hi"])
    side_z = other_axis(halo["z_hi"])
    side_n = other_axis(halo["n_hi"])
    side_wall = other_axis(halo["hi"]) <= 0.0
    side_in = other_axis(low_face)

    def cell(x, k):
        at = k if k < DEPTH else TILE - STRIPS + k
        return jnp.broadcast_to(x[:, at : at + 1], x.shape)

    def ahead(x, k, side):
        return jnp.where(lane == TILE - 1, cell(side, k), pltpu.roll(x, TILE - 1, 1))

    reach = DEPTH - 1 - turn
    low_keep = list(range(reach))
    high_keep = list(range(STRIPS - reach, STRIPS))
    face = {-1: low_face, last: high_face}
    for k in low_keep + [x - 1 for x in high_keep]:
        face[k] = flux(get(dyn, 1, k), h[k], h[k + 1], z[k + 1] - z[k], RUB * (n[k] + n[k + 1]))
    new = {}
    for k in low_keep + high_keep:
        side = flux(
            get(dyn, 2, k), h[k], ahead(h[k], k, side_h), ahead(z[k], k, side_z) - z[k],
            RUB * (n[k] + ahead(n[k], k, side_n)),
        )
        side = jnp.where((lane == TILE - 1) & side_wall, 0.0, side)
        before = jnp.where(lane == 0, cell(side_in, k), pltpu.roll(side, 1, 1))
        new[k] = h[k] + GAIN * ((face[k - 1] - face[k]) + (before - side))
        dyn_out[:, pl.ds(2 * FIELD + k * TILE, TILE)] = side
    blank = jnp.zeros((2 * SLOTS, TILE), f32)
    for k in range(STRIPS):
        dyn_out[:, pl.ds(k * TILE, TILE)] = new[k] if k in new else blank
        dyn_out[:, pl.ds(FIELD + k * TILE, TILE)] = face[k] if k in face else blank
        if k not in new:
            dyn_out[:, pl.ds(2 * FIELD + k * TILE, TILE)] = blank
    for axis in range(2):
        home = slice(axis * SLOTS, (axis + 1) * SLOTS)
        up = route(picks[axis][1], new[last][home])
        down = route(picks[axis][0], new[0][home])
        up, down = swap(is_odd(base, axis), up, down)
        if axis == 0:
            x_0[...] = up
            x_1[...] = down
        else:
            y_0[pl.ds(len(ride) * STATE, MOVERS), :] = up
            y_1[pl.ds(len(ride) * STATE, MOVERS), :] = down
    finish_chunk(ride, y_0, y_1, sem.at[0])
    if final:
        finish_chunk(LATE, late_0, late_1, sem.at[1])


def run_tiles(
    queue, origin, count, moves_sources, tiles, nb_s, edges, columns, outs, before_loop,
    inbox, outbox, in_sem, out_sem, *spaces,
):
    depth, discharge, bed, friction = tiles
    depth_out, flow_out = outs

    def fetch(j):
        t = queue[j]
        buf = j % BUFFERS
        sem = in_sem.at[buf]
        box = inbox.at[buf]
        kind = origin[t]

        if depth is not None:

            @pl.when(kind == 0)
            def _():
                one = pl.ds(pl.multiple_of(t * TILE, TILE), TILE)
                two = pl.ds(pl.multiple_of(t * (2 * TILE), TILE), 2 * TILE)
                pltpu.make_async_copy(depth.at[one], box.at[pl.ds(0, TILE)], sem).start()
                pltpu.make_async_copy(discharge.at[two], box.at[pl.ds(TILE, 2 * TILE)], sem).start()
                pltpu.make_async_copy(bed.at[one], box.at[pl.ds(3 * TILE, TILE)], sem).start()
                pltpu.make_async_copy(friction.at[one], box.at[pl.ds(4 * TILE, TILE)], sem).start()

        for code, ref, at in moves_sources:

            @pl.when(kind == code)
            def _():
                pltpu.make_async_copy(ref.at[pl.ds(at, STATE)], box, sem).start()

    def arrived(buf):
        box = inbox.at[buf]
        pltpu.make_async_copy(box, box, in_sem.at[buf]).wait()

    def send(t, buf):
        box = outbox.at[buf]
        one = pl.ds(pl.multiple_of(t * TILE, TILE), TILE)
        two = pl.ds(pl.multiple_of(t * (2 * TILE), TILE), 2 * TILE)
        pltpu.make_async_copy(box.at[pl.ds(0, TILE)], depth_out.at[one], out_sem.at[buf]).start()
        pltpu.make_async_copy(box.at[pl.ds(TILE, 2 * TILE)], flow_out.at[two], out_sem.at[buf]).start()

    def sent(buf):
        box = outbox.at[buf]
        pltpu.make_async_copy(box, box, out_sem.at[buf]).wait()

    def prime():
        for j in range(BUFFERS - 2):

            @pl.when(j < count)
            def _():
                fetch(j)

    prime()
    before_loop()
    part_rows = 16
    parts = TILE // part_rows
    lane = iota((part_rows, TILE), 1)
    row = iota((part_rows, TILE), 0)
    at_first = lane == 0
    at_last = lane == TILE - 1
    bottom = row == part_rows - 1

    def ready(j):
        @pl.when(j < count)
        def _():
            arrived(j % BUFFERS)

        @pl.when((j >= OUT_BUFFERS) & (j < count))
        def _():
            sent(j % OUT_BUFFERS)

    def work(j, space):
        water, stream_x, stream_y, slope_x, slope_y, rub_x, rub_y = space
        t = queue[jnp.minimum(j, count - 1)]
        box = inbox.at[j % BUFFERS]
        out = outbox.at[j % OUT_BUFFERS]
        wall_x = nb_s[1, t] < 0
        wall_y = nb_s[3, t] < 0

        def edge_row(e):
            return edges[e, pl.ds(t, 1), :]

        z_next = edge_row(8)
        n_next = edge_row(9)
        for p in range(parts):
            rows = pl.ds(p * part_rows, part_rows)
            zr = pl.ds(3 * TILE + p * part_rows, part_rows)
            nr = pl.ds(4 * TILE + p * part_rows, part_rows)
            z = box[zr, :] * (1.0 / UNIT_H)
            n = box[nr, :]
            if p < parts - 1:
                z_dn = box[pl.ds(3 * TILE + p * part_rows + 1, part_rows), :] * (1.0 / UNIT_H)
                n_dn = box[pl.ds(4 * TILE + p * part_rows + 1, part_rows), :]
            else:
                z_dn = jnp.where(bottom, z_next, pltpu.roll(z, part_rows - 1, 0))
                n_dn = jnp.where(bottom, n_next, pltpu.roll(n, part_rows - 1, 0))
            side = columns[2, rows, :]
            z_rt = jnp.where(at_last, pltpu.roll(side, TILE - 1 - t, 1), pltpu.roll(z, TILE - 1, 1))
            n_rt = jnp.where(at_last, pltpu.roll(side, TILE - 1 - SLOTS - t, 1), pltpu.roll(n, TILE - 1, 1))
            slope_x[rows, :] = z_dn - z
            slope_y[rows, :] = z_rt - z
            rub_x[rows, :] = DRAG * (n + n_dn)
            rub_y[rows, :] = DRAG * (n + n_rt)
            water[rows, :] = box[rows, :] * (1.0 / UNIT_H)
        for s in range(4):
            water[pl.ds(TILE, 1), :] = edge_row(4 + s)
            stream_x[pl.ds(7, 1), :] = edge_row(s)
            for p in range(parts):
                rows = pl.ds(p * part_rows, part_rows)
                h = water[rows, :]
                h_dn = water[pl.ds(p * part_rows + 1, part_rows), :]
                side = pltpu.roll(columns[s // 2, rows, :], TILE - 1 - 64 * (s % 2) - 2 * t, 1)
                h_rt = jnp.where(at_last, side, pltpu.roll(h, TILE - 1, 1))
                if s == 0:
                    flow_x = box[pl.ds(TILE + p * part_rows, part_rows), :] * (1.0 / UNIT_Q)
                    flow_y = box[pl.ds(2 * TILE + p * part_rows, part_rows), :] * (1.0 / UNIT_Q)
                else:
                    flow_x = stream_x[pl.ds(8 + p * part_rows, part_rows), :]
                    flow_y = stream_y[rows, :]
                new_x = unit_flux(flow_x, h, h_dn, slope_x[rows, :], rub_x[rows, :])
                if p == parts - 1:
                    new_x = jnp.where(bottom & wall_x, 0.0, new_x)
                new_y = unit_flux(flow_y, h, h_rt, slope_y[rows, :], rub_y[rows, :])
                new_y = jnp.where(at_last & wall_y, 0.0, new_y)
                if s < 3:
                    stream_y[rows, :] = new_y
                else:
                    out[pl.ds(TILE + p * part_rows, part_rows), :] = new_x * UNIT_Q
                    out[pl.ds(2 * TILE + p * part_rows, part_rows), :] = new_y * UNIT_Q
                in_y = jnp.where(at_first, side, pltpu.roll(new_y, 1, 1))
                stream_x[pl.ds(8 + p * part_rows, part_rows), :] = new_x
                in_x = stream_x[pl.ds(7 + p * part_rows, part_rows), :]
                h_new = h + ((in_x - new_x) + (in_y - new_y))
                if s < 3:
                    water[rows, :] = h_new
                else:
                    out[rows, :] = h_new * UNIT_H

    def two_tiles(pair, carry):
        for i in range(2):
            j = 2 * pair + i

            @pl.when(j + BUFFERS - 2 < count)
            def _():
                fetch(j + BUFFERS - 2)

            ready(j)
        half = len(spaces) // 2
        for i in range(2):
            work(2 * pair + i, spaces[i * half : (i + 1) * half])
        for i in range(2):
            j = 2 * pair + i

            @pl.when(j < count)
            def _():
                send(queue[j], j % OUT_BUFFERS)

        return carry

    lax.fori_loop(0, (count + 1) // 2, two_tiles, 0)
    for b in range(OUT_BUFFERS):

        @pl.when(b < count)
        def _():
            sent(b)


def chunk_sources(entries, *chunks):
    found = []
    for pairing, ref in enumerate(chunks):
        for i, m in enumerate(entries):
            found.append((1 + pairing * MOVERS + m, ref, i * STATE))
    return found


def note_arrivals(entries, moves, base, visit):
    for m in entries:
        for pairing in range(2):
            lander = moves[way_of(base, pairing), 1, m]

            @pl.when(lander >= 0)
            def _():
                visit(lander - base[0], 1 + pairing * MOVERS + m)


def tile_kernel(
    moves, base, ids, nb_s, nb, dyn, fixed, still, x_0, x_1, l3, u3, t0, t1, t2,
    l1, l2, u1, u2, early_0, early_1, depth, discharge, bed, friction,
    depth_out, flow_out, edges, columns,
    zeros, turned, queue, origin, zero_sem, *scratch,
):
    def clear(t, total):
        origin[t] = 0
        return total + jnp.where(ids[t] >= 0, 1, 0)

    live = lax.fori_loop(0, SLOTS, clear, 0)

    def mark(t, code):
        origin[t] = code

    note_arrivals(EARLY + RIDERS[1] + RIDERS[2] + RIDERS[3], moves, base, mark)
    note_arrivals(LATE, moves, base, lambda t, code: mark(t, -1))

    def enqueue(t, size):
        keep = origin[t] >= 0
        queue[size] = t
        return size + jnp.where(keep, 1, 0)

    count = lax.fori_loop(0, live, enqueue, 0)
    zeros[...] = jnp.zeros(zeros.shape, f32)

    def blank(t, carry):
        one = pl.ds(pl.multiple_of(t * TILE, TILE), TILE)
        two = pl.ds(pl.multiple_of(t * (2 * TILE), TILE), 2 * TILE)
        pltpu.make_async_copy(zeros.at[pl.ds(0, TILE)], depth_out.at[one], zero_sem).start()
        pltpu.make_async_copy(zeros.at[pl.ds(TILE, 2 * TILE)], flow_out.at[two], zero_sem).start()
        return carry

    def before_loop():
        lax.fori_loop(live, SLOTS, blank, 0)
        halo, _ = gather_halos(nb, base, dyn, fixed, ((x_0, x_1), (l3, u3)), 3)

        def kept(j):
            return still[:, pl.ds(j * TILE, TILE)]

        n_first = fixed[:, pl.ds(FIELD, TILE)]
        z_first = fixed[:, pl.ds(0, TILE)]
        low_face = flux(
            kept(4), halo["h_lo"], dyn[:, pl.ds(0, TILE)], z_first - kept(0), RUB * (kept(1) + n_first)
        )
        low_face = jnp.where(halo["lo"] > 0.0, low_face, 0.0)
        trails = [(t[:, pl.ds(0, TILE)], t[:, pl.ds(TILE, TILE)]) for t in (t0, t1, t2)]
        trails.append((low_face, halo["h_hi"]))
        for s, (inflow, ahead_h) in enumerate(trails):
            inflow = inflow * (1.0 / UNIT_Q)
            ahead_h = ahead_h * (1.0 / UNIT_H)
            edges[s] = inflow[:SLOTS]
            edges[4 + s] = ahead_h[:SLOTS]
            turned[pl.ds(64 * (s % 2), SLOTS, stride=2), :] = ahead_h[SLOTS:]
            turned[pl.ds(64 * (s % 2) + 1, SLOTS, stride=2), :] = inflow[SLOTS:]
            if s % 2:
                columns[s // 2] = turned[...].T
        z_ahead = kept(2) * (1.0 / UNIT_H)
        edges[8] = z_ahead[:SLOTS]
        edges[9] = kept(3)[:SLOTS]
        turned[pl.ds(0, SLOTS), :] = z_ahead[SLOTS:]
        turned[pl.ds(SLOTS, SLOTS), :] = kept(3)[SLOTS:]
        columns[2] = turned[...].T

    sources = chunk_sources(EARLY, early_0, early_1)
    for entries, chunk_0, chunk_1 in zip(RIDERS[1:], (l1, l2, l3), (u1, u2, u3)):
        sources += chunk_sources(entries, chunk_0, chunk_1)
    run_tiles(
        queue, origin, count, sources, (depth, discharge, bed, friction), nb_s, edges, columns,
        (depth_out, flow_out), before_loop, *scratch,
    )

    def blanked(t, carry):
        pltpu.make_async_copy(zeros, zeros, zero_sem).wait()
        return carry

    lax.fori_loop(live, SLOTS, blanked, 0)


def late_kernel(
    moves, base, nb_s, edges, columns, late_0, late_1, depth_in, flow_in,
    depth_out, flow_out, queue, origin, size, *scratch,
):
    size[0] = 0

    def enqueue(t, code):
        queue[size[0]] = t
        origin[t] = code
        size[0] = size[0] + 1

    note_arrivals(LATE, moves, base, enqueue)
    run_tiles(
        queue, origin, size[0], chunk_sources(LATE, late_0, late_1), (None,) * 4, nb_s, edges, columns,
        (depth_out, flow_out), lambda: None, *scratch,
    )


SMEM = pl.BlockSpec(memory_space=pltpu.SMEM)
VMEM = pl.BlockSpec(memory_space=pltpu.VMEM)
HBM = pl.BlockSpec(memory_space=pltpu.HBM)


def trade(block, axis, pairing):
    size = lax.axis_size(axis)
    pairs = []
    for i in range(size):
        other = i ^ 1 if pairing == 0 else ((i + 1) ^ 1) - 1
        if 0 <= other < size:
            pairs.append((i, other))
    return lax.ppermute(block, axis, pairs)


def trade_both(block_0, block_1, axis):
    got_1 = trade(block_1, axis, 1)
    got_0 = trade(block_0, axis, 0)
    return got_0, got_1


def exchange(x_0, x_1, y_0, y_1):
    got_y = trade_both(y_0, y_1, "gy")
    got_x = trade_both(x_0, x_1, "gx")
    return *got_x, *got_y


def held(*shape):
    return pltpu.VMEM(shape, f32)


def on_core(*arrays):
    return [pltpu.with_memory_space_constraint(a, pltpu.VMEM) for a in arrays]


def call(kernel, **settings):
    return pl.pallas_call(kernel, **settings)


def struct(*shape):
    return jax.ShapeDtypeStruct(shape, f32)


def loop_scratch():
    space = [
        pltpu.VMEM((TILE + 8, TILE), f32),
        pltpu.VMEM((TILE + 8, TILE), f32),
        *[pltpu.VMEM((TILE, TILE), f32)] * 5,
    ]
    return [
        pltpu.VMEM((BUFFERS, STATE, TILE), f32),
        pltpu.VMEM((OUT_BUFFERS, 3 * TILE, TILE), f32),
        pltpu.SemaphoreType.DMA((BUFFERS,)),
        pltpu.SemaphoreType.DMA((OUT_BUFFERS,)),
        *space,
        *space,
    ]


def shards(depth, discharge, bed, friction, tile_ids, neighbors, moves):
    base = (lax.axis_index(("gx", "gy")) * SLOTS).astype(i32).reshape(1)
    plan = moves[0].transpose(0, 2, 1)
    nb = neighbors.T
    tiles = [
        pltpu.with_memory_space_constraint(a, pltpu.HBM)
        for a in (
            depth.reshape(SLOTS * TILE, TILE),
            discharge.reshape(SLOTS * 2 * TILE, TILE),
            bed.reshape(SLOTS * TILE, TILE),
            friction.reshape(SLOTS * TILE, TILE),
        )
    ]
    early_rows = len(EARLY) * STATE
    frames, up, down, early_0, early_1 = pl.pallas_call(
        extract_kernel,
        in_specs=[SMEM, SMEM] + [HBM] * 4,
        out_specs=[VMEM] * 5,
        out_shape=[
            held(2 * SLOTS, 5 * FIELD),
            held(MOVERS, 10 * FIELD),
            held(MOVERS, 10 * FIELD),
            held(early_rows, TILE),
            held(early_rows, TILE),
        ],
        scratch_shapes=[
            pltpu.VMEM((SLOTS * TILE, TILE), f32),
            pltpu.VMEM((SLOTS * 2 * TILE, TILE), f32),
            pltpu.VMEM((SLOTS * TILE, TILE), f32),
            pltpu.VMEM((SLOTS * TILE, TILE), f32),
            pltpu.VMEM((2, 5, TILE, TILE), f32),
            pltpu.VMEM((2, TILE, TILE), f32),
            pltpu.SemaphoreType.DMA((SLOTS // GROUP, 4)),
            pltpu.SemaphoreType.DMA((2,)),
        ],
        compiler_params=pltpu.CompilerParams(vmem_limit_bytes=20 * 2**20),
        name="extract",
    )(plan, base, *tiles)
    from_0, from_1 = trade_both(up, down, "gy")
    early_0, early_1 = trade_both(early_0, early_1, "gy")

    first_rows = 4 * MOVERS
    dyn, fixed, *sends = call(
        settle_kernel,
        in_specs=[SMEM, SMEM] + [VMEM] * 4 + [HBM] * 4,
        out_specs=[VMEM] * 6,
        out_shape=[
            held(2 * SLOTS, 3 * FIELD),
            held(2 * SLOTS, 2 * FIELD),
            held(first_rows, TILE),
            held(first_rows, TILE),
            held(len(RIDERS[0]) * STATE + first_rows, TILE),
            held(len(RIDERS[0]) * STATE + first_rows, TILE),
        ],
        scratch_shapes=[pltpu.SemaphoreType.DMA((2,))],
        compiler_params=pltpu.CompilerParams(vmem_limit_bytes=12 * 2**20),
    )(plan, base, *on_core(nb, frames, from_0, from_1), *tiles)
    got = exchange(*sends)
    lows = [got[2]]
    highs = [got[3]]
    still = []
    trails = []
    late = []
    for turn in range(3):

        def body(*refs, turn=turn):
            step_kernel(turn, *refs)

        shapes = [
            (2 * SLOTS, 3 * FIELD),
            (2 * SLOTS, 5 * TILE),
            (2 * SLOTS, 2 * TILE),
            (MOVERS, TILE),
            (MOVERS, TILE),
            (len(RIDERS[turn + 1]) * STATE + MOVERS, TILE),
            (len(RIDERS[turn + 1]) * STATE + MOVERS, TILE),
        ]
        if turn == 2:
            shapes += [(len(LATE) * STATE, TILE)] * 2
        dyn, kept, trail, *sends = call(
            body,
            in_specs=[SMEM, SMEM] + [VMEM] * (7 + len(still)) + [HBM] * 4,
            out_specs=[VMEM] * len(shapes),
            out_shape=[held(*s) for s in shapes],
            scratch_shapes=[pltpu.SemaphoreType.DMA((2, 2))],
            compiler_params=pltpu.CompilerParams(vmem_limit_bytes=12 * 2**20),
        )(plan, base, *on_core(nb, dyn, fixed, *still, *got), *tiles)
        still = [kept]
        trails.append(trail)
        late = sends[4:]
        got = exchange(*sends[:4])
        lows.append(got[2])
        highs.append(got[3])

    late_0, late_1 = trade_both(*late, "gy")
    kept_inputs = on_core(
        nb, dyn, fixed, *still, *got, *trails, *lows[1:3], *highs[1:3], early_0, early_1
    )
    new_depth, new_flow, edges, columns = call(
        tile_kernel,
        in_specs=[SMEM] * 4 + [VMEM] * len(kept_inputs) + [HBM] * 4,
        out_specs=[HBM, HBM, VMEM, VMEM],
        out_shape=[
            struct(SLOTS * TILE, TILE),
            struct(SLOTS * 2 * TILE, TILE),
            held(10, SLOTS, TILE),
            held(3, TILE, TILE),
        ],
        scratch_shapes=[
            pltpu.VMEM((3 * TILE, TILE), f32),
            pltpu.VMEM((TILE, TILE), f32),
            pltpu.SMEM((SLOTS,), i32),
            pltpu.SMEM((SLOTS,), i32),
            pltpu.SemaphoreType.DMA,
            *loop_scratch(),
        ],
        compiler_params=pltpu.CompilerParams(vmem_limit_bytes=12 * 2**20),
    )(plan, base, tile_ids, nb, *kept_inputs, *tiles)
    new_depth, new_flow = pl.pallas_call(
        late_kernel,
        in_specs=[SMEM] * 3 + [VMEM] * 4 + [HBM] * 2,
        out_specs=[HBM, HBM],
        out_shape=[struct(SLOTS * TILE, TILE), struct(SLOTS * 2 * TILE, TILE)],
        input_output_aliases={7: 0, 8: 1},
        scratch_shapes=[
            pltpu.SMEM((SLOTS,), i32),
            pltpu.SMEM((SLOTS,), i32),
            pltpu.SMEM((1,), i32),
            *loop_scratch(),
        ],
        compiler_params=pltpu.CompilerParams(vmem_limit_bytes=12 * 2**20),
        name="late_tiles",
    )(plan, base, nb, *on_core(edges, columns, late_0, late_1), new_depth, new_flow)
    return (
        new_depth.reshape(SLOTS, TILE, TILE),
        new_flow.reshape(SLOTS, 2, TILE, TILE),
    )


def solution(mesh):
    return jax.shard_map(
        shards,
        mesh=mesh,
        in_specs=(
            P(("gx", "gy"), None, None),
            P(("gx", "gy"), None, None, None),
            P(("gx", "gy"), None, None),
            P(("gx", "gy"), None, None),
            P(("gx", "gy")),
            P(("gx", "gy"), None),
            P(("gx", "gy"), None, None, None),
        ),
        out_specs=(P(("gx", "gy"), None, None), P(("gx", "gy"), None, None, None)),
        check_vma=False,
    )
```

```python
import jax
import jax.numpy as jnp
from jax import lax
from jax.experimental import pallas as pl
from jax.experimental.pallas import tpu as pltpu
from jax.sharding import PartitionSpec as P


TILE = 128
SLOTS = 32
MOVERS = 8
DEPTH = 4
STRIPS = 2 * DEPTH
FIELD = STRIPS * TILE
STATE = 5 * TILE
EARLY = (0,)
CHUNKS = ((1,), (2,), (3,), (4, 5, 6, 7))
LATE = CHUNKS[3]
GROUP = 8
GY = 16
BUFFERS = 6
OUT_BUFFERS = 4

gravity = 9.81
step_time = 0.25
spacing = 2.0
min_depth = 0.15
PULL = gravity * step_time / spacing
RUB = gravity * step_time * 0.5
GAIN = step_time / spacing
UNIT_H = 2.0 / (GAIN * PULL)
UNIT_Q = UNIT_H / GAIN
FLOOR = 2.0 * min_depth / UNIT_H
DRAG = RUB * UNIT_Q * (0.5 * UNIT_H) ** (-7.0 / 3.0)

f32 = jnp.float32
bf16 = jnp.bfloat16
i32 = jnp.int32


def flux(flow, h_lo, h_hi, slope, rub):
    depth_face = jnp.maximum(0.5 * (h_lo + h_hi), min_depth)
    drive = flow - (PULL * depth_face) * ((h_hi - h_lo) + slope)
    loss = jnp.exp2(jnp.log2(depth_face) * (-7.0 / 3.0))
    return drive / (1.0 + (rub * jnp.abs(flow)) * loss)


def unit_flux(flow, h_lo, h_hi, slope, rub):
    depth_sum = jnp.maximum(h_lo + h_hi, FLOOR)
    drive = flow - depth_sum * ((h_hi - h_lo) + slope)
    loss = jnp.exp2(jnp.log2(depth_sum) * (-7.0 / 3.0))
    return drive / (1.0 + (rub * jnp.abs(flow)) * loss)


def iota(shape, dim):
    return lax.broadcasted_iota(i32, shape, dim)


def route(onehot, rows):
    a = rows.astype(bf16)
    rest = rows - a.astype(f32)
    b = rest.astype(bf16)
    c = (rest - b.astype(f32)).astype(bf16)
    take = onehot.astype(bf16)

    def part(x):
        return jnp.dot(take, x, preferred_element_type=f32)

    return part(a) + part(b) + part(c)


def side_links(nb_ref, base, side):
    square = (SLOTS, SLOTS)
    rows = iota(square, 0)
    cols = iota(square, 1)
    link_row = jnp.broadcast_to(nb_ref[side : side + 1, :].astype(f32), square)
    diagonal = rows == cols

    def column(x):
        return jnp.broadcast_to(jnp.sum(jnp.where(diagonal, x, 0.0), 1, keepdims=True), square)

    first = base.astype(f32)

    def remote(link):
        return jnp.where((link >= 0.0) & ((link < first) | (link >= first + SLOTS)), 1.0, 0.0)

    link_b = column(link_row)
    missing = link_b[:, :1] < 0.0
    far_b = remote(link_b)
    far = far_b[:, :1]
    far_row = remote(link_row)
    near = jnp.where(link_b - first == cols.astype(f32), 1.0, 0.0)
    rank = jnp.sum(jnp.where(link_row < link_b, far_row, 0.0), 1, keepdims=True)
    order_row = jnp.sum(jnp.where(rows < cols, far_b, 0.0), 0, keepdims=True)
    far_row = far_row[:1]
    place = jnp.where(
        (jnp.broadcast_to(rank, (SLOTS, MOVERS)) == iota((SLOTS, MOVERS), 1).astype(f32))
        & (jnp.broadcast_to(far, (SLOTS, MOVERS)) > 0.0),
        1.0,
        0.0,
    )
    pick = jnp.where(
        (jnp.broadcast_to(order_row, (MOVERS, SLOTS)) == iota((MOVERS, SLOTS), 0).astype(f32))
        & (jnp.broadcast_to(far_row, (MOVERS, SLOTS)) > 0.0),
        1.0,
        0.0,
    )
    exists = jnp.where(missing, 0.0, 1.0)
    return near, place, pick, exists


def halo_of(links, rows, message):
    near, place, _, _ = links
    return route(near, rows) + route(place, message)


def extract_kernel(
    moves, base, depth, discharge, bed, friction, frames, out_0, out_1, early_0, early_1,
    depth_v, flow_v, bed_v, rough_v, acc, turned, load_sem, sem,
):
    lane = iota((TILE, TILE), 1)
    groups = SLOTS // GROUP
    loads = []
    for g in range(groups):
        one = pl.ds(g * GROUP * TILE, GROUP * TILE)
        two = pl.ds(g * GROUP * 2 * TILE, GROUP * 2 * TILE)
        pairs = ((depth, depth_v, one), (discharge, flow_v, two), (bed, bed_v, one), (friction, rough_v, one))
        copies = [pltpu.make_async_copy(a.at[r], b.at[r], load_sem.at[g, i]) for i, (a, b, r) in enumerate(pairs)]
        for c in copies:
            c.start()
        loads.append(copies)
    start_chunk(EARLY, moves, base, (depth, discharge, bed, friction), early_0, early_1, sem)

    def strip(f, k):
        return pl.ds((f * STRIPS + k) * TILE, TILE)

    sources = ((depth_v, 0, 1), (flow_v, 0, 2), (flow_v, 1, 2), (bed_v, 0, 1), (rough_v, 0, 1))
    for g in range(groups):
        for c in loads[g]:
            c.wait()
        home = pl.ds(g * GROUP, GROUP)
        for f, (ref, part, parts) in enumerate(sources):
            top = (g * GROUP * parts + part) * TILE
            for k in range(STRIPS):
                row = k if k < DEPTH else TILE - STRIPS + k
                frames[home, strip(f, k)] = ref[pl.ds(top + row, GROUP, stride=parts * TILE), :]
            half = g * GROUP * STRIPS // TILE
            packed = acc[half, f] if g * GROUP * STRIPS % TILE else None
            for t in range(GROUP):
                tile = ref[pl.ds(top + t * parts * TILE, TILE), :]
                at = (g * GROUP + t) * STRIPS % TILE
                turn = pltpu.roll(tile, (at + DEPTH) % TILE, 1)
                packed = turn if packed is None else jnp.where(lane >= at, turn, packed)
            acc[half, f] = packed

    per = TILE // STRIPS
    for f in range(5):
        to = (0, 2, 1, 3, 4)[f]
        for half in range(SLOTS // per):
            turned[half] = acc[half, f].T
            for k in range(STRIPS):
                frames[pl.ds(SLOTS + half * per, per), strip(to, k)] = turned[
                    half, pl.ds((k + DEPTH) % STRIPS, per, stride=STRIPS), :
                ]
    shape = (2 * MOVERS, SLOTS)
    pick = jnp.zeros(shape, f32)
    for m in range(MOVERS):
        for pairing in range(2):
            leaver = moves[way_of(base, pairing), 0, m] - base[0]
            spot = (iota(shape, 0) == pairing * MOVERS + m) & (iota(shape, 1) == leaver)
            pick = jnp.where(spot, 1.0, pick)
    for axis in range(2):
        for c in range(5):
            got = route(pick, frames[pl.ds(axis * SLOTS, SLOTS), pl.ds(c * FIELD, FIELD)])
            to = pl.ds((axis * 5 + c) * FIELD, FIELD)
            out_0[:, to] = got[:MOVERS]
            out_1[:, to] = got[MOVERS:]
    finish_chunk(EARLY, early_0, early_1, sem)


def start_chunk(entries, moves, base, tiles, out_0, out_1, sem):
    depth, discharge, bed, friction = tiles
    for pairing, out in enumerate((out_0, out_1)):
        way = way_of(base, pairing)
        for i, m in enumerate(entries):
            slot = jnp.clip(moves[way, 0, m] - base[0], 0, SLOTS - 1)
            at = i * STATE
            one = pl.ds(pl.multiple_of(slot * TILE, TILE), TILE)
            two = pl.ds(pl.multiple_of(slot * (2 * TILE), TILE), 2 * TILE)
            pltpu.make_async_copy(depth.at[one], out.at[pl.ds(at, TILE)], sem.at[pairing]).start()
            pltpu.make_async_copy(discharge.at[two], out.at[pl.ds(at + TILE, 2 * TILE)], sem.at[pairing]).start()
            pltpu.make_async_copy(bed.at[one], out.at[pl.ds(at + 3 * TILE, TILE)], sem.at[pairing]).start()
            pltpu.make_async_copy(friction.at[one], out.at[pl.ds(at + 4 * TILE, TILE)], sem.at[pairing]).start()


def finish_chunk(entries, out_0, out_1, sem):
    if not entries:
        return
    body = pl.ds(0, len(entries) * STATE)
    for pairing, out in enumerate((out_0, out_1)):
        pltpu.make_async_copy(out.at[body], out.at[body], sem.at[pairing]).wait()


def is_odd(base, axis):
    return ((base[0] // (SLOTS * (GY if axis == 0 else 1))) % 2) == 1


def way_of(base, pairing):
    odd = (base[0] // SLOTS) % 2
    return odd if pairing else 1 - odd


def swap(odd, a, b):
    return jnp.where(odd, b, a), jnp.where(odd, a, b)


def settle_kernel(
    moves, base, nb, frames, from_0, from_1, depth, discharge, bed, friction,
    dyn, fixed, x_0, x_1, y_0, y_1, chunk_0, chunk_1, sem,
):
    start_chunk(CHUNKS[0], moves, base, (depth, discharge, bed, friction), chunk_0, chunk_1, sem)
    shape = (SLOTS, 2 * MOVERS)
    land = jnp.zeros(shape, f32)
    left = jnp.zeros((SLOTS, TILE), f32)
    for m in range(MOVERS):
        for pairing in range(2):
            way = way_of(base, pairing)
            lander = moves[way, 1, m] - base[0]
            leaver = moves[way, 0, m] - base[0]
            spot = (iota(shape, 0) == lander) & (iota(shape, 1) == pairing * MOVERS + m)
            land = jnp.where(spot, 1.0, land)
            row = iota((SLOTS, TILE), 0)
            left = jnp.where((row == leaver) | (row == lander), 1.0, left)
    for axis in range(2):
        home = pl.ds(axis * SLOTS, SLOTS)
        for f in range(5):
            part = pl.ds(f * FIELD, FIELD)
            came = pl.ds((axis * 5 + f) * FIELD, FIELD)
            fresh = route(land, jnp.concatenate([from_0[:, came], from_1[:, came]], 0))
            for k in range(STRIPS):
                sub = pl.ds(f * FIELD + k * TILE, TILE)
                value = jnp.where(left > 0.0, 0.0, frames[home, sub]) + fresh[:, k * TILE : (k + 1) * TILE]
                if f < 3:
                    dyn[home, sub] = value
                else:
                    fixed[home, pl.ds((f - 3) * FIELD + k * TILE, TILE)] = value

    def edge(ref, axis, f, k):
        return ref[pl.ds(axis * SLOTS, SLOTS), pl.ds(f * FIELD + k * TILE, TILE)]

    last = STRIPS - 1
    blank = jnp.zeros((MOVERS, TILE), f32)
    for axis in range(2):
        lower = side_links(nb, base[0], 2 * axis)
        higher = side_links(nb, base[0], 2 * axis + 1)
        ups = (edge(dyn, axis, 0, last), edge(fixed, axis, 0, last), edge(fixed, axis, 1, last), edge(dyn, axis, 1, last))
        downs = (edge(dyn, axis, 0, 0), edge(fixed, axis, 0, 0), edge(fixed, axis, 1, 0))
        for f in range(4):
            up = route(higher[2], ups[f])
            down = route(lower[2], downs[f]) if f < 3 else blank
            up, down = swap(is_odd(base, axis), up, down)
            if axis == 0:
                x_0[pl.ds(f * MOVERS, MOVERS), :] = up
                x_1[pl.ds(f * MOVERS, MOVERS), :] = down
            else:
                y_0[pl.ds(f * MOVERS, MOVERS), :] = up
                y_1[pl.ds(f * MOVERS, MOVERS), :] = down
    finish_chunk(CHUNKS[0], chunk_0, chunk_1, sem)


def other_axis(x):
    return jnp.concatenate([x[SLOTS:], x[:SLOTS]], 0)


def gather_halos(nb, base_ref, dyn, fixed, messages, first):
    last = STRIPS - 1
    out = {}
    parts = {name: [] for name in ("h_lo", "h_hi", "z_lo", "n_lo", "q_lo", "z_hi", "n_hi", "lo", "hi")}
    picks = []
    for axis in range(2):
        home = pl.ds(axis * SLOTS, SLOTS)
        lower = side_links(nb, base_ref[0], 2 * axis)
        higher = side_links(nb, base_ref[0], 2 * axis + 1)
        picks.append((lower[2], higher[2]))

        def message(f):
            rows = pl.ds(f * MOVERS, MOVERS)
            pair = messages[axis]
            from_higher, from_lower = swap(is_odd(base_ref, axis), pair[0][rows, :], pair[1][rows, :])
            return from_lower, from_higher

        def strip(ref, f, k):
            return ref[home, pl.ds(f * FIELD + k * TILE, TILE)]

        def low(f, rows):
            return halo_of(lower, rows, message(f)[0])

        def high(f, rows):
            return halo_of(higher, rows, message(f)[1])

        parts["h_lo"].append(low(0, strip(dyn, 0, last)))
        parts["h_hi"].append(high(0, strip(dyn, 0, 0)))
        if first:
            parts["z_lo"].append(low(1, strip(fixed, 0, last)))
            parts["n_lo"].append(low(2, strip(fixed, 1, last)))
            parts["q_lo"].append(low(3, strip(dyn, 1, last)))
            parts["z_hi"].append(high(1, strip(fixed, 0, 0)))
            parts["n_hi"].append(high(2, strip(fixed, 1, 0)))
        parts["lo"].append(jnp.broadcast_to(lower[3], (SLOTS, TILE)))
        parts["hi"].append(jnp.broadcast_to(higher[3], (SLOTS, TILE)))
    for name, pieces in parts.items():
        if pieces:
            out[name] = jnp.concatenate(pieces, 0)
    return out, picks


def step_kernel(turn, moves, base, nb, dyn, fixed, *rest):
    first = turn == 0
    if first:
        still = None
        (x0, x1, y0, y1), rest = rest[:4], rest[4:]
    else:
        still = rest[0]
        (x0, x1, y0, y1), rest = rest[1:5], rest[5:]
    depth, discharge, bed, friction = rest[:4]
    tiles = (depth, discharge, bed, friction)
    dyn_out, still_out, trail, x_0, x_1, y_0, y_1, chunk_0, chunk_1, sem = rest[4:]
    start_chunk(CHUNKS[turn + 1], moves, base, tiles, chunk_0, chunk_1, sem)
    halo, picks = gather_halos(nb, base, dyn, fixed, ((x0, x1), (y0, y1)), first)
    names = ("z_lo", "n_lo", "z_hi", "n_hi", "q_lo")
    if not first:
        for j, name in enumerate(names):
            halo[name] = still[:, pl.ds(j * TILE, TILE)]

    def get(ref, f, k):
        return ref[:, pl.ds(f * FIELD + k * TILE, TILE)]

    last = STRIPS - 1
    h = [get(dyn, 0, k) for k in range(STRIPS)]
    z = [get(fixed, 0, k) for k in range(STRIPS)]
    n = [get(fixed, 1, k) for k in range(STRIPS)]
    low_face = flux(halo["q_lo"], halo["h_lo"], h[0], z[0] - halo["z_lo"], RUB * (halo["n_lo"] + n[0]))
    low_face = jnp.where(halo["lo"] > 0.0, low_face, 0.0)
    high_face = flux(get(dyn, 1, last), h[last], halo["h_hi"], halo["z_hi"] - z[last], RUB * (n[last] + halo["n_hi"]))
    high_face = jnp.where(halo["hi"] > 0.0, high_face, 0.0)
    for j, name in enumerate(names[:4]):
        still_out[:, pl.ds(j * TILE, TILE)] = halo[name]
    still_out[:, pl.ds(4 * TILE, TILE)] = low_face
    trail[:, pl.ds(0, TILE)] = low_face
    trail[:, pl.ds(TILE, TILE)] = halo["h_hi"]

    lane = iota((2 * SLOTS, TILE), 1)
    side_h = other_axis(halo["h_hi"])
    side_z = other_axis(halo["z_hi"])
    side_n = other_axis(halo["n_hi"])
    side_wall = other_axis(halo["hi"]) <= 0.0
    side_in = other_axis(low_face)

    def cell(x, k):
        at = k if k < DEPTH else TILE - STRIPS + k
        return jnp.broadcast_to(x[:, at : at + 1], x.shape)

    def ahead(x, k, side):
        return jnp.where(lane == TILE - 1, cell(side, k), pltpu.roll(x, TILE - 1, 1))

    reach = DEPTH - 1 - turn
    low_keep = list(range(reach))
    high_keep = list(range(STRIPS - reach, STRIPS))
    face = {-1: low_face, last: high_face}
    for k in low_keep + [x - 1 for x in high_keep]:
        face[k] = flux(get(dyn, 1, k), h[k], h[k + 1], z[k + 1] - z[k], RUB * (n[k] + n[k + 1]))
    new = {}
    for k in low_keep + high_keep:
        side = flux(
            get(dyn, 2, k), h[k], ahead(h[k], k, side_h), ahead(z[k], k, side_z) - z[k],
            RUB * (n[k] + ahead(n[k], k, side_n)),
        )
        side = jnp.where((lane == TILE - 1) & side_wall, 0.0, side)
        before = jnp.where(lane == 0, cell(side_in, k), pltpu.roll(side, 1, 1))
        new[k] = h[k] + GAIN * ((face[k - 1] - face[k]) + (before - side))
        dyn_out[:, pl.ds(2 * FIELD + k * TILE, TILE)] = side
    blank = jnp.zeros((2 * SLOTS, TILE), f32)
    for k in range(STRIPS):
        dyn_out[:, pl.ds(k * TILE, TILE)] = new[k] if k in new else blank
        dyn_out[:, pl.ds(FIELD + k * TILE, TILE)] = face[k] if k in face else blank
        if k not in new:
            dyn_out[:, pl.ds(2 * FIELD + k * TILE, TILE)] = blank
    for axis in range(2):
        home = slice(axis * SLOTS, (axis + 1) * SLOTS)
        up = route(picks[axis][1], new[last][home])
        down = route(picks[axis][0], new[0][home])
        up, down = swap(is_odd(base, axis), up, down)
        if axis == 0:
            x_0[...] = up
            x_1[...] = down
        else:
            y_0[...] = up
            y_1[...] = down
    finish_chunk(CHUNKS[turn + 1], chunk_0, chunk_1, sem)


def run_tiles(
    queue, origin, count, moves_sources, tiles, nb_s, edges, columns, outs, before_loop,
    inbox, outbox, in_sem, out_sem, *spaces,
):
    depth, discharge, bed, friction = tiles
    depth_out, flow_out = outs

    def fetch(j):
        t = queue[j]
        buf = j % BUFFERS
        sem = in_sem.at[buf]
        box = inbox.at[buf]
        kind = origin[t]

        if depth is not None:

            @pl.when(kind == 0)
            def _():
                one = pl.ds(pl.multiple_of(t * TILE, TILE), TILE)
                two = pl.ds(pl.multiple_of(t * (2 * TILE), TILE), 2 * TILE)
                pltpu.make_async_copy(depth.at[one], box.at[pl.ds(0, TILE)], sem).start()
                pltpu.make_async_copy(discharge.at[two], box.at[pl.ds(TILE, 2 * TILE)], sem).start()
                pltpu.make_async_copy(bed.at[one], box.at[pl.ds(3 * TILE, TILE)], sem).start()
                pltpu.make_async_copy(friction.at[one], box.at[pl.ds(4 * TILE, TILE)], sem).start()

        for code, ref, at in moves_sources:

            @pl.when(kind == code)
            def _():
                pltpu.make_async_copy(ref.at[pl.ds(at, STATE)], box, sem).start()

    def arrived(buf):
        box = inbox.at[buf]
        pltpu.make_async_copy(box, box, in_sem.at[buf]).wait()

    def send(t, buf):
        box = outbox.at[buf]
        one = pl.ds(pl.multiple_of(t * TILE, TILE), TILE)
        two = pl.ds(pl.multiple_of(t * (2 * TILE), TILE), 2 * TILE)
        pltpu.make_async_copy(box.at[pl.ds(0, TILE)], depth_out.at[one], out_sem.at[buf]).start()
        pltpu.make_async_copy(box.at[pl.ds(TILE, 2 * TILE)], flow_out.at[two], out_sem.at[buf]).start()

    def sent(buf):
        box = outbox.at[buf]
        pltpu.make_async_copy(box, box, out_sem.at[buf]).wait()

    def prime():
        for j in range(BUFFERS - 2):

            @pl.when(j < count)
            def _():
                fetch(j)

    prime()
    before_loop()
    part_rows = 16
    parts = TILE // part_rows
    lane = iota((part_rows, TILE), 1)
    row = iota((part_rows, TILE), 0)
    at_first = lane == 0
    at_last = lane == TILE - 1
    bottom = row == part_rows - 1

    def ready(j):
        @pl.when(j < count)
        def _():
            arrived(j % BUFFERS)

        @pl.when((j >= OUT_BUFFERS) & (j < count))
        def _():
            sent(j % OUT_BUFFERS)

    def work(j, space):
        water, stream_x, stream_y, slope_x, slope_y, rub_x, rub_y = space
        t = queue[jnp.minimum(j, count - 1)]
        box = inbox.at[j % BUFFERS]
        out = outbox.at[j % OUT_BUFFERS]
        wall_x = nb_s[1, t] < 0
        wall_y = nb_s[3, t] < 0

        def edge_row(e):
            return edges[e, pl.ds(t, 1), :]

        z_next = edge_row(8)
        n_next = edge_row(9)
        for p in range(parts):
            rows = pl.ds(p * part_rows, part_rows)
            zr = pl.ds(3 * TILE + p * part_rows, part_rows)
            nr = pl.ds(4 * TILE + p * part_rows, part_rows)
            z = box[zr, :] * (1.0 / UNIT_H)
            n = box[nr, :]
            if p < parts - 1:
                z_dn = box[pl.ds(3 * TILE + p * part_rows + 1, part_rows), :] * (1.0 / UNIT_H)
                n_dn = box[pl.ds(4 * TILE + p * part_rows + 1, part_rows), :]
            else:
                z_dn = jnp.where(bottom, z_next, pltpu.roll(z, part_rows - 1, 0))
                n_dn = jnp.where(bottom, n_next, pltpu.roll(n, part_rows - 1, 0))
            side = columns[2, rows, :]
            z_rt = jnp.where(at_last, pltpu.roll(side, TILE - 1 - t, 1), pltpu.roll(z, TILE - 1, 1))
            n_rt = jnp.where(at_last, pltpu.roll(side, TILE - 1 - SLOTS - t, 1), pltpu.roll(n, TILE - 1, 1))
            slope_x[rows, :] = z_dn - z
            slope_y[rows, :] = z_rt - z
            rub_x[rows, :] = DRAG * (n + n_dn)
            rub_y[rows, :] = DRAG * (n + n_rt)
            water[rows, :] = box[rows, :] * (1.0 / UNIT_H)
        for s in range(4):
            water[pl.ds(TILE, 1), :] = edge_row(4 + s)
            stream_x[pl.ds(7, 1), :] = edge_row(s)
            for p in range(parts):
                rows = pl.ds(p * part_rows, part_rows)
                h = water[rows, :]
                h_dn = water[pl.ds(p * part_rows + 1, part_rows), :]
                side = pltpu.roll(columns[s // 2, rows, :], TILE - 1 - 64 * (s % 2) - 2 * t, 1)
                h_rt = jnp.where(at_last, side, pltpu.roll(h, TILE - 1, 1))
                if s == 0:
                    flow_x = box[pl.ds(TILE + p * part_rows, part_rows), :] * (1.0 / UNIT_Q)
                    flow_y = box[pl.ds(2 * TILE + p * part_rows, part_rows), :] * (1.0 / UNIT_Q)
                else:
                    flow_x = stream_x[pl.ds(8 + p * part_rows, part_rows), :]
                    flow_y = stream_y[rows, :]
                new_x = unit_flux(flow_x, h, h_dn, slope_x[rows, :], rub_x[rows, :])
                if p == parts - 1:
                    new_x = jnp.where(bottom & wall_x, 0.0, new_x)
                new_y = unit_flux(flow_y, h, h_rt, slope_y[rows, :], rub_y[rows, :])
                new_y = jnp.where(at_last & wall_y, 0.0, new_y)
                if s < 3:
                    stream_y[rows, :] = new_y
                else:
                    out[pl.ds(TILE + p * part_rows, part_rows), :] = new_x * UNIT_Q
                    out[pl.ds(2 * TILE + p * part_rows, part_rows), :] = new_y * UNIT_Q
                in_y = jnp.where(at_first, side, pltpu.roll(new_y, 1, 1))
                stream_x[pl.ds(8 + p * part_rows, part_rows), :] = new_x
                in_x = stream_x[pl.ds(7 + p * part_rows, part_rows), :]
                h_new = h + ((in_x - new_x) + (in_y - new_y))
                if s < 3:
                    water[rows, :] = h_new
                else:
                    out[rows, :] = h_new * UNIT_H

    def two_tiles(pair, carry):
        for i in range(2):
            j = 2 * pair + i

            @pl.when(j + BUFFERS - 2 < count)
            def _():
                fetch(j + BUFFERS - 2)

            ready(j)
        half = len(spaces) // 2
        for i in range(2):
            work(2 * pair + i, spaces[i * half : (i + 1) * half])
        for i in range(2):
            j = 2 * pair + i

            @pl.when(j < count)
            def _():
                send(queue[j], j % OUT_BUFFERS)

        return carry

    lax.fori_loop(0, (count + 1) // 2, two_tiles, 0)
    for b in range(OUT_BUFFERS):

        @pl.when(b < count)
        def _():
            sent(b)


def chunk_sources(entries, *chunks):
    found = []
    for pairing, ref in enumerate(chunks):
        for i, m in enumerate(entries):
            found.append((1 + pairing * MOVERS + m, ref, i * STATE))
    return found


def note_arrivals(entries, moves, base, visit):
    for m in entries:
        for pairing in range(2):
            lander = moves[way_of(base, pairing), 1, m]

            @pl.when(lander >= 0)
            def _():
                visit(lander - base[0], 1 + pairing * MOVERS + m)


def tile_kernel(
    moves, base, ids, nb_s, nb, dyn, fixed, still, x_0, x_1, y_0, y_1, t0, t1, t2,
    early_0, early_1, a_0, a_1, b_0, b_1, c_0, c_1, depth, discharge, bed, friction,
    depth_out, flow_out, edges, columns,
    zeros, turned, queue, origin, zero_sem, *scratch,
):
    def clear(t, total):
        origin[t] = 0
        return total + jnp.where(ids[t] >= 0, 1, 0)

    live = lax.fori_loop(0, SLOTS, clear, 0)

    def mark(t, code):
        origin[t] = code

    note_arrivals(EARLY + CHUNKS[0] + CHUNKS[1] + CHUNKS[2], moves, base, mark)
    note_arrivals(LATE, moves, base, lambda t, code: mark(t, -1))

    def enqueue(t, size):
        keep = origin[t] >= 0
        queue[size] = t
        return size + jnp.where(keep, 1, 0)

    count = lax.fori_loop(0, live, enqueue, 0)
    zeros[...] = jnp.zeros(zeros.shape, f32)

    def blank(t, carry):
        one = pl.ds(pl.multiple_of(t * TILE, TILE), TILE)
        two = pl.ds(pl.multiple_of(t * (2 * TILE), TILE), 2 * TILE)
        pltpu.make_async_copy(zeros.at[pl.ds(0, TILE)], depth_out.at[one], zero_sem).start()
        pltpu.make_async_copy(zeros.at[pl.ds(TILE, 2 * TILE)], flow_out.at[two], zero_sem).start()
        return carry

    def before_loop():
        lax.fori_loop(live, SLOTS, blank, 0)
        halo, _ = gather_halos(nb, base, dyn, fixed, ((x_0, x_1), (y_0, y_1)), False)

        def kept(j):
            return still[:, pl.ds(j * TILE, TILE)]

        n_first = fixed[:, pl.ds(FIELD, TILE)]
        z_first = fixed[:, pl.ds(0, TILE)]
        low_face = flux(
            kept(4), halo["h_lo"], dyn[:, pl.ds(0, TILE)], z_first - kept(0), RUB * (kept(1) + n_first)
        )
        low_face = jnp.where(halo["lo"] > 0.0, low_face, 0.0)
        trails = [(t[:, pl.ds(0, TILE)], t[:, pl.ds(TILE, TILE)]) for t in (t0, t1, t2)]
        trails.append((low_face, halo["h_hi"]))
        for s, (inflow, ahead_h) in enumerate(trails):
            inflow = inflow * (1.0 / UNIT_Q)
            ahead_h = ahead_h * (1.0 / UNIT_H)
            edges[s] = inflow[:SLOTS]
            edges[4 + s] = ahead_h[:SLOTS]
            turned[pl.ds(64 * (s % 2), SLOTS, stride=2), :] = ahead_h[SLOTS:]
            turned[pl.ds(64 * (s % 2) + 1, SLOTS, stride=2), :] = inflow[SLOTS:]
            if s % 2:
                columns[s // 2] = turned[...].T
        z_ahead = kept(2) * (1.0 / UNIT_H)
        edges[8] = z_ahead[:SLOTS]
        edges[9] = kept(3)[:SLOTS]
        turned[pl.ds(0, SLOTS), :] = z_ahead[SLOTS:]
        turned[pl.ds(SLOTS, SLOTS), :] = kept(3)[SLOTS:]
        columns[2] = turned[...].T

    sources = chunk_sources(EARLY, early_0, early_1)
    for entries, *chunks in zip(CHUNKS, (a_0, b_0, c_0), (a_1, b_1, c_1)):
        sources += chunk_sources(entries, *chunks)
    run_tiles(
        queue, origin, count, sources, (depth, discharge, bed, friction), nb_s, edges, columns,
        (depth_out, flow_out), before_loop, *scratch,
    )

    def blanked(t, carry):
        pltpu.make_async_copy(zeros, zeros, zero_sem).wait()
        return carry

    lax.fori_loop(live, SLOTS, blanked, 0)


def late_kernel(
    moves, base, nb_s, edges, columns, late_0, late_1, depth_in, flow_in,
    depth_out, flow_out, queue, origin, size, *scratch,
):
    size[0] = 0

    def enqueue(t, code):
        queue[size[0]] = t
        origin[t] = code
        size[0] = size[0] + 1

    note_arrivals(LATE, moves, base, enqueue)
    run_tiles(
        queue, origin, size[0], chunk_sources(LATE, late_0, late_1), (None,) * 4, nb_s, edges, columns,
        (depth_out, flow_out), lambda: None, *scratch,
    )


SMEM = pl.BlockSpec(memory_space=pltpu.SMEM)
VMEM = pl.BlockSpec(memory_space=pltpu.VMEM)
HBM = pl.BlockSpec(memory_space=pltpu.HBM)


def trade(block, axis, pairing):
    size = lax.axis_size(axis)
    pairs = [(i, (((i + pairing) ^ 1) - pairing) % size) for i in range(size)]
    return lax.ppermute(block, axis, pairs)


def trade_both(block_0, block_1, axis):
    got_1 = trade(block_1, axis, 1)
    got_0 = trade(block_0, axis, 0)
    return got_0, got_1


def exchange(x_0, x_1, y_0, y_1):
    got_x = trade_both(x_0, x_1, "gx")
    got_y = trade_both(y_0, y_1, "gy")
    return *got_x, *got_y


def held(*shape):
    return pltpu.VMEM(shape, f32)


def on_core(*arrays):
    return [pltpu.with_memory_space_constraint(a, pltpu.VMEM) for a in arrays]


def call(kernel, **settings):
    return pl.pallas_call(kernel, **settings)


def struct(*shape):
    return jax.ShapeDtypeStruct(shape, f32)


def loop_scratch():
    space = [
        pltpu.VMEM((TILE + 8, TILE), f32),
        pltpu.VMEM((TILE + 8, TILE), f32),
        *[pltpu.VMEM((TILE, TILE), f32)] * 5,
    ]
    return [
        pltpu.VMEM((BUFFERS, STATE, TILE), f32),
        pltpu.VMEM((OUT_BUFFERS, 3 * TILE, TILE), f32),
        pltpu.SemaphoreType.DMA((BUFFERS,)),
        pltpu.SemaphoreType.DMA((OUT_BUFFERS,)),
        *space,
        *space,
    ]


def shards(depth, discharge, bed, friction, tile_ids, neighbors, moves):
    base = (lax.axis_index(("gx", "gy")) * SLOTS).astype(i32).reshape(1)
    plan = moves[0].transpose(0, 2, 1)
    nb = neighbors.T
    tiles = [
        pltpu.with_memory_space_constraint(a, pltpu.HBM)
        for a in (
            depth.reshape(SLOTS * TILE, TILE),
            discharge.reshape(SLOTS * 2 * TILE, TILE),
            bed.reshape(SLOTS * TILE, TILE),
            friction.reshape(SLOTS * TILE, TILE),
        )
    ]
    early_rows = len(EARLY) * STATE
    frames, up, down, early_0, early_1 = pl.pallas_call(
        extract_kernel,
        in_specs=[SMEM, SMEM] + [HBM] * 4,
        out_specs=[VMEM] * 5,
        out_shape=[
            held(2 * SLOTS, 5 * FIELD),
            held(MOVERS, 10 * FIELD),
            held(MOVERS, 10 * FIELD),
            held(early_rows, TILE),
            held(early_rows, TILE),
        ],
        scratch_shapes=[
            pltpu.VMEM((SLOTS * TILE, TILE), f32),
            pltpu.VMEM((SLOTS * 2 * TILE, TILE), f32),
            pltpu.VMEM((SLOTS * TILE, TILE), f32),
            pltpu.VMEM((SLOTS * TILE, TILE), f32),
            pltpu.VMEM((2, 5, TILE, TILE), f32),
            pltpu.VMEM((2, TILE, TILE), f32),
            pltpu.SemaphoreType.DMA((SLOTS // GROUP, 4)),
            pltpu.SemaphoreType.DMA((2,)),
        ],
        compiler_params=pltpu.CompilerParams(vmem_limit_bytes=20 * 2**20),
        name="extract",
    )(plan, base, *tiles)
    from_0, from_1 = trade_both(up, down, "gy")
    early_0, early_1 = trade_both(early_0, early_1, "gy")

    first_rows = 4 * MOVERS
    dyn, fixed, *sends = call(
        settle_kernel,
        in_specs=[SMEM, SMEM] + [VMEM] * 4 + [HBM] * 4,
        out_specs=[VMEM] * 8,
        out_shape=[
            held(2 * SLOTS, 3 * FIELD),
            held(2 * SLOTS, 2 * FIELD),
            held(first_rows, TILE),
            held(first_rows, TILE),
            held(first_rows, TILE),
            held(first_rows, TILE),
            *[held(len(CHUNKS[0]) * STATE, TILE)] * 2,
        ],
        scratch_shapes=[pltpu.SemaphoreType.DMA((2,))],
        compiler_params=pltpu.CompilerParams(vmem_limit_bytes=12 * 2**20),
    )(plan, base, *on_core(nb, frames, from_0, from_1), *tiles)
    got = exchange(*sends[:4])
    chunks = [trade_both(*sends[4:], "gy")]
    still = []
    trails = []
    for turn in range(3):

        def body(*refs, turn=turn):
            step_kernel(turn, *refs)

        shapes = [
            (2 * SLOTS, 3 * FIELD),
            (2 * SLOTS, 5 * TILE),
            (2 * SLOTS, 2 * TILE),
            (MOVERS, TILE),
            (MOVERS, TILE),
            (MOVERS, TILE),
            (MOVERS, TILE),
            *[(len(CHUNKS[turn + 1]) * STATE, TILE)] * 2,
        ]
        dyn, kept, trail, *sends = call(
            body,
            in_specs=[SMEM, SMEM] + [VMEM] * (7 + len(still)) + [HBM] * 4,
            out_specs=[VMEM] * len(shapes),
            out_shape=[held(*s) for s in shapes],
            scratch_shapes=[pltpu.SemaphoreType.DMA((2,))],
            compiler_params=pltpu.CompilerParams(vmem_limit_bytes=12 * 2**20),
        )(plan, base, *on_core(nb, dyn, fixed, *still, *got), *tiles)
        still = [kept]
        trails.append(trail)
        got = exchange(*sends[:4])
        chunks.append(trade_both(*sends[4:], "gy"))

    late_0, late_1 = chunks[3]
    kept_inputs = on_core(
        nb, dyn, fixed, *still, *got, *trails, early_0, early_1, *chunks[0], *chunks[1], *chunks[2]
    )
    new_depth, new_flow, edges, columns = call(
        tile_kernel,
        in_specs=[SMEM] * 4 + [VMEM] * len(kept_inputs) + [HBM] * 4,
        out_specs=[HBM, HBM, VMEM, VMEM],
        out_shape=[
            struct(SLOTS * TILE, TILE),
            struct(SLOTS * 2 * TILE, TILE),
            held(10, SLOTS, TILE),
            held(3, TILE, TILE),
        ],
        scratch_shapes=[
            pltpu.VMEM((3 * TILE, TILE), f32),
            pltpu.VMEM((TILE, TILE), f32),
            pltpu.SMEM((SLOTS,), i32),
            pltpu.SMEM((SLOTS,), i32),
            pltpu.SemaphoreType.DMA,
            *loop_scratch(),
        ],
        compiler_params=pltpu.CompilerParams(vmem_limit_bytes=12 * 2**20),
    )(plan, base, tile_ids, nb, *kept_inputs, *tiles)
    new_depth, new_flow = pl.pallas_call(
        late_kernel,
        in_specs=[SMEM] * 3 + [VMEM] * 4 + [HBM] * 2,
        out_specs=[HBM, HBM],
        out_shape=[struct(SLOTS * TILE, TILE), struct(SLOTS * 2 * TILE, TILE)],
        input_output_aliases={7: 0, 8: 1},
        scratch_shapes=[
            pltpu.SMEM((SLOTS,), i32),
            pltpu.SMEM((SLOTS,), i32),
            pltpu.SMEM((1,), i32),
            *loop_scratch(),
        ],
        compiler_params=pltpu.CompilerParams(vmem_limit_bytes=12 * 2**20),
        name="late_tiles",
    )(plan, base, nb, *on_core(edges, columns, late_0, late_1), new_depth, new_flow)
    return (
        new_depth.reshape(SLOTS, TILE, TILE),
        new_flow.reshape(SLOTS, 2, TILE, TILE),
    )


def solution(mesh):
    return jax.shard_map(
        shards,
        mesh=mesh,
        in_specs=(
            P(("gx", "gy"), None, None),
            P(("gx", "gy"), None, None, None),
            P(("gx", "gy"), None, None),
            P(("gx", "gy"), None, None),
            P(("gx", "gy")),
            P(("gx", "gy"), None),
            P(("gx", "gy"), None, None, None),
        ),
        out_specs=(P(("gx", "gy"), None, None), P(("gx", "gy"), None, None, None)),
        check_vma=False,
    )
```

```python
import jax
import jax.numpy as jnp
from jax import lax
from jax.experimental import pallas as pl
from jax.experimental.pallas import tpu as pltpu
from jax.sharding import PartitionSpec as P


TILE = 128
SLOTS = 32
MOVERS = 8
DEPTH = 4
STRIPS = 2 * DEPTH
FIELD = STRIPS * TILE
STATE = 5 * TILE
EARLY = (0,)
CHUNKS = ((1,), (2,), (3,), (4, 5, 6, 7))
LATE = CHUNKS[3]
LOADS = (EARLY,) + CHUNKS
GROUP = 8
GY = 16
BUFFERS = 6
OUT_BUFFERS = 4

gravity = 9.81
step_time = 0.25
spacing = 2.0
min_depth = 0.15
PULL = gravity * step_time / spacing
RUB = gravity * step_time * 0.5
GAIN = step_time / spacing
UNIT_H = 2.0 / (GAIN * PULL)
UNIT_Q = UNIT_H / GAIN
FLOOR = 2.0 * min_depth / UNIT_H
DRAG = RUB * UNIT_Q * (0.5 * UNIT_H) ** (-7.0 / 3.0)

f32 = jnp.float32
bf16 = jnp.bfloat16
i32 = jnp.int32


def flux(flow, h_lo, h_hi, slope, rub):
    depth_face = jnp.maximum(0.5 * (h_lo + h_hi), min_depth)
    drive = flow - (PULL * depth_face) * ((h_hi - h_lo) + slope)
    loss = jnp.exp2(jnp.log2(depth_face) * (-7.0 / 3.0))
    return drive / (1.0 + (rub * jnp.abs(flow)) * loss)


def unit_flux(flow, h_lo, h_hi, slope, rub):
    depth_sum = jnp.maximum(h_lo + h_hi, FLOOR)
    drive = flow - depth_sum * ((h_hi - h_lo) + slope)
    loss = jnp.exp2(jnp.log2(depth_sum) * (-7.0 / 3.0))
    return drive / (1.0 + (rub * jnp.abs(flow)) * loss)


def iota(shape, dim):
    return lax.broadcasted_iota(i32, shape, dim)


def route(onehot, rows):
    a = rows.astype(bf16)
    rest = rows - a.astype(f32)
    b = rest.astype(bf16)
    c = (rest - b.astype(f32)).astype(bf16)
    take = onehot.astype(bf16)

    def part(x):
        return jnp.dot(take, x, preferred_element_type=f32)

    return part(a) + part(b) + part(c)


def side_links(nb_ref, base, side):
    square = (SLOTS, SLOTS)
    rows = iota(square, 0)
    cols = iota(square, 1)
    link_row = jnp.broadcast_to(nb_ref[side : side + 1, :].astype(f32), square)
    diagonal = rows == cols

    def column(x):
        return jnp.broadcast_to(jnp.sum(jnp.where(diagonal, x, 0.0), 1, keepdims=True), square)

    first = base.astype(f32)

    def remote(link):
        return jnp.where((link >= 0.0) & ((link < first) | (link >= first + SLOTS)), 1.0, 0.0)

    link_b = column(link_row)
    missing = link_b[:, :1] < 0.0
    far_b = remote(link_b)
    far = far_b[:, :1]
    far_row = remote(link_row)
    near = jnp.where(link_b - first == cols.astype(f32), 1.0, 0.0)
    rank = jnp.sum(jnp.where(link_row < link_b, far_row, 0.0), 1, keepdims=True)
    order_row = jnp.sum(jnp.where(rows < cols, far_b, 0.0), 0, keepdims=True)
    far_row = far_row[:1]
    place = jnp.where(
        (jnp.broadcast_to(rank, (SLOTS, MOVERS)) == iota((SLOTS, MOVERS), 1).astype(f32))
        & (jnp.broadcast_to(far, (SLOTS, MOVERS)) > 0.0),
        1.0,
        0.0,
    )
    pick = jnp.where(
        (jnp.broadcast_to(order_row, (MOVERS, SLOTS)) == iota((MOVERS, SLOTS), 0).astype(f32))
        & (jnp.broadcast_to(far_row, (MOVERS, SLOTS)) > 0.0),
        1.0,
        0.0,
    )
    exists = jnp.where(missing, 0.0, 1.0)
    return near, place, pick, exists


def halo_of(links, rows, message):
    near, place, _, _ = links
    return route(near, rows) + route(place, message)


def extract_kernel(
    depth, discharge, bed, friction, frames, depth_v, flow_v, bed_v, rough_v, acc, turned, load_sem,
):
    lane = iota((TILE, TILE), 1)
    groups = SLOTS // GROUP
    loads = []
    for g in range(groups):
        one = pl.ds(g * GROUP * TILE, GROUP * TILE)
        two = pl.ds(g * GROUP * 2 * TILE, GROUP * 2 * TILE)
        pairs = ((depth, depth_v, one), (discharge, flow_v, two), (bed, bed_v, one), (friction, rough_v, one))
        copies = [pltpu.make_async_copy(a.at[r], b.at[r], load_sem.at[g, i]) for i, (a, b, r) in enumerate(pairs)]
        for c in copies:
            c.start()
        loads.append(copies)

    def strip(f, k):
        return pl.ds((f * STRIPS + k) * TILE, TILE)

    sources = ((depth_v, 0, 1), (flow_v, 0, 2), (flow_v, 1, 2), (bed_v, 0, 1), (rough_v, 0, 1))
    for g in range(groups):
        for c in loads[g]:
            c.wait()
        home = pl.ds(g * GROUP, GROUP)
        for f, (ref, part, parts) in enumerate(sources):
            top = (g * GROUP * parts + part) * TILE
            for k in range(STRIPS):
                row = k if k < DEPTH else TILE - STRIPS + k
                frames[home, strip(f, k)] = ref[pl.ds(top + row, GROUP, stride=parts * TILE), :]
            half = g * GROUP * STRIPS // TILE
            packed = acc[half, f] if g * GROUP * STRIPS % TILE else None
            for t in range(GROUP):
                tile = ref[pl.ds(top + t * parts * TILE, TILE), :]
                at = (g * GROUP + t) * STRIPS % TILE
                turn = pltpu.roll(tile, (at + DEPTH) % TILE, 1)
                packed = turn if packed is None else jnp.where(lane >= at, turn, packed)
            acc[half, f] = packed

    per = TILE // STRIPS
    for f in range(5):
        to = (0, 2, 1, 3, 4)[f]
        for half in range(SLOTS // per):
            turned[half] = acc[half, f].T
            for k in range(STRIPS):
                frames[pl.ds(SLOTS + half * per, per), strip(to, k)] = turned[
                    half, pl.ds((k + DEPTH) % STRIPS, per, stride=STRIPS), :
                ]


def pack_kernel(moves, base, depth, discharge, bed, friction, out_0, out_1, *rest):
    boxes, (acc, turned, sem) = rest[: 2 * len(LOADS)], rest[2 * len(LOADS) :]
    for g, entries in enumerate(LOADS):
        start_chunk(entries, moves, base, (depth, discharge, bed, friction), *boxes[2 * g : 2 * g + 2], sem.at[g])
    lane = iota((TILE, TILE), 1)
    outs = (out_0, out_1)
    for g, entries in enumerate(LOADS):
        finish_chunk(entries, *boxes[2 * g : 2 * g + 2], sem.at[g])
        for i, m in enumerate(entries):
            for pairing in range(2):
                box = boxes[2 * g + pairing]
                at = (2 * m + pairing) * STRIPS
                for f in range(5):
                    top = i * STATE + f * TILE
                    for k in range(STRIPS):
                        row = k if k < DEPTH else TILE - STRIPS + k
                        to = pl.ds((f * STRIPS + k) * TILE, TILE)
                        outs[pairing][pl.ds(m, 1), to] = box[pl.ds(top + row, 1), :]
                    turn = pltpu.roll(box[pl.ds(top, TILE), :], (at + DEPTH) % TILE, 1)
                    acc[f] = turn if at == 0 else jnp.where(lane >= at, turn, acc[f])
    for f in range(5):
        to = 5 * STRIPS + (0, 2, 1, 3, 4)[f] * STRIPS
        turned[...] = acc[f].T
        for pairing in range(2):
            for k in range(STRIPS):
                outs[pairing][:, pl.ds((to + k) * TILE, TILE)] = turned[
                    pl.ds(pairing * STRIPS + (k + DEPTH) % STRIPS, MOVERS, stride=2 * STRIPS), :
                ]


def start_chunk(entries, moves, base, tiles, out_0, out_1, sem):
    depth, discharge, bed, friction = tiles
    for pairing, out in enumerate((out_0, out_1)):
        way = way_of(base, pairing)
        for i, m in enumerate(entries):
            slot = jnp.clip(moves[way, 0, m] - base[0], 0, SLOTS - 1)
            at = i * STATE
            one = pl.ds(pl.multiple_of(slot * TILE, TILE), TILE)
            two = pl.ds(pl.multiple_of(slot * (2 * TILE), TILE), 2 * TILE)
            pltpu.make_async_copy(depth.at[one], out.at[pl.ds(at, TILE)], sem.at[pairing]).start()
            pltpu.make_async_copy(discharge.at[two], out.at[pl.ds(at + TILE, 2 * TILE)], sem.at[pairing]).start()
            pltpu.make_async_copy(bed.at[one], out.at[pl.ds(at + 3 * TILE, TILE)], sem.at[pairing]).start()
            pltpu.make_async_copy(friction.at[one], out.at[pl.ds(at + 4 * TILE, TILE)], sem.at[pairing]).start()


def finish_chunk(entries, out_0, out_1, sem):
    if not entries:
        return
    body = pl.ds(0, len(entries) * STATE)
    for pairing, out in enumerate((out_0, out_1)):
        pltpu.make_async_copy(out.at[body], out.at[body], sem.at[pairing]).wait()


def is_odd(base, axis):
    return ((base[0] // (SLOTS * (GY if axis == 0 else 1))) % 2) == 1


def way_of(base, pairing):
    odd = (base[0] // SLOTS) % 2
    return odd if pairing else 1 - odd


def swap(odd, a, b):
    return jnp.where(odd, b, a), jnp.where(odd, a, b)


def settle_kernel(
    moves, base, nb, frames, from_0, from_1, dyn, fixed, x_0, x_1, y_0, y_1,
):
    shape = (SLOTS, 2 * MOVERS)
    land = jnp.zeros(shape, f32)
    left = jnp.zeros((SLOTS, TILE), f32)
    for m in range(MOVERS):
        for pairing in range(2):
            way = way_of(base, pairing)
            lander = moves[way, 1, m] - base[0]
            leaver = moves[way, 0, m] - base[0]
            spot = (iota(shape, 0) == lander) & (iota(shape, 1) == pairing * MOVERS + m)
            land = jnp.where(spot, 1.0, land)
            row = iota((SLOTS, TILE), 0)
            left = jnp.where((row == leaver) | (row == lander), 1.0, left)
    for axis in range(2):
        home = pl.ds(axis * SLOTS, SLOTS)
        for f in range(5):
            part = pl.ds(f * FIELD, FIELD)
            came = pl.ds((axis * 5 + f) * FIELD, FIELD)
            fresh = route(land, jnp.concatenate([from_0[:, came], from_1[:, came]], 0))
            for k in range(STRIPS):
                sub = pl.ds(f * FIELD + k * TILE, TILE)
                value = jnp.where(left > 0.0, 0.0, frames[home, sub]) + fresh[:, k * TILE : (k + 1) * TILE]
                if f < 3:
                    dyn[home, sub] = value
                else:
                    fixed[home, pl.ds((f - 3) * FIELD + k * TILE, TILE)] = value

    def edge(ref, axis, f, k):
        return ref[pl.ds(axis * SLOTS, SLOTS), pl.ds(f * FIELD + k * TILE, TILE)]

    last = STRIPS - 1
    blank = jnp.zeros((MOVERS, TILE), f32)
    for axis in range(2):
        lower = side_links(nb, base[0], 2 * axis)
        higher = side_links(nb, base[0], 2 * axis + 1)
        ups = (edge(dyn, axis, 0, last), edge(fixed, axis, 0, last), edge(fixed, axis, 1, last), edge(dyn, axis, 1, last))
        downs = (edge(dyn, axis, 0, 0), edge(fixed, axis, 0, 0), edge(fixed, axis, 1, 0))
        for f in range(4):
            up = route(higher[2], ups[f])
            down = route(lower[2], downs[f]) if f < 3 else blank
            up, down = swap(is_odd(base, axis), up, down)
            if axis == 0:
                x_0[pl.ds(f * MOVERS, MOVERS), :] = up
                x_1[pl.ds(f * MOVERS, MOVERS), :] = down
            else:
                y_0[pl.ds(f * MOVERS, MOVERS), :] = up
                y_1[pl.ds(f * MOVERS, MOVERS), :] = down


def other_axis(x):
    return jnp.concatenate([x[SLOTS:], x[:SLOTS]], 0)


def gather_halos(nb, base_ref, dyn, fixed, messages, first):
    last = STRIPS - 1
    out = {}
    parts = {name: [] for name in ("h_lo", "h_hi", "z_lo", "n_lo", "q_lo", "z_hi", "n_hi", "lo", "hi")}
    picks = []
    for axis in range(2):
        home = pl.ds(axis * SLOTS, SLOTS)
        lower = side_links(nb, base_ref[0], 2 * axis)
        higher = side_links(nb, base_ref[0], 2 * axis + 1)
        picks.append((lower[2], higher[2]))

        def message(f):
            rows = pl.ds(f * MOVERS, MOVERS)
            pair = messages[axis]
            from_higher, from_lower = swap(is_odd(base_ref, axis), pair[0][rows, :], pair[1][rows, :])
            return from_lower, from_higher

        def strip(ref, f, k):
            return ref[home, pl.ds(f * FIELD + k * TILE, TILE)]

        def low(f, rows):
            return halo_of(lower, rows, message(f)[0])

        def high(f, rows):
            return halo_of(higher, rows, message(f)[1])

        parts["h_lo"].append(low(0, strip(dyn, 0, last)))
        parts["h_hi"].append(high(0, strip(dyn, 0, 0)))
        if first:
            parts["z_lo"].append(low(1, strip(fixed, 0, last)))
            parts["n_lo"].append(low(2, strip(fixed, 1, last)))
            parts["q_lo"].append(low(3, strip(dyn, 1, last)))
            parts["z_hi"].append(high(1, strip(fixed, 0, 0)))
            parts["n_hi"].append(high(2, strip(fixed, 1, 0)))
        parts["lo"].append(jnp.broadcast_to(lower[3], (SLOTS, TILE)))
        parts["hi"].append(jnp.broadcast_to(higher[3], (SLOTS, TILE)))
    for name, pieces in parts.items():
        if pieces:
            out[name] = jnp.concatenate(pieces, 0)
    return out, picks


def step_kernel(turn, base, nb, dyn, fixed, *rest):
    first = turn == 0
    if first:
        still = None
        (x0, x1, y0, y1), rest = rest[:4], rest[4:]
    else:
        still = rest[0]
        (x0, x1, y0, y1), rest = rest[1:5], rest[5:]
    dyn_out, still_out, trail, x_0, x_1, y_0, y_1 = rest
    halo, picks = gather_halos(nb, base, dyn, fixed, ((x0, x1), (y0, y1)), first)
    names = ("z_lo", "n_lo", "z_hi", "n_hi", "q_lo")
    if not first:
        for j, name in enumerate(names):
            halo[name] = still[:, pl.ds(j * TILE, TILE)]

    def get(ref, f, k):
        return ref[:, pl.ds(f * FIELD + k * TILE, TILE)]

    last = STRIPS - 1
    h = [get(dyn, 0, k) for k in range(STRIPS)]
    z = [get(fixed, 0, k) for k in range(STRIPS)]
    n = [get(fixed, 1, k) for k in range(STRIPS)]
    low_face = flux(halo["q_lo"], halo["h_lo"], h[0], z[0] - halo["z_lo"], RUB * (halo["n_lo"] + n[0]))
    low_face = jnp.where(halo["lo"] > 0.0, low_face, 0.0)
    high_face = flux(get(dyn, 1, last), h[last], halo["h_hi"], halo["z_hi"] - z[last], RUB * (n[last] + halo["n_hi"]))
    high_face = jnp.where(halo["hi"] > 0.0, high_face, 0.0)
    for j, name in enumerate(names[:4]):
        still_out[:, pl.ds(j * TILE, TILE)] = halo[name]
    still_out[:, pl.ds(4 * TILE, TILE)] = low_face
    trail[:, pl.ds(0, TILE)] = low_face
    trail[:, pl.ds(TILE, TILE)] = halo["h_hi"]

    lane = iota((2 * SLOTS, TILE), 1)
    side_h = other_axis(halo["h_hi"])
    side_z = other_axis(halo["z_hi"])
    side_n = other_axis(halo["n_hi"])
    side_wall = other_axis(halo["hi"]) <= 0.0
    side_in = other_axis(low_face)

    def cell(x, k):
        at = k if k < DEPTH else TILE - STRIPS + k
        return jnp.broadcast_to(x[:, at : at + 1], x.shape)

    def ahead(x, k, side):
        return jnp.where(lane == TILE - 1, cell(side, k), pltpu.roll(x, TILE - 1, 1))

    reach = DEPTH - 1 - turn
    low_keep = list(range(reach))
    high_keep = list(range(STRIPS - reach, STRIPS))
    face = {-1: low_face, last: high_face}
    for k in low_keep + [x - 1 for x in high_keep]:
        face[k] = flux(get(dyn, 1, k), h[k], h[k + 1], z[k + 1] - z[k], RUB * (n[k] + n[k + 1]))
    new = {}
    for k in low_keep + high_keep:
        side = flux(
            get(dyn, 2, k), h[k], ahead(h[k], k, side_h), ahead(z[k], k, side_z) - z[k],
            RUB * (n[k] + ahead(n[k], k, side_n)),
        )
        side = jnp.where((lane == TILE - 1) & side_wall, 0.0, side)
        before = jnp.where(lane == 0, cell(side_in, k), pltpu.roll(side, 1, 1))
        new[k] = h[k] + GAIN * ((face[k - 1] - face[k]) + (before - side))
        dyn_out[:, pl.ds(2 * FIELD + k * TILE, TILE)] = side
    blank = jnp.zeros((2 * SLOTS, TILE), f32)
    for k in range(STRIPS):
        dyn_out[:, pl.ds(k * TILE, TILE)] = new[k] if k in new else blank
        dyn_out[:, pl.ds(FIELD + k * TILE, TILE)] = face[k] if k in face else blank
        if k not in new:
            dyn_out[:, pl.ds(2 * FIELD + k * TILE, TILE)] = blank
    for axis in range(2):
        home = slice(axis * SLOTS, (axis + 1) * SLOTS)
        up = route(picks[axis][1], new[last][home])
        down = route(picks[axis][0], new[0][home])
        up, down = swap(is_odd(base, axis), up, down)
        if axis == 0:
            x_0[...] = up
            x_1[...] = down
        else:
            y_0[...] = up
            y_1[...] = down


def run_tiles(
    queue, origin, count, moves_sources, tiles, nb_s, edges, columns, outs, before_loop,
    inbox, outbox, in_sem, out_sem, *spaces,
):
    depth, discharge, bed, friction = tiles
    depth_out, flow_out = outs

    def fetch(j):
        t = queue[j]
        buf = j % BUFFERS
        sem = in_sem.at[buf]
        box = inbox.at[buf]
        kind = origin[t]

        if depth is not None:

            @pl.when(kind == 0)
            def _():
                one = pl.ds(pl.multiple_of(t * TILE, TILE), TILE)
                two = pl.ds(pl.multiple_of(t * (2 * TILE), TILE), 2 * TILE)
                pltpu.make_async_copy(depth.at[one], box.at[pl.ds(0, TILE)], sem).start()
                pltpu.make_async_copy(discharge.at[two], box.at[pl.ds(TILE, 2 * TILE)], sem).start()
                pltpu.make_async_copy(bed.at[one], box.at[pl.ds(3 * TILE, TILE)], sem).start()
                pltpu.make_async_copy(friction.at[one], box.at[pl.ds(4 * TILE, TILE)], sem).start()

        for code, ref, at in moves_sources:

            @pl.when(kind == code)
            def _():
                pltpu.make_async_copy(ref.at[pl.ds(at, STATE)], box, sem).start()

    def arrived(buf):
        box = inbox.at[buf]
        pltpu.make_async_copy(box, box, in_sem.at[buf]).wait()

    def send(t, buf):
        box = outbox.at[buf]
        one = pl.ds(pl.multiple_of(t * TILE, TILE), TILE)
        two = pl.ds(pl.multiple_of(t * (2 * TILE), TILE), 2 * TILE)
        pltpu.make_async_copy(box.at[pl.ds(0, TILE)], depth_out.at[one], out_sem.at[buf]).start()
        pltpu.make_async_copy(box.at[pl.ds(TILE, 2 * TILE)], flow_out.at[two], out_sem.at[buf]).start()

    def sent(buf):
        box = outbox.at[buf]
        pltpu.make_async_copy(box, box, out_sem.at[buf]).wait()

    def prime():
        for j in range(BUFFERS - 2):

            @pl.when(j < count)
            def _():
                fetch(j)

    prime()
    before_loop()
    part_rows = 32
    parts = TILE // part_rows
    lane = iota((part_rows, TILE), 1)
    row = iota((part_rows, TILE), 0)
    at_first = lane == 0
    at_last = lane == TILE - 1
    bottom = row == part_rows - 1

    def ready(j):
        @pl.when(j < count)
        def _():
            arrived(j % BUFFERS)

        @pl.when((j >= OUT_BUFFERS) & (j < count))
        def _():
            sent(j % OUT_BUFFERS)

    def work(j, space):
        water, stream_x, stream_y, slope_x, slope_y, rub_x, rub_y = space
        t = queue[jnp.minimum(j, count - 1)]
        box = inbox.at[j % BUFFERS]
        out = outbox.at[j % OUT_BUFFERS]
        wall_x = nb_s[1, t] < 0
        wall_y = nb_s[3, t] < 0

        def edge_row(e):
            return edges[e, pl.ds(t, 1), :]

        z_next = edge_row(8)
        n_next = edge_row(9)
        for p in range(parts):
            rows = pl.ds(p * part_rows, part_rows)
            zr = pl.ds(3 * TILE + p * part_rows, part_rows)
            nr = pl.ds(4 * TILE + p * part_rows, part_rows)
            z = box[zr, :] * (1.0 / UNIT_H)
            n = box[nr, :]
            if p < parts - 1:
                z_dn = box[pl.ds(3 * TILE + p * part_rows + 1, part_rows), :] * (1.0 / UNIT_H)
                n_dn = box[pl.ds(4 * TILE + p * part_rows + 1, part_rows), :]
            else:
                z_dn = jnp.where(bottom, z_next, pltpu.roll(z, part_rows - 1, 0))
                n_dn = jnp.where(bottom, n_next, pltpu.roll(n, part_rows - 1, 0))
            side = columns[2, rows, :]
            z_rt = jnp.where(at_last, pltpu.roll(side, TILE - 1 - t, 1), pltpu.roll(z, TILE - 1, 1))
            n_rt = jnp.where(at_last, pltpu.roll(side, TILE - 1 - SLOTS - t, 1), pltpu.roll(n, TILE - 1, 1))
            slope_x[rows, :] = z_dn - z
            slope_y[rows, :] = z_rt - z
            rub_x[rows, :] = DRAG * (n + n_dn)
            rub_y[rows, :] = DRAG * (n + n_rt)
            water[rows, :] = box[rows, :] * (1.0 / UNIT_H)
        for s in range(4):
            water[pl.ds(TILE, 1), :] = edge_row(4 + s)
            stream_x[pl.ds(7, 1), :] = edge_row(s)
            for p in range(parts):
                rows = pl.ds(p * part_rows, part_rows)
                h = water[rows, :]
                h_dn = water[pl.ds(p * part_rows + 1, part_rows), :]
                side = pltpu.roll(columns[s // 2, rows, :], TILE - 1 - 64 * (s % 2) - 2 * t, 1)
                h_rt = jnp.where(at_last, side, pltpu.roll(h, TILE - 1, 1))
                if s == 0:
                    flow_x = box[pl.ds(TILE + p * part_rows, part_rows), :] * (1.0 / UNIT_Q)
                    flow_y = box[pl.ds(2 * TILE + p * part_rows, part_rows), :] * (1.0 / UNIT_Q)
                else:
                    flow_x = stream_x[pl.ds(8 + p * part_rows, part_rows), :]
                    flow_y = stream_y[rows, :]
                new_x = unit_flux(flow_x, h, h_dn, slope_x[rows, :], rub_x[rows, :])
                if p == parts - 1:
                    new_x = jnp.where(bottom & wall_x, 0.0, new_x)
                new_y = unit_flux(flow_y, h, h_rt, slope_y[rows, :], rub_y[rows, :])
                new_y = jnp.where(at_last & wall_y, 0.0, new_y)
                if s < 3:
                    stream_y[rows, :] = new_y
                else:
                    out[pl.ds(TILE + p * part_rows, part_rows), :] = new_x * UNIT_Q
                    out[pl.ds(2 * TILE + p * part_rows, part_rows), :] = new_y * UNIT_Q
                in_y = jnp.where(at_first, side, pltpu.roll(new_y, 1, 1))
                stream_x[pl.ds(8 + p * part_rows, part_rows), :] = new_x
                in_x = stream_x[pl.ds(7 + p * part_rows, part_rows), :]
                h_new = h + ((in_x - new_x) + (in_y - new_y))
                if s < 3:
                    water[rows, :] = h_new
                else:
                    out[rows, :] = h_new * UNIT_H

    def two_tiles(pair, carry):
        for i in range(2):
            j = 2 * pair + i

            @pl.when(j + BUFFERS - 2 < count)
            def _():
                fetch(j + BUFFERS - 2)

            ready(j)
        half = len(spaces) // 2
        for i in range(2):
            work(2 * pair + i, spaces[i * half : (i + 1) * half])
        for i in range(2):
            j = 2 * pair + i

            @pl.when(j < count)
            def _():
                send(queue[j], j % OUT_BUFFERS)

        return carry

    lax.fori_loop(0, (count + 1) // 2, two_tiles, 0)
    for b in range(OUT_BUFFERS):

        @pl.when(b < count)
        def _():
            sent(b)


def chunk_sources(entries, *chunks):
    found = []
    for pairing, ref in enumerate(chunks):
        for i, m in enumerate(entries):
            found.append((1 + pairing * MOVERS + m, ref, i * STATE))
    return found


def note_arrivals(entries, moves, base, visit):
    for m in entries:
        for pairing in range(2):
            lander = moves[way_of(base, pairing), 1, m]

            @pl.when(lander >= 0)
            def _():
                visit(lander - base[0], 1 + pairing * MOVERS + m)


def tile_kernel(
    moves, base, ids, nb_s, nb, dyn, fixed, still, x_0, x_1, y_0, y_1, t0, t1, t2,
    early_0, early_1, a_0, a_1, b_0, b_1, c_0, c_1, depth, discharge, bed, friction,
    depth_out, flow_out, edges, columns,
    zeros, turned, queue, origin, zero_sem, *scratch,
):
    def clear(t, total):
        origin[t] = 0
        return total + jnp.where(ids[t] >= 0, 1, 0)

    live = lax.fori_loop(0, SLOTS, clear, 0)

    def mark(t, code):
        origin[t] = code

    note_arrivals(EARLY + CHUNKS[0] + CHUNKS[1] + CHUNKS[2], moves, base, mark)
    note_arrivals(LATE, moves, base, lambda t, code: mark(t, -1))

    def enqueue(t, size):
        keep = origin[t] >= 0
        queue[size] = t
        return size + jnp.where(keep, 1, 0)

    count = lax.fori_loop(0, live, enqueue, 0)
    zeros[...] = jnp.zeros(zeros.shape, f32)

    def blank(t, carry):
        one = pl.ds(pl.multiple_of(t * TILE, TILE), TILE)
        two = pl.ds(pl.multiple_of(t * (2 * TILE), TILE), 2 * TILE)
        pltpu.make_async_copy(zeros.at[pl.ds(0, TILE)], depth_out.at[one], zero_sem).start()
        pltpu.make_async_copy(zeros.at[pl.ds(TILE, 2 * TILE)], flow_out.at[two], zero_sem).start()
        return carry

    def before_loop():
        lax.fori_loop(live, SLOTS, blank, 0)
        halo, _ = gather_halos(nb, base, dyn, fixed, ((x_0, x_1), (y_0, y_1)), False)

        def kept(j):
            return still[:, pl.ds(j * TILE, TILE)]

        n_first = fixed[:, pl.ds(FIELD, TILE)]
        z_first = fixed[:, pl.ds(0, TILE)]
        low_face = flux(
            kept(4), halo["h_lo"], dyn[:, pl.ds(0, TILE)], z_first - kept(0), RUB * (kept(1) + n_first)
        )
        low_face = jnp.where(halo["lo"] > 0.0, low_face, 0.0)
        trails = [(t[:, pl.ds(0, TILE)], t[:, pl.ds(TILE, TILE)]) for t in (t0, t1, t2)]
        trails.append((low_face, halo["h_hi"]))
        for s, (inflow, ahead_h) in enumerate(trails):
            inflow = inflow * (1.0 / UNIT_Q)
            ahead_h = ahead_h * (1.0 / UNIT_H)
            edges[s] = inflow[:SLOTS]
            edges[4 + s] = ahead_h[:SLOTS]
            turned[pl.ds(64 * (s % 2), SLOTS, stride=2), :] = ahead_h[SLOTS:]
            turned[pl.ds(64 * (s % 2) + 1, SLOTS, stride=2), :] = inflow[SLOTS:]
            if s % 2:
                columns[s // 2] = turned[...].T
        z_ahead = kept(2) * (1.0 / UNIT_H)
        edges[8] = z_ahead[:SLOTS]
        edges[9] = kept(3)[:SLOTS]
        turned[pl.ds(0, SLOTS), :] = z_ahead[SLOTS:]
        turned[pl.ds(SLOTS, SLOTS), :] = kept(3)[SLOTS:]
        columns[2] = turned[...].T

    sources = chunk_sources(EARLY, early_0, early_1)
    for entries, *chunks in zip(CHUNKS, (a_0, b_0, c_0), (a_1, b_1, c_1)):
        sources += chunk_sources(entries, *chunks)
    run_tiles(
        queue, origin, count, sources, (depth, discharge, bed, friction), nb_s, edges, columns,
        (depth_out, flow_out), before_loop, *scratch,
    )

    def blanked(t, carry):
        pltpu.make_async_copy(zeros, zeros, zero_sem).wait()
        return carry

    lax.fori_loop(live, SLOTS, blanked, 0)


def late_kernel(
    moves, base, nb_s, edges, columns, late_0, late_1, depth_in, flow_in,
    depth_out, flow_out, queue, origin, size, *scratch,
):
    size[0] = 0

    def enqueue(t, code):
        queue[size[0]] = t
        origin[t] = code
        size[0] = size[0] + 1

    note_arrivals(LATE, moves, base, enqueue)
    run_tiles(
        queue, origin, size[0], chunk_sources(LATE, late_0, late_1), (None,) * 4, nb_s, edges, columns,
        (depth_out, flow_out), lambda: None, *scratch,
    )


SMEM = pl.BlockSpec(memory_space=pltpu.SMEM)
VMEM = pl.BlockSpec(memory_space=pltpu.VMEM)
HBM = pl.BlockSpec(memory_space=pltpu.HBM)


def trade(block, axis, pairing):
    size = lax.axis_size(axis)
    pairs = [(i, (((i + pairing) ^ 1) - pairing) % size) for i in range(size)]
    return lax.ppermute(block, axis, pairs)


def trade_both(block_0, block_1, axis):
    got_1 = trade(block_1, axis, 1)
    got_0 = trade(block_0, axis, 0)
    return got_0, got_1


def exchange(x_0, x_1, y_0, y_1):
    got_x = trade_both(x_0, x_1, "gx")
    got_y = trade_both(y_0, y_1, "gy")
    return *got_x, *got_y


def held(*shape):
    return pltpu.VMEM(shape, f32)


def on_core(*arrays):
    return [pltpu.with_memory_space_constraint(a, pltpu.VMEM) for a in arrays]


def call(kernel, **settings):
    return pl.pallas_call(kernel, **settings)


def struct(*shape):
    return jax.ShapeDtypeStruct(shape, f32)


def loop_scratch():
    space = [
        pltpu.VMEM((TILE + 8, TILE), f32),
        pltpu.VMEM((TILE + 8, TILE), f32),
        *[pltpu.VMEM((TILE, TILE), f32)] * 5,
    ]
    return [
        pltpu.VMEM((BUFFERS, STATE, TILE), f32),
        pltpu.VMEM((OUT_BUFFERS, 3 * TILE, TILE), f32),
        pltpu.SemaphoreType.DMA((BUFFERS,)),
        pltpu.SemaphoreType.DMA((OUT_BUFFERS,)),
        *space,
        *space,
    ]


def shards(depth, discharge, bed, friction, tile_ids, neighbors, moves):
    base = (lax.axis_index(("gx", "gy")) * SLOTS).astype(i32).reshape(1)
    plan = moves[0].transpose(0, 2, 1)
    nb = neighbors.T
    tiles = [
        pltpu.with_memory_space_constraint(a, pltpu.HBM)
        for a in (
            depth.reshape(SLOTS * TILE, TILE),
            discharge.reshape(SLOTS * 2 * TILE, TILE),
            bed.reshape(SLOTS * TILE, TILE),
            friction.reshape(SLOTS * TILE, TILE),
        )
    ]
    out_0, out_1, *cargo = call(
        pack_kernel,
        in_specs=[SMEM, SMEM] + [HBM] * 4,
        out_specs=[VMEM] * (2 + 2 * len(LOADS)),
        out_shape=[held(MOVERS, 10 * FIELD)] * 2
        + [held(len(entries) * STATE, TILE) for entries in LOADS for _ in range(2)],
        scratch_shapes=[
            pltpu.VMEM((5, TILE, TILE), f32),
            pltpu.VMEM((TILE, TILE), f32),
            pltpu.SemaphoreType.DMA((len(LOADS), 2)),
        ],
        compiler_params=pltpu.CompilerParams(vmem_limit_bytes=12 * 2**20),
    )(plan, base, *tiles)
    from_0, from_1 = trade_both(out_0, out_1, "gy")
    early_0, early_1 = trade_both(*cargo[:2], "gy")
    frames = call(
        extract_kernel,
        in_specs=[HBM] * 4,
        out_specs=VMEM,
        out_shape=held(2 * SLOTS, 5 * FIELD),
        scratch_shapes=[
            pltpu.VMEM((SLOTS * TILE, TILE), f32),
            pltpu.VMEM((SLOTS * 2 * TILE, TILE), f32),
            pltpu.VMEM((SLOTS * TILE, TILE), f32),
            pltpu.VMEM((SLOTS * TILE, TILE), f32),
            pltpu.VMEM((2, 5, TILE, TILE), f32),
            pltpu.VMEM((2, TILE, TILE), f32),
            pltpu.SemaphoreType.DMA((SLOTS // GROUP, 4)),
        ],
        compiler_params=pltpu.CompilerParams(vmem_limit_bytes=20 * 2**20),
    )(*tiles)

    first_rows = 4 * MOVERS
    dyn, fixed, *sends = call(
        settle_kernel,
        in_specs=[SMEM, SMEM] + [VMEM] * 4,
        out_specs=[VMEM] * 6,
        out_shape=[
            held(2 * SLOTS, 3 * FIELD),
            held(2 * SLOTS, 2 * FIELD),
            held(first_rows, TILE),
            held(first_rows, TILE),
            held(first_rows, TILE),
            held(first_rows, TILE),
        ],
        compiler_params=pltpu.CompilerParams(vmem_limit_bytes=12 * 2**20),
    )(plan, base, *on_core(nb, frames, from_0, from_1))
    got = exchange(*sends)
    chunks = [trade_both(*cargo[2:4], "gy")]
    still = []
    trails = []
    for turn in range(3):

        def body(*refs, turn=turn):
            step_kernel(turn, *refs)

        shapes = [
            (2 * SLOTS, 3 * FIELD),
            (2 * SLOTS, 5 * TILE),
            (2 * SLOTS, 2 * TILE),
            (MOVERS, TILE),
            (MOVERS, TILE),
            (MOVERS, TILE),
            (MOVERS, TILE),
        ]
        dyn, kept, trail, *sends = call(
            body,
            in_specs=[SMEM] + [VMEM] * (7 + len(still)),
            out_specs=[VMEM] * len(shapes),
            out_shape=[held(*s) for s in shapes],
                compiler_params=pltpu.CompilerParams(vmem_limit_bytes=12 * 2**20),
        )(base, *on_core(nb, dyn, fixed, *still, *got))
        still = [kept]
        trails.append(trail)
        got = exchange(*sends)
        chunks.append(trade_both(*cargo[2 * turn + 4 : 2 * turn + 6], "gy"))

    late_0, late_1 = chunks[3]
    kept_inputs = on_core(
        nb, dyn, fixed, *still, *got, *trails, early_0, early_1, *chunks[0], *chunks[1], *chunks[2]
    )
    new_depth, new_flow, edges, columns = call(
        tile_kernel,
        in_specs=[SMEM] * 4 + [VMEM] * len(kept_inputs) + [HBM] * 4,
        out_specs=[HBM, HBM, VMEM, VMEM],
        out_shape=[
            struct(SLOTS * TILE, TILE),
            struct(SLOTS * 2 * TILE, TILE),
            held(10, SLOTS, TILE),
            held(3, TILE, TILE),
        ],
        scratch_shapes=[
            pltpu.VMEM((3 * TILE, TILE), f32),
            pltpu.VMEM((TILE, TILE), f32),
            pltpu.SMEM((SLOTS,), i32),
            pltpu.SMEM((SLOTS,), i32),
            pltpu.SemaphoreType.DMA,
            *loop_scratch(),
        ],
        compiler_params=pltpu.CompilerParams(vmem_limit_bytes=12 * 2**20),
    )(plan, base, tile_ids, nb, *kept_inputs, *tiles)
    new_depth, new_flow = pl.pallas_call(
        late_kernel,
        in_specs=[SMEM] * 3 + [VMEM] * 4 + [HBM] * 2,
        out_specs=[HBM, HBM],
        out_shape=[struct(SLOTS * TILE, TILE), struct(SLOTS * 2 * TILE, TILE)],
        input_output_aliases={7: 0, 8: 1},
        scratch_shapes=[
            pltpu.SMEM((SLOTS,), i32),
            pltpu.SMEM((SLOTS,), i32),
            pltpu.SMEM((1,), i32),
            *loop_scratch(),
        ],
        compiler_params=pltpu.CompilerParams(vmem_limit_bytes=12 * 2**20),
        name="late_tiles",
    )(plan, base, nb, *on_core(edges, columns, late_0, late_1), new_depth, new_flow)
    return (
        new_depth.reshape(SLOTS, TILE, TILE),
        new_flow.reshape(SLOTS, 2, TILE, TILE),
    )


def solution(mesh):
    return jax.shard_map(
        shards,
        mesh=mesh,
        in_specs=(
            P(("gx", "gy"), None, None),
            P(("gx", "gy"), None, None, None),
            P(("gx", "gy"), None, None),
            P(("gx", "gy"), None, None),
            P(("gx", "gy")),
            P(("gx", "gy"), None),
            P(("gx", "gy"), None, None, None),
        ),
        out_specs=(P(("gx", "gy"), None, None), P(("gx", "gy"), None, None, None)),
        check_vma=False,
    )
```

```python
import jax
import jax.numpy as jnp
from jax import lax
from jax.experimental import pallas as pl
from jax.experimental.pallas import tpu as pltpu
from jax.sharding import PartitionSpec as P


TILE = 128
SLOTS = 32
MOVERS = 8
DEPTH = 4
STRIPS = 2 * DEPTH
FIELD = STRIPS * TILE
STATE = 5 * TILE
EARLY = (0,)
CHUNKS = ((1,), (2,), (3,), (4, 5, 6, 7))
LATE = CHUNKS[3]
LOADS = (EARLY,) + CHUNKS
GROUP = 8
GY = 16
SIDE = 2
BUFFERS = SIDE + 4
OUT_BUFFERS = 2 * SIDE

gravity = 9.81
step_time = 0.25
spacing = 2.0
min_depth = 0.15
PULL = gravity * step_time / spacing
RUB = gravity * step_time * 0.5
GAIN = step_time / spacing
UNIT_H = 2.0 / (GAIN * PULL)
UNIT_Q = UNIT_H / GAIN
FLOOR = 2.0 * min_depth / UNIT_H
DRAG = RUB * UNIT_Q * (0.5 * UNIT_H) ** (-7.0 / 3.0)

f32 = jnp.float32
bf16 = jnp.bfloat16
i32 = jnp.int32


def flux(flow, h_lo, h_hi, slope, rub):
    depth_face = jnp.maximum(0.5 * (h_lo + h_hi), min_depth)
    drive = flow - (PULL * depth_face) * ((h_hi - h_lo) + slope)
    loss = jnp.exp2(jnp.log2(depth_face) * (-7.0 / 3.0))
    return drive / (1.0 + (rub * jnp.abs(flow)) * loss)


def unit_flux(flow, h_lo, h_hi, slope, rub):
    depth_sum = jnp.maximum(h_lo + h_hi, FLOOR)
    drive = flow - depth_sum * ((h_hi - h_lo) + slope)
    loss = jnp.exp2(jnp.log2(depth_sum) * (-7.0 / 3.0))
    return drive / (1.0 + (rub * jnp.abs(flow)) * loss)


def iota(shape, dim):
    return lax.broadcasted_iota(i32, shape, dim)


def route(onehot, rows):
    a = rows.astype(bf16)
    rest = rows - a.astype(f32)
    b = rest.astype(bf16)
    c = (rest - b.astype(f32)).astype(bf16)
    take = onehot.astype(bf16)

    def part(x):
        return jnp.dot(take, x, preferred_element_type=f32)

    return part(a) + part(b) + part(c)


def side_links(nb_ref, base, side):
    square = (SLOTS, SLOTS)
    rows = iota(square, 0)
    cols = iota(square, 1)
    link_row = jnp.broadcast_to(nb_ref[side : side + 1, :].astype(f32), square)
    diagonal = rows == cols

    def column(x):
        return jnp.broadcast_to(jnp.sum(jnp.where(diagonal, x, 0.0), 1, keepdims=True), square)

    first = base.astype(f32)

    def remote(link):
        return jnp.where((link >= 0.0) & ((link < first) | (link >= first + SLOTS)), 1.0, 0.0)

    link_b = column(link_row)
    missing = link_b[:, :1] < 0.0
    far_b = remote(link_b)
    far = far_b[:, :1]
    far_row = remote(link_row)
    near = jnp.where(link_b - first == cols.astype(f32), 1.0, 0.0)
    rank = jnp.sum(jnp.where(link_row < link_b, far_row, 0.0), 1, keepdims=True)
    order_row = jnp.sum(jnp.where(rows < cols, far_b, 0.0), 0, keepdims=True)
    far_row = far_row[:1]
    place = jnp.where(
        (jnp.broadcast_to(rank, (SLOTS, MOVERS)) == iota((SLOTS, MOVERS), 1).astype(f32))
        & (jnp.broadcast_to(far, (SLOTS, MOVERS)) > 0.0),
        1.0,
        0.0,
    )
    pick = jnp.where(
        (jnp.broadcast_to(order_row, (MOVERS, SLOTS)) == iota((MOVERS, SLOTS), 0).astype(f32))
        & (jnp.broadcast_to(far_row, (MOVERS, SLOTS)) > 0.0),
        1.0,
        0.0,
    )
    exists = jnp.where(missing, 0.0, 1.0)
    return near, place, pick, exists


def halo_of(links, rows, message):
    near, place, _, _ = links
    return route(near, rows) + route(place, message)


def extract_kernel(
    depth, discharge, bed, friction, frames, depth_v, flow_v, bed_v, rough_v, acc, turned, load_sem,
):
    lane = iota((TILE, TILE), 1)
    groups = SLOTS // GROUP
    loads = []
    for g in range(groups):
        one = pl.ds(g * GROUP * TILE, GROUP * TILE)
        two = pl.ds(g * GROUP * 2 * TILE, GROUP * 2 * TILE)
        pairs = ((depth, depth_v, one), (discharge, flow_v, two), (bed, bed_v, one), (friction, rough_v, one))
        copies = [pltpu.make_async_copy(a.at[r], b.at[r], load_sem.at[g, i]) for i, (a, b, r) in enumerate(pairs)]
        for c in copies:
            c.start()
        loads.append(copies)

    def strip(f, k):
        return pl.ds((f * STRIPS + k) * TILE, TILE)

    sources = ((depth_v, 0, 1), (flow_v, 0, 2), (flow_v, 1, 2), (bed_v, 0, 1), (rough_v, 0, 1))
    for g in range(groups):
        for c in loads[g]:
            c.wait()
        home = pl.ds(g * GROUP, GROUP)
        for f, (ref, part, parts) in enumerate(sources):
            top = (g * GROUP * parts + part) * TILE
            for k in range(STRIPS):
                row = k if k < DEPTH else TILE - STRIPS + k
                frames[home, strip(f, k)] = ref[pl.ds(top + row, GROUP, stride=parts * TILE), :]
            half = g * GROUP * STRIPS // TILE
            packed = acc[half, f] if g * GROUP * STRIPS % TILE else None
            for t in range(GROUP):
                tile = ref[pl.ds(top + t * parts * TILE, TILE), :]
                at = (g * GROUP + t) * STRIPS % TILE
                turn = pltpu.roll(tile, (at + DEPTH) % TILE, 1)
                packed = turn if packed is None else jnp.where(lane >= at, turn, packed)
            acc[half, f] = packed

    per = TILE // STRIPS
    for f in range(5):
        to = (0, 2, 1, 3, 4)[f]
        for half in range(SLOTS // per):
            turned[half] = acc[half, f].T
            for k in range(STRIPS):
                frames[pl.ds(SLOTS + half * per, per), strip(to, k)] = turned[
                    half, pl.ds((k + DEPTH) % STRIPS, per, stride=STRIPS), :
                ]


def pack_kernel(moves, base, depth, discharge, bed, friction, out_0, out_1, *rest):
    boxes, (acc, turned, sem) = rest[: 2 * len(LOADS)], rest[2 * len(LOADS) :]
    for g, entries in enumerate(LOADS):
        start_chunk(entries, moves, base, (depth, discharge, bed, friction), *boxes[2 * g : 2 * g + 2], sem.at[g])
    lane = iota((TILE, TILE), 1)
    outs = (out_0, out_1)
    for g, entries in enumerate(LOADS):
        finish_chunk(entries, *boxes[2 * g : 2 * g + 2], sem.at[g])
        for i, m in enumerate(entries):
            for pairing in range(2):
                box = boxes[2 * g + pairing]
                at = (2 * m + pairing) * STRIPS
                for f in range(5):
                    top = i * STATE + f * TILE
                    for k in range(STRIPS):
                        row = k if k < DEPTH else TILE - STRIPS + k
                        to = pl.ds((f * STRIPS + k) * TILE, TILE)
                        outs[pairing][pl.ds(m, 1), to] = box[pl.ds(top + row, 1), :]
                    turn = pltpu.roll(box[pl.ds(top, TILE), :], (at + DEPTH) % TILE, 1)
                    acc[f] = turn if at == 0 else jnp.where(lane >= at, turn, acc[f])
    for f in range(5):
        to = 5 * STRIPS + (0, 2, 1, 3, 4)[f] * STRIPS
        turned[...] = acc[f].T
        for pairing in range(2):
            for k in range(STRIPS):
                outs[pairing][:, pl.ds((to + k) * TILE, TILE)] = turned[
                    pl.ds(pairing * STRIPS + (k + DEPTH) % STRIPS, MOVERS, stride=2 * STRIPS), :
                ]


def start_chunk(entries, moves, base, tiles, out_0, out_1, sem):
    depth, discharge, bed, friction = tiles
    for pairing, out in enumerate((out_0, out_1)):
        way = way_of(base, pairing)
        for i, m in enumerate(entries):
            slot = jnp.clip(moves[way, 0, m] - base[0], 0, SLOTS - 1)
            at = i * STATE
            one = pl.ds(pl.multiple_of(slot * TILE, TILE), TILE)
            two = pl.ds(pl.multiple_of(slot * (2 * TILE), TILE), 2 * TILE)
            pltpu.make_async_copy(depth.at[one], out.at[pl.ds(at, TILE)], sem.at[pairing]).start()
            pltpu.make_async_copy(discharge.at[two], out.at[pl.ds(at + TILE, 2 * TILE)], sem.at[pairing]).start()
            pltpu.make_async_copy(bed.at[one], out.at[pl.ds(at + 3 * TILE, TILE)], sem.at[pairing]).start()
            pltpu.make_async_copy(friction.at[one], out.at[pl.ds(at + 4 * TILE, TILE)], sem.at[pairing]).start()


def finish_chunk(entries, out_0, out_1, sem):
    if not entries:
        return
    body = pl.ds(0, len(entries) * STATE)
    for pairing, out in enumerate((out_0, out_1)):
        pltpu.make_async_copy(out.at[body], out.at[body], sem.at[pairing]).wait()


def is_odd(base, axis):
    return ((base[0] // (SLOTS * (GY if axis == 0 else 1))) % 2) == 1


def way_of(base, pairing):
    odd = (base[0] // SLOTS) % 2
    return odd if pairing else 1 - odd


def swap(odd, a, b):
    return jnp.where(odd, b, a), jnp.where(odd, a, b)


def settle_kernel(
    moves, base, nb, frames, from_0, from_1, dyn, fixed, x_0, x_1, y_0, y_1,
):
    shape = (SLOTS, 2 * MOVERS)
    land = jnp.zeros(shape, f32)
    left = jnp.zeros((SLOTS, TILE), f32)
    for m in range(MOVERS):
        for pairing in range(2):
            way = way_of(base, pairing)
            lander = moves[way, 1, m] - base[0]
            leaver = moves[way, 0, m] - base[0]
            spot = (iota(shape, 0) == lander) & (iota(shape, 1) == pairing * MOVERS + m)
            land = jnp.where(spot, 1.0, land)
            row = iota((SLOTS, TILE), 0)
            left = jnp.where((row == leaver) | (row == lander), 1.0, left)
    for axis in range(2):
        home = pl.ds(axis * SLOTS, SLOTS)
        for f in range(5):
            part = pl.ds(f * FIELD, FIELD)
            came = pl.ds((axis * 5 + f) * FIELD, FIELD)
            fresh = route(land, jnp.concatenate([from_0[:, came], from_1[:, came]], 0))
            for k in range(STRIPS):
                sub = pl.ds(f * FIELD + k * TILE, TILE)
                value = jnp.where(left > 0.0, 0.0, frames[home, sub]) + fresh[:, k * TILE : (k + 1) * TILE]
                if f < 3:
                    dyn[home, sub] = value
                else:
                    fixed[home, pl.ds((f - 3) * FIELD + k * TILE, TILE)] = value

    def edge(ref, axis, f, k):
        return ref[pl.ds(axis * SLOTS, SLOTS), pl.ds(f * FIELD + k * TILE, TILE)]

    last = STRIPS - 1
    blank = jnp.zeros((MOVERS, TILE), f32)
    for axis in range(2):
        lower = side_links(nb, base[0], 2 * axis)
        higher = side_links(nb, base[0], 2 * axis + 1)
        ups = (edge(dyn, axis, 0, last), edge(fixed, axis, 0, last), edge(fixed, axis, 1, last), edge(dyn, axis, 1, last))
        downs = (edge(dyn, axis, 0, 0), edge(fixed, axis, 0, 0), edge(fixed, axis, 1, 0))
        for f in range(4):
            up = route(higher[2], ups[f])
            down = route(lower[2], downs[f]) if f < 3 else blank
            up, down = swap(is_odd(base, axis), up, down)
            if axis == 0:
                x_0[pl.ds(f * MOVERS, MOVERS), :] = up
                x_1[pl.ds(f * MOVERS, MOVERS), :] = down
            else:
                y_0[pl.ds(f * MOVERS, MOVERS), :] = up
                y_1[pl.ds(f * MOVERS, MOVERS), :] = down


def other_axis(x):
    return jnp.concatenate([x[SLOTS:], x[:SLOTS]], 0)


def gather_halos(nb, base_ref, dyn, fixed, messages, first):
    last = STRIPS - 1
    out = {}
    parts = {name: [] for name in ("h_lo", "h_hi", "z_lo", "n_lo", "q_lo", "z_hi", "n_hi", "lo", "hi")}
    picks = []
    for axis in range(2):
        home = pl.ds(axis * SLOTS, SLOTS)
        lower = side_links(nb, base_ref[0], 2 * axis)
        higher = side_links(nb, base_ref[0], 2 * axis + 1)
        picks.append((lower[2], higher[2]))

        def message(f):
            rows = pl.ds(f * MOVERS, MOVERS)
            pair = messages[axis]
            from_higher, from_lower = swap(is_odd(base_ref, axis), pair[0][rows, :], pair[1][rows, :])
            return from_lower, from_higher

        def strip(ref, f, k):
            return ref[home, pl.ds(f * FIELD + k * TILE, TILE)]

        def low(f, rows):
            return halo_of(lower, rows, message(f)[0])

        def high(f, rows):
            return halo_of(higher, rows, message(f)[1])

        parts["h_lo"].append(low(0, strip(dyn, 0, last)))
        parts["h_hi"].append(high(0, strip(dyn, 0, 0)))
        if first:
            parts["z_lo"].append(low(1, strip(fixed, 0, last)))
            parts["n_lo"].append(low(2, strip(fixed, 1, last)))
            parts["q_lo"].append(low(3, strip(dyn, 1, last)))
            parts["z_hi"].append(high(1, strip(fixed, 0, 0)))
            parts["n_hi"].append(high(2, strip(fixed, 1, 0)))
        parts["lo"].append(jnp.broadcast_to(lower[3], (SLOTS, TILE)))
        parts["hi"].append(jnp.broadcast_to(higher[3], (SLOTS, TILE)))
    for name, pieces in parts.items():
        if pieces:
            out[name] = jnp.concatenate(pieces, 0)
    return out, picks


def step_kernel(turn, base, nb, dyn, fixed, *rest):
    first = turn == 0
    if first:
        still = None
        (x0, x1, y0, y1), rest = rest[:4], rest[4:]
    else:
        still = rest[0]
        (x0, x1, y0, y1), rest = rest[1:5], rest[5:]
    dyn_out, still_out, trail, x_0, x_1, y_0, y_1 = rest
    halo, picks = gather_halos(nb, base, dyn, fixed, ((x0, x1), (y0, y1)), first)
    names = ("z_lo", "n_lo", "z_hi", "n_hi", "q_lo")
    if not first:
        for j, name in enumerate(names):
            halo[name] = still[:, pl.ds(j * TILE, TILE)]

    def get(ref, f, k):
        return ref[:, pl.ds(f * FIELD + k * TILE, TILE)]

    last = STRIPS - 1
    h = [get(dyn, 0, k) for k in range(STRIPS)]
    z = [get(fixed, 0, k) for k in range(STRIPS)]
    n = [get(fixed, 1, k) for k in range(STRIPS)]
    low_face = flux(halo["q_lo"], halo["h_lo"], h[0], z[0] - halo["z_lo"], RUB * (halo["n_lo"] + n[0]))
    low_face = jnp.where(halo["lo"] > 0.0, low_face, 0.0)
    high_face = flux(get(dyn, 1, last), h[last], halo["h_hi"], halo["z_hi"] - z[last], RUB * (n[last] + halo["n_hi"]))
    high_face = jnp.where(halo["hi"] > 0.0, high_face, 0.0)
    for j, name in enumerate(names[:4]):
        still_out[:, pl.ds(j * TILE, TILE)] = halo[name]
    still_out[:, pl.ds(4 * TILE, TILE)] = low_face
    trail[:, pl.ds(0, TILE)] = low_face
    trail[:, pl.ds(TILE, TILE)] = halo["h_hi"]

    lane = iota((2 * SLOTS, TILE), 1)
    side_h = other_axis(halo["h_hi"])
    side_z = other_axis(halo["z_hi"])
    side_n = other_axis(halo["n_hi"])
    side_wall = other_axis(halo["hi"]) <= 0.0
    side_in = other_axis(low_face)

    def cell(x, k):
        at = k if k < DEPTH else TILE - STRIPS + k
        return jnp.broadcast_to(x[:, at : at + 1], x.shape)

    def ahead(x, k, side):
        return jnp.where(lane == TILE - 1, cell(side, k), pltpu.roll(x, TILE - 1, 1))

    reach = DEPTH - 1 - turn
    low_keep = list(range(reach))
    high_keep = list(range(STRIPS - reach, STRIPS))
    face = {-1: low_face, last: high_face}
    for k in low_keep + [x - 1 for x in high_keep]:
        face[k] = flux(get(dyn, 1, k), h[k], h[k + 1], z[k + 1] - z[k], RUB * (n[k] + n[k + 1]))
    new = {}
    for k in low_keep + high_keep:
        side = flux(
            get(dyn, 2, k), h[k], ahead(h[k], k, side_h), ahead(z[k], k, side_z) - z[k],
            RUB * (n[k] + ahead(n[k], k, side_n)),
        )
        side = jnp.where((lane == TILE - 1) & side_wall, 0.0, side)
        before = jnp.where(lane == 0, cell(side_in, k), pltpu.roll(side, 1, 1))
        new[k] = h[k] + GAIN * ((face[k - 1] - face[k]) + (before - side))
        dyn_out[:, pl.ds(2 * FIELD + k * TILE, TILE)] = side
    blank = jnp.zeros((2 * SLOTS, TILE), f32)
    for k in range(STRIPS):
        dyn_out[:, pl.ds(k * TILE, TILE)] = new[k] if k in new else blank
        dyn_out[:, pl.ds(FIELD + k * TILE, TILE)] = face[k] if k in face else blank
        if k not in new:
            dyn_out[:, pl.ds(2 * FIELD + k * TILE, TILE)] = blank
    for axis in range(2):
        home = slice(axis * SLOTS, (axis + 1) * SLOTS)
        up = route(picks[axis][1], new[last][home])
        down = route(picks[axis][0], new[0][home])
        up, down = swap(is_odd(base, axis), up, down)
        if axis == 0:
            x_0[...] = up
            x_1[...] = down
        else:
            y_0[...] = up
            y_1[...] = down


def run_tiles(
    queue, origin, count, moves_sources, tiles, nb_s, edges, columns, outs, before_loop,
    inbox, outbox, in_sem, out_sem, *spaces, direct=None,
):
    depth, discharge, bed, friction = tiles
    depth_out, flow_out = outs

    def fetch(j):
        t = queue[j]
        buf = j % BUFFERS
        sem = in_sem.at[buf]
        box = inbox.at[buf]
        kind = origin[t]

        if depth is not None:

            @pl.when(kind == 0)
            def _():
                one = pl.ds(pl.multiple_of(t * TILE, TILE), TILE)
                two = pl.ds(pl.multiple_of(t * (2 * TILE), TILE), 2 * TILE)
                pltpu.make_async_copy(depth.at[one], box.at[pl.ds(0, TILE)], sem).start()
                pltpu.make_async_copy(discharge.at[two], box.at[pl.ds(TILE, 2 * TILE)], sem).start()
                pltpu.make_async_copy(bed.at[one], box.at[pl.ds(3 * TILE, TILE)], sem).start()
                pltpu.make_async_copy(friction.at[one], box.at[pl.ds(4 * TILE, TILE)], sem).start()

        @pl.when(kind != 0)
        def _():
            for code, ref, at in moves_sources:

                @pl.when(kind == code)
                def _():
                    pltpu.make_async_copy(ref.at[pl.ds(at, STATE)], box, sem).start()

    def arrived(buf):
        box = inbox.at[buf]
        pltpu.make_async_copy(box, box, in_sem.at[buf]).wait()

    def send(t, buf):
        box = outbox.at[buf]
        one = pl.ds(pl.multiple_of(t * TILE, TILE), TILE)
        two = pl.ds(pl.multiple_of(t * (2 * TILE), TILE), 2 * TILE)
        pltpu.make_async_copy(box.at[pl.ds(0, TILE)], depth_out.at[one], out_sem.at[buf]).start()
        pltpu.make_async_copy(box.at[pl.ds(TILE, 2 * TILE)], flow_out.at[two], out_sem.at[buf]).start()

    def sent(buf):
        box = outbox.at[buf]
        pltpu.make_async_copy(box, box, out_sem.at[buf]).wait()

    def prime():
        for j in range(BUFFERS - SIDE):

            @pl.when(j < count)
            def _():
                fetch(j)

    if direct is None:
        prime()
        before_loop()
    part_rows = 32
    parts = TILE // part_rows
    lane = iota((part_rows, TILE), 1)
    row = iota((part_rows, TILE), 0)
    at_first = lane == 0
    at_last = lane == TILE - 1
    bottom = row == part_rows - 1

    def ready(j):
        @pl.when(j < count)
        def _():
            arrived(j % BUFFERS)

        @pl.when((j >= OUT_BUFFERS) & (j < count))
        def _():
            sent(j % OUT_BUFFERS)

    def work(t, box, out, space):
        water, stream_x, stream_y, slope_x, slope_y, rub_x, rub_y = space
        wall_x = nb_s[1, t] < 0
        wall_y = nb_s[3, t] < 0

        def edge_row(e):
            return edges[e, pl.ds(t, 1), :]

        z_next = edge_row(8)
        n_next = edge_row(9)
        for p in range(parts):
            rows = pl.ds(p * part_rows, part_rows)
            zr = pl.ds(3 * TILE + p * part_rows, part_rows)
            nr = pl.ds(4 * TILE + p * part_rows, part_rows)
            z = box[zr, :] * (1.0 / UNIT_H)
            n = box[nr, :]
            if p < parts - 1:
                z_dn = box[pl.ds(3 * TILE + p * part_rows + 1, part_rows), :] * (1.0 / UNIT_H)
                n_dn = box[pl.ds(4 * TILE + p * part_rows + 1, part_rows), :]
            else:
                z_dn = jnp.where(bottom, z_next, pltpu.roll(z, part_rows - 1, 0))
                n_dn = jnp.where(bottom, n_next, pltpu.roll(n, part_rows - 1, 0))
            side = columns[2, rows, :]
            z_rt = jnp.where(at_last, pltpu.roll(side, TILE - 1 - t, 1), pltpu.roll(z, TILE - 1, 1))
            n_rt = jnp.where(at_last, pltpu.roll(side, TILE - 1 - SLOTS - t, 1), pltpu.roll(n, TILE - 1, 1))
            slope_x[rows, :] = z_dn - z
            slope_y[rows, :] = z_rt - z
            rub_x[rows, :] = DRAG * (n + n_dn)
            rub_y[rows, :] = DRAG * (n + n_rt)
            water[rows, :] = box[rows, :] * (1.0 / UNIT_H)
        for s in range(4):
            water[pl.ds(TILE, 1), :] = edge_row(4 + s)
            stream_x[pl.ds(7, 1), :] = edge_row(s)
            for p in range(parts):
                rows = pl.ds(p * part_rows, part_rows)
                h = water[rows, :]
                h_dn = water[pl.ds(p * part_rows + 1, part_rows), :]
                side = pltpu.roll(columns[s // 2, rows, :], TILE - 1 - 64 * (s % 2) - 2 * t, 1)
                h_rt = jnp.where(at_last, side, pltpu.roll(h, TILE - 1, 1))
                if s == 0:
                    flow_x = box[pl.ds(TILE + p * part_rows, part_rows), :] * (1.0 / UNIT_Q)
                    flow_y = box[pl.ds(2 * TILE + p * part_rows, part_rows), :] * (1.0 / UNIT_Q)
                else:
                    flow_x = stream_x[pl.ds(8 + p * part_rows, part_rows), :]
                    flow_y = stream_y[rows, :]
                new_x = unit_flux(flow_x, h, h_dn, slope_x[rows, :], rub_x[rows, :])
                if p == parts - 1:
                    new_x = jnp.where(bottom & wall_x, 0.0, new_x)
                new_y = unit_flux(flow_y, h, h_rt, slope_y[rows, :], rub_y[rows, :])
                new_y = jnp.where(at_last & wall_y, 0.0, new_y)
                if s < 3:
                    stream_y[rows, :] = new_y
                else:
                    out[pl.ds(TILE + p * part_rows, part_rows), :] = new_x * UNIT_Q
                    out[pl.ds(2 * TILE + p * part_rows, part_rows), :] = new_y * UNIT_Q
                in_y = jnp.where(at_first, side, pltpu.roll(new_y, 1, 1))
                stream_x[pl.ds(8 + p * part_rows, part_rows), :] = new_x
                in_x = stream_x[pl.ds(7 + p * part_rows, part_rows), :]
                h_new = h + ((in_x - new_x) + (in_y - new_y))
                if s < 3:
                    water[rows, :] = h_new
                else:
                    out[rows, :] = h_new * UNIT_H

    def side_by_side(turn, carry):
        for i in range(SIDE):
            j = SIDE * turn + i

            @pl.when(j + BUFFERS - SIDE < count)
            def _():
                fetch(j + BUFFERS - SIDE)

            ready(j)
        share = len(spaces) // SIDE
        for i in range(SIDE):
            j = SIDE * turn + i
            t = queue[jnp.minimum(j, count - 1)]
            work(t, inbox.at[j % BUFFERS], outbox.at[j % OUT_BUFFERS], spaces[i * share : (i + 1) * share])
        for i in range(SIDE):
            j = SIDE * turn + i

            @pl.when(j < count)
            def _():
                send(queue[j], j % OUT_BUFFERS)

        return carry

    if direct is not None:
        direct(work, send, sent, outbox, spaces)
        return
    lax.fori_loop(0, (count + SIDE - 1) // SIDE, side_by_side, 0)
    for b in range(OUT_BUFFERS):

        @pl.when(b < count)
        def _():
            sent(b)


def chunk_sources(entries, *chunks):
    found = []
    for pairing, ref in enumerate(chunks):
        for i, m in enumerate(entries):
            found.append((1 + pairing * MOVERS + m, ref, i * STATE))
    return found


def note_arrivals(entries, moves, base, visit):
    for m in entries:
        for pairing in range(2):
            lander = moves[way_of(base, pairing), 1, m]

            @pl.when(lander >= 0)
            def _():
                visit(lander - base[0], 1 + pairing * MOVERS + m)


def tile_kernel(
    moves, base, ids, nb_s, nb, dyn, fixed, still, x_0, x_1, y_0, y_1, t0, t1, t2,
    early_0, early_1, a_0, a_1, b_0, b_1, c_0, c_1, depth, discharge, bed, friction,
    depth_out, flow_out, edges, columns,
    zeros, turned, queue, origin, zero_sem, *scratch,
):
    def clear(t, total):
        origin[t] = 0
        return total + jnp.where(ids[t] >= 0, 1, 0)

    live = lax.fori_loop(0, SLOTS, clear, 0)

    def mark(t, code):
        origin[t] = code

    note_arrivals(EARLY + CHUNKS[0] + CHUNKS[1] + CHUNKS[2], moves, base, mark)
    note_arrivals(LATE, moves, base, lambda t, code: mark(t, -1))

    def enqueue(t, size):
        keep = origin[t] >= 0
        queue[size] = t
        return size + jnp.where(keep, 1, 0)

    count = lax.fori_loop(0, live, enqueue, 0)
    zeros[...] = jnp.zeros(zeros.shape, f32)

    def blank(t, carry):
        one = pl.ds(pl.multiple_of(t * TILE, TILE), TILE)
        two = pl.ds(pl.multiple_of(t * (2 * TILE), TILE), 2 * TILE)
        pltpu.make_async_copy(zeros.at[pl.ds(0, TILE)], depth_out.at[one], zero_sem).start()
        pltpu.make_async_copy(zeros.at[pl.ds(TILE, 2 * TILE)], flow_out.at[two], zero_sem).start()
        return carry

    def before_loop():
        lax.fori_loop(live, SLOTS, blank, 0)
        halo, _ = gather_halos(nb, base, dyn, fixed, ((x_0, x_1), (y_0, y_1)), False)

        def kept(j):
            return still[:, pl.ds(j * TILE, TILE)]

        n_first = fixed[:, pl.ds(FIELD, TILE)]
        z_first = fixed[:, pl.ds(0, TILE)]
        low_face = flux(
            kept(4), halo["h_lo"], dyn[:, pl.ds(0, TILE)], z_first - kept(0), RUB * (kept(1) + n_first)
        )
        low_face = jnp.where(halo["lo"] > 0.0, low_face, 0.0)
        trails = [(t[:, pl.ds(0, TILE)], t[:, pl.ds(TILE, TILE)]) for t in (t0, t1, t2)]
        trails.append((low_face, halo["h_hi"]))
        for s, (inflow, ahead_h) in enumerate(trails):
            inflow = inflow * (1.0 / UNIT_Q)
            ahead_h = ahead_h * (1.0 / UNIT_H)
            edges[s] = inflow[:SLOTS]
            edges[4 + s] = ahead_h[:SLOTS]
            turned[pl.ds(64 * (s % 2), SLOTS, stride=2), :] = ahead_h[SLOTS:]
            turned[pl.ds(64 * (s % 2) + 1, SLOTS, stride=2), :] = inflow[SLOTS:]
            if s % 2:
                columns[s // 2] = turned[...].T
        z_ahead = kept(2) * (1.0 / UNIT_H)
        edges[8] = z_ahead[:SLOTS]
        edges[9] = kept(3)[:SLOTS]
        turned[pl.ds(0, SLOTS), :] = z_ahead[SLOTS:]
        turned[pl.ds(SLOTS, SLOTS), :] = kept(3)[SLOTS:]
        columns[2] = turned[...].T

    sources = chunk_sources(EARLY, early_0, early_1)
    for entries, *chunks in zip(CHUNKS, (a_0, b_0, c_0), (a_1, b_1, c_1)):
        sources += chunk_sources(entries, *chunks)
    run_tiles(
        queue, origin, count, sources, (depth, discharge, bed, friction), nb_s, edges, columns,
        (depth_out, flow_out), before_loop, *scratch,
    )

    def blanked(t, carry):
        pltpu.make_async_copy(zeros, zeros, zero_sem).wait()
        return carry

    lax.fori_loop(live, SLOTS, blanked, 0)


def late_kernel(
    moves, base, nb_s, edges, columns, late_0, late_1, depth_in, flow_in,
    depth_out, flow_out, *scratch,
):
    chunks = (late_0, late_1)

    def lander(i, pairing):
        return moves[way_of(base, pairing), 1, LATE[0] + i]

    def each_pair(work, send, sent, outbox, spaces):
        share = len(spaces) // 2

        def two(i, carry):
            for pairing in range(2):
                @pl.when((i >= 2) & (lander(jnp.maximum(i - 2, 0), pairing) >= 0))
                def _():
                    sent((2 * i + pairing) % 4)

            for pairing in range(2):
                t = jnp.clip(lander(i, pairing) - base[0], 0, SLOTS - 1)
                box = chunks[pairing].at[pl.ds(pl.multiple_of(i * STATE, STATE), STATE)]
                work(t, box, outbox.at[(2 * i + pairing) % 4], spaces[pairing * share : (pairing + 1) * share])
            for pairing in range(2):

                @pl.when(lander(i, pairing) >= 0)
                def _():
                    send(lander(i, pairing) - base[0], (2 * i + pairing) % 4)

            return carry

        used = 0
        for i in range(len(LATE)):
            used = used + jnp.where((lander(i, 0) >= 0) | (lander(i, 1) >= 0), 1, 0)
        lax.fori_loop(0, used, two, 0)
        for back in range(2):
            for pairing in range(2):
                i = used - 1 - back

                @pl.when((i >= 0) & (lander(jnp.maximum(i, 0), pairing) >= 0))
                def _():
                    sent((2 * i + pairing) % 4)

    run_tiles(
        None, None, 0, (), (None,) * 4, nb_s, edges, columns, (depth_out, flow_out), None, *scratch,
        direct=each_pair,
    )


SMEM = pl.BlockSpec(memory_space=pltpu.SMEM)
VMEM = pl.BlockSpec(memory_space=pltpu.VMEM)
HBM = pl.BlockSpec(memory_space=pltpu.HBM)


def trade(block, axis, pairing):
    size = lax.axis_size(axis)
    pairs = [(i, (((i + pairing) ^ 1) - pairing) % size) for i in range(size)]
    return lax.ppermute(block, axis, pairs)


def trade_both(block_0, block_1, axis):
    got_1 = trade(block_1, axis, 1)
    got_0 = trade(block_0, axis, 0)
    return got_0, got_1


def exchange(x_0, x_1, y_0, y_1):
    got_x = trade_both(x_0, x_1, "gx")
    got_y = trade_both(y_0, y_1, "gy")
    return *got_x, *got_y


def held(*shape):
    return pltpu.VMEM(shape, f32)


def on_core(*arrays):
    return [pltpu.with_memory_space_constraint(a, pltpu.VMEM) for a in arrays]


def call(kernel, **settings):
    return pl.pallas_call(kernel, **settings)


def struct(*shape):
    return jax.ShapeDtypeStruct(shape, f32)


def loop_scratch():
    space = [
        pltpu.VMEM((TILE + 8, TILE), f32),
        pltpu.VMEM((TILE + 8, TILE), f32),
        *[pltpu.VMEM((TILE, TILE), f32)] * 5,
    ]
    return [
        pltpu.VMEM((BUFFERS, STATE, TILE), f32),
        pltpu.VMEM((OUT_BUFFERS, 3 * TILE, TILE), f32),
        pltpu.SemaphoreType.DMA((BUFFERS,)),
        pltpu.SemaphoreType.DMA((OUT_BUFFERS,)),
        *(space * SIDE),
    ]


def shards(depth, discharge, bed, friction, tile_ids, neighbors, moves):
    base = (lax.axis_index(("gx", "gy")) * SLOTS).astype(i32).reshape(1)
    plan = moves[0].transpose(0, 2, 1)
    nb = neighbors.T
    tiles = [
        pltpu.with_memory_space_constraint(a, pltpu.HBM)
        for a in (
            depth.reshape(SLOTS * TILE, TILE),
            discharge.reshape(SLOTS * 2 * TILE, TILE),
            bed.reshape(SLOTS * TILE, TILE),
            friction.reshape(SLOTS * TILE, TILE),
        )
    ]
    out_0, out_1, *cargo = call(
        pack_kernel,
        in_specs=[SMEM, SMEM] + [HBM] * 4,
        out_specs=[VMEM] * (2 + 2 * len(LOADS)),
        out_shape=[held(MOVERS, 10 * FIELD)] * 2
        + [held(len(entries) * STATE, TILE) for entries in LOADS for _ in range(2)],
        scratch_shapes=[
            pltpu.VMEM((5, TILE, TILE), f32),
            pltpu.VMEM((TILE, TILE), f32),
            pltpu.SemaphoreType.DMA((len(LOADS), 2)),
        ],
        compiler_params=pltpu.CompilerParams(vmem_limit_bytes=12 * 2**20),
    )(plan, base, *tiles)
    from_0, from_1 = trade_both(out_0, out_1, "gy")
    early_0, early_1 = trade_both(*cargo[:2], "gy")
    frames = call(
        extract_kernel,
        in_specs=[HBM] * 4,
        out_specs=VMEM,
        out_shape=held(2 * SLOTS, 5 * FIELD),
        scratch_shapes=[
            pltpu.VMEM((SLOTS * TILE, TILE), f32),
            pltpu.VMEM((SLOTS * 2 * TILE, TILE), f32),
            pltpu.VMEM((SLOTS * TILE, TILE), f32),
            pltpu.VMEM((SLOTS * TILE, TILE), f32),
            pltpu.VMEM((2, 5, TILE, TILE), f32),
            pltpu.VMEM((2, TILE, TILE), f32),
            pltpu.SemaphoreType.DMA((SLOTS // GROUP, 4)),
        ],
        compiler_params=pltpu.CompilerParams(vmem_limit_bytes=20 * 2**20),
    )(*tiles)

    first_rows = 4 * MOVERS
    dyn, fixed, *sends = call(
        settle_kernel,
        in_specs=[SMEM, SMEM] + [VMEM] * 4,
        out_specs=[VMEM] * 6,
        out_shape=[
            held(2 * SLOTS, 3 * FIELD),
            held(2 * SLOTS, 2 * FIELD),
            held(first_rows, TILE),
            held(first_rows, TILE),
            held(first_rows, TILE),
            held(first_rows, TILE),
        ],
        compiler_params=pltpu.CompilerParams(vmem_limit_bytes=12 * 2**20),
    )(plan, base, *on_core(nb, frames, from_0, from_1))
    got = exchange(*sends)
    chunks = [trade_both(*cargo[2:4], "gy")]
    still = []
    trails = []
    for turn in range(3):

        def body(*refs, turn=turn):
            step_kernel(turn, *refs)

        shapes = [
            (2 * SLOTS, 3 * FIELD),
            (2 * SLOTS, 5 * TILE),
            (2 * SLOTS, 2 * TILE),
            (MOVERS, TILE),
            (MOVERS, TILE),
            (MOVERS, TILE),
            (MOVERS, TILE),
        ]
        dyn, kept, trail, *sends = call(
            body,
            in_specs=[SMEM] + [VMEM] * (7 + len(still)),
            out_specs=[VMEM] * len(shapes),
            out_shape=[held(*s) for s in shapes],
                compiler_params=pltpu.CompilerParams(vmem_limit_bytes=12 * 2**20),
        )(base, *on_core(nb, dyn, fixed, *still, *got))
        still = [kept]
        trails.append(trail)
        got = exchange(*sends)
        chunks.append(trade_both(*cargo[2 * turn + 4 : 2 * turn + 6], "gy"))

    late_0, late_1 = chunks[3]
    kept_inputs = on_core(
        nb, dyn, fixed, *still, *got, *trails, early_0, early_1, *chunks[0], *chunks[1], *chunks[2]
    )
    new_depth, new_flow, edges, columns = call(
        tile_kernel,
        in_specs=[SMEM] * 4 + [VMEM] * len(kept_inputs) + [HBM] * 4,
        out_specs=[HBM, HBM, VMEM, VMEM],
        out_shape=[
            struct(SLOTS * TILE, TILE),
            struct(SLOTS * 2 * TILE, TILE),
            held(10, SLOTS, TILE),
            held(3, TILE, TILE),
        ],
        scratch_shapes=[
            pltpu.VMEM((3 * TILE, TILE), f32),
            pltpu.VMEM((TILE, TILE), f32),
            pltpu.SMEM((SLOTS,), i32),
            pltpu.SMEM((SLOTS,), i32),
            pltpu.SemaphoreType.DMA,
            *loop_scratch(),
        ],
        compiler_params=pltpu.CompilerParams(vmem_limit_bytes=12 * 2**20),
    )(plan, base, tile_ids, nb, *kept_inputs, *tiles)
    new_depth, new_flow = pl.pallas_call(
        late_kernel,
        in_specs=[SMEM] * 3 + [VMEM] * 4 + [HBM] * 2,
        out_specs=[HBM, HBM],
        out_shape=[struct(SLOTS * TILE, TILE), struct(SLOTS * 2 * TILE, TILE)],
        input_output_aliases={7: 0, 8: 1},
        scratch_shapes=loop_scratch(),
        compiler_params=pltpu.CompilerParams(vmem_limit_bytes=12 * 2**20),
        name="late_tiles",
    )(plan, base, nb, *on_core(edges, columns, late_0, late_1), new_depth, new_flow)
    return (
        new_depth.reshape(SLOTS, TILE, TILE),
        new_flow.reshape(SLOTS, 2, TILE, TILE),
    )


def solution(mesh):
    return jax.shard_map(
        shards,
        mesh=mesh,
        in_specs=(
            P(("gx", "gy"), None, None),
            P(("gx", "gy"), None, None, None),
            P(("gx", "gy"), None, None),
            P(("gx", "gy"), None, None),
            P(("gx", "gy")),
            P(("gx", "gy"), None),
            P(("gx", "gy"), None, None, None),
        ),
        out_specs=(P(("gx", "gy"), None, None), P(("gx", "gy"), None, None, None)),
        check_vma=False,
    )
```
